32 devices in a mesh: dp: 8 (over z, y), mp: 4 (over x, core).
Axes of the slice: x: 2, y: 2, z: 4, core: 2. Of those that a mesh axis runs over, the one named last changes fastest.
Arguments:
- tokens: bfloat16 [16384, 768], P(('dp', 'mp')), may hold values from -6 to 6
- doc_lengths: int32 [8, 4], P('dp'), may hold values from 1 to 1024, 1792 in all within a row
- attn_gain: float32 [768], replicated, may hold values from 0.5 to 1.5
- attn_shift: float32 [768], replicated, may hold values from -1.75 to 1.75
- query_weight: bfloat16 [768, 768], P(None, 'mp'), may hold values from -0.21875 to 0.21875
- query_bias: float32 [768], P('mp'), may hold values from -1.75 to 1.75
- key_weight: bfloat16 [768, 64], replicated, may hold values from -0.21875 to 0.21875
- key_bias: float32 [64], replicated, may hold values from -3 to 3
- value_weight: bfloat16 [768, 64], replicated, may hold values from -0.21875 to 0.21875
- value_bias: float32 [64], replicated, may hold values from -1.75 to 1.75
- out_weight: bfloat16 [768, 768], P('mp'), may hold values from -0.875 to 0.875
- out_bias: float32 [768], replicated, may hold values from -1.75 to 1.75
- mlp_gain: float32 [768], replicated, may hold values from 0.5 to 1.5
- mlp_shift: float32 [768], replicated, may hold values from -1.75 to 1.75
- up_weight: bfloat16 [768, 3072], P(None, 'mp'), may hold values from -0.21875 to 0.21875
- up_bias: float32 [3072], P('mp'), may hold values from -1.75 to 1.75
- down_weight: bfloat16 [3072, 768], P('mp'), may hold values from -0.21875 to 0.21875
- down_bias: float32 [768], replicated, may hold values from -1.75 to 1.75
- out_grad: bfloat16 [16384, 768], P(('dp', 'mp')), may hold values from -6 to 6
Outputs:
- block_out: bfloat16 [16384, 768], P(('dp', 'mp'))
- input_grad: bfloat16 [16384, 768], P(('dp', 'mp'))
- attn_gain_grad: float32 [768], replicated
- attn_shift_grad: float32 [768], replicated
- query_weight_grad: float32 [768, 768], P(None, 'mp')
- query_bias_grad: float32 [768], P('mp')
- key_weight_grad: float32 [768, 64], replicated
- key_bias_grad: float32 [64], replicated
- value_weight_grad: float32 [768, 64], replicated
- value_bias_grad: float32 [64], replicated
- out_weight_grad: float32 [768, 768], P('mp')
- out_bias_grad: float32 [768], replicated
- mlp_gain_grad: float32 [768], replicated
- mlp_shift_grad: float32 [768], replicated
- up_weight_grad: float32 [768, 3072], P(None, 'mp')
- up_bias_grad: float32 [3072], P('mp')
- down_weight_grad: float32 [3072, 768], P('mp')
- down_bias_grad: float32 [768], replicated
The draws below stay inside these ranges and needn't reach their ends.
All inputs are finite; a program needn't handle non-finite values.
Results may differ from the reference program's by a relative error of at most 0.02.
Values may be sent and summed in bfloat16 or wider, within the bound.
A program may use at most 128 MiB of HBM per device.

```python
import math
import jax
import jax.numpy as jnp
import numpy as np
from jax import lax

D = 768
H = 12
HD = 64
FF = 3072
ROT = 16
SLOT = 2048
VALID = 1792
LONGEST = 1024
DOCS = 4
ROWS = 8
TOKENS = 16384


def level_of(key, shape, pieces, low, high):
    def one(axis_at, shards_of):
        steps = jax.random.uniform(jax.random.fold_in(jax.random.fold_in(key, 6), axis_at), (shards_of,), jnp.float32, low / len(pieces), high / len(pieces))
        return jnp.repeat(jnp.exp(steps), shape[axis_at] // shards_of).reshape((-1,) + (1,) * (len(shape) - axis_at - 1))

    factor_of = one(*pieces[0])
    for cut in pieces[1:]:
        factor_of = factor_of * one(*cut)
    return factor_of


def profile(count, total, reach, slope):
    weights = [(1 << 20) // math.isqrt(grade ** slope) + 1 for grade in range(2, count + 1)]
    rest, counts = total - reach - (count - 1), [1] * (count - 1)
    while rest > 0:
        movable = [i for i in range(count - 1) if counts[i] < reach]
        mass, remaining = sum([weights[i] for i in movable]), rest
        for i in movable:
            extra = min(reach - counts[i], max(1, remaining * weights[i] // mass), rest)
            counts[i] = counts[i] + extra
            rest = rest - extra
    return np.array([reach] + counts)


def ragged_sizes(stream_key, count, total, most, skew):
    if count == 2:
        one = jax.random.randint(stream_key, (), max(1, total - most), min(most, total - 1) + 1)
        return jnp.stack([one, total - one])
    sizes = jnp.asarray(profile(count, total, most, skew), jnp.int32)
    couples = (count - 1) // 2
    donor, sink = sizes[1:1 + 2 * couples:2], sizes[2:2 + 2 * couples:2]
    slack = jnp.minimum(donor - 1, most - sink)
    shifted = jax.random.randint(jax.random.fold_in(stream_key, 1), (couples,), 0, 1 << 20) % (slack + 1)
    sizes = sizes.at[1:1 + 2 * couples:2].set(donor - shifted).at[2:2 + 2 * couples:2].set(sink + shifted)
    return sizes[jax.random.permutation(jax.random.fold_in(stream_key, 2), count)]


def noise(stream_key, shape, width, limit, split=(), kind=jnp.bfloat16):
    drawn = jax.random.normal(stream_key, shape, jnp.float32) * width
    if len(split) > 0:
        drawn = level_of(stream_key, shape, split, -0.22, 0.18) * drawn
    return jnp.clip(drawn, min=-limit, max=limit).astype(kind)


def setup_inputs(seed: int = 0) -> dict:
    splits = jax.random.split(jax.random.key(seed), 20)
    return {
        "tokens": noise(splits[0], (TOKENS, D), 1.0, 6.0, ((0, 32),)),
        "doc_lengths": jax.vmap(lambda own: ragged_sizes(own, DOCS, VALID, LONGEST, 2))(jax.random.split(splits[1], ROWS)).reshape((ROWS, DOCS)).astype(jnp.int32),
        "attn_gain": jnp.clip(1.0 + 0.1 * jax.random.normal(splits[2], (D,), jnp.float32), 0.5, 1.5),
        "attn_shift": noise(splits[3], (D,), 0.3, 1.75, (), jnp.float32),
        "query_weight": noise(splits[4], (D, H * HD), D ** -0.5, 0.21875, ((1, 4),)),
        "query_bias": noise(splits[5], (H * HD,), 0.3, 1.75, ((0, 4),), jnp.float32),
        "key_weight": noise(splits[6], (D, HD), D ** -0.5, 0.21875),
        "key_bias": noise(splits[7], (HD,), 0.5, 3.0, (), jnp.float32),
        "value_weight": noise(splits[8], (D, HD), D ** -0.5, 0.21875),
        "value_bias": noise(splits[9], (HD,), 0.3, 1.75, (), jnp.float32),
        "out_weight": noise(splits[10], (H * HD, D), (H * HD // 16) ** -0.5, 0.875, ((0, 4),)),
        "out_bias": noise(splits[11], (D,), 0.3, 1.75, (), jnp.float32),
        "mlp_gain": jnp.clip(1.0 + 0.1 * jax.random.normal(splits[12], (D,), jnp.float32), 0.5, 1.5),
        "mlp_shift": noise(splits[13], (D,), 0.3, 1.75, (), jnp.float32),
        "up_weight": noise(splits[14], (D, FF), D ** -0.5, 0.21875, ((1, 4),)),
        "up_bias": noise(splits[15], (FF,), 0.3, 1.75, ((0, 4),), jnp.float32),
        "down_weight": noise(splits[16], (FF, D), (FF // 4) ** -0.5, 0.21875, ((0, 4),)),
        "down_bias": noise(splits[17], (D,), 0.3, 1.75, (), jnp.float32),
        "out_grad": noise(splits[18], (TOKENS, D), 1.0, 6.0, ((0, 32),)),
    }


epsilon = 1e-05

@jax.custom_vjp
def low(v):
    return lax.optimization_barrier(v.astype(jnp.bfloat16)).astype(jnp.float32)

@jax.custom_vjp
def low_back(v):
    return v

def low_keep(v):
    return (low(v), None)

def low_pass(kept, grad):
    return (grad,)

def back_keep(v):
    return (v, None)

def back_low(kept, grad):
    return (low(grad),)
low.defvjp(low_keep, low_pass)
low_back.defvjp(back_keep, back_low)

def matmul(left, right):
    return jnp.dot(left, right, precision=lax.Precision.HIGHEST)

def layer_norm(values, gain, shift):
    average = lax.optimization_barrier(jnp.mean(values, axis=-1, keepdims=True))
    centered = values - average
    inv_std = lax.rsqrt(lax.optimization_barrier(jnp.mean(centered * centered, axis=-1, keepdims=True)) + epsilon)
    return centered * inv_std * gain + shift

def rotate(values, cos_table, sine_table):
    half_rot = ROT // 2
    lower_part = values[..., :half_rot]
    upper_part = values[..., half_rot:ROT]
    return jnp.concatenate([lower_part * cos_table - upper_part * sine_table, upper_part * cos_table + lower_part * sine_table, values[..., ROT:]], axis=-1)

def row_layout(lengths):
    slot_index = jnp.arange(SLOT, dtype=jnp.int32)
    doc_ends = jnp.cumsum(lengths, axis=-1).astype(jnp.int32)
    doc_starts = doc_ends - lengths
    segment = lax.optimization_barrier(jnp.sum((slot_index[:, None] >= doc_ends[..., None, :]).astype(jnp.int32), axis=-1))
    doc_begins = jnp.concatenate([doc_starts, doc_ends[..., -1:]], axis=-1)
    labels = jnp.arange(DOCS + 1, dtype=jnp.int32)
    picked = lax.optimization_barrier(jnp.sum(jnp.where(segment[..., None] == labels, doc_begins[..., None, :], 0), axis=-1))
    return (segment, slot_index - picked)

def angles(position):
    half_rot = ROT // 2
    frequency = 10000.0 ** (-(2.0 * jnp.arange(half_rot, dtype=jnp.float32)) / ROT)
    angle_grid = position.astype(jnp.float32)[..., None] * frequency
    return (jnp.cos(angle_grid), jnp.sin(angle_grid))

def forward_row(row_tokens, segment, cos_table, sine_table, params):
    attn_gain, attn_shift, query_weight, query_bias, key_weight, key_bias, value_weight, value_bias, out_weight, out_bias, mlp_gain, mlp_shift, up_weight, up_bias, down_weight, down_bias = params
    attn_in = low(layer_norm(row_tokens, attn_gain, attn_shift))
    queries = low_back(matmul(attn_in, query_weight) + query_bias).reshape(SLOT, H, HD)
    queries = low(rotate(queries, cos_table[:, None, :], sine_table[:, None, :]))
    key_rows = low(rotate(low_back(matmul(attn_in, key_weight) + key_bias), cos_table, sine_table))
    value_rows = low(low_back(matmul(attn_in, value_weight) + value_bias))
    block_rows = min(512, SLOT)
    block_count = SLOT // block_rows
    key_index = jnp.arange(SLOT, dtype=jnp.int32)

    def attend(block_item):
        query_block, first_row = block_item
        query_index = first_row + jnp.arange(block_rows, dtype=jnp.int32)
        seg_rows = lax.dynamic_slice_in_dim(segment, first_row, block_rows)
        allowed = (seg_rows[:, None] == segment[None, :]) & (key_index[None, :] <= query_index[:, None])
        scores = low_back(jnp.einsum('bhe,ke->hbk', query_block, key_rows, precision=lax.Precision.HIGHEST) * HD ** (-0.5))
        scores = jnp.where(allowed[None], scores, -1e+30)
        probs_low = low(jax.nn.softmax(scores, axis=-1))
        return jnp.einsum('hbk,ke->bhe', probs_low, value_rows, precision=lax.Precision.HIGHEST)
    starts_list = jnp.arange(block_count, dtype=jnp.int32) * block_rows
    context = lax.map(jax.checkpoint(attend), (queries.reshape(block_count, block_rows, H, HD), starts_list))
    context = low(low_back(context.reshape(SLOT, H * HD)))
    attn_out = matmul(context, out_weight) + out_bias
    mlp_in = low(layer_norm(row_tokens, mlp_gain, mlp_shift))
    hidden_pre = low_back(matmul(mlp_in, up_weight) + up_bias)
    hidden = low(jax.nn.gelu(hidden_pre, approximate=False))
    return row_tokens + attn_out + matmul(hidden, down_weight) + down_bias

def reference(tokens, doc_lengths, attn_gain, attn_shift, query_weight, query_bias, key_weight, key_bias, value_weight, value_bias, out_weight, out_bias, mlp_gain, mlp_shift, up_weight, up_bias, down_weight, down_bias, out_grad):
    params = tuple((weight_item.astype(jnp.float32) for weight_item in (attn_gain, attn_shift, query_weight, query_bias, key_weight, key_bias, value_weight, value_bias, out_weight, out_bias, mlp_gain, mlp_shift, up_weight, up_bias, down_weight, down_bias)))
    row_inputs = tokens.astype(jnp.float32).reshape(ROWS, SLOT, D)
    row_grads = out_grad.astype(jnp.float32).reshape(ROWS, SLOT, D)

    def row_step(totals, row_item):
        row_tokens, lengths, row_grad = row_item
        segment, position = row_layout(lengths)
        cos_table, sine_table = angles(position)
        row_grad = row_grad * (segment < DOCS).astype(jnp.float32)[:, None]

        def apply_row(inputs, weights):
            return forward_row(inputs, segment, cos_table, sine_table, weights)
        output, pullback = jax.vjp(apply_row, row_tokens, params)
        token_grad, weight_grads = pullback(row_grad)
        return (jax.tree.map(jnp.add, totals, weight_grads), (output, token_grad))
    zero_grads = jax.tree.map(jnp.zeros_like, params)
    totals, (outputs, token_grads) = lax.scan(row_step, zero_grads, (row_inputs, doc_lengths, row_grads))
    return (outputs.reshape(TOKENS, D).astype(jnp.bfloat16), token_grads.reshape(TOKENS, D).astype(jnp.bfloat16), totals[0], totals[1], totals[2], totals[3], totals[4], totals[5], totals[6], totals[7], totals[8], totals[9], totals[10], totals[11], totals[12], totals[13], totals[14], totals[15])
```

```python
from functools import partial

import jax
import jax.numpy as jnp
from jax import lax
from jax.experimental import pallas as pl
from jax.experimental.pallas import tpu as pltpu
from jax.sharding import PartitionSpec as P

HD = 64
ROT = 16
HALF = ROT // 2
SLOT = 2048
VALID = 1792
LONGEST = 1024
DOCS = 4
EPS = 1e-05
BLK = 256
NBLK = SLOT // BLK
BAND = LONGEST // BLK
PADBLK = VALID // BLK
LANES = 128
F32 = jnp.float32
BF16 = jnp.bfloat16


def dot(a, b):
    return lax.dot_general(a, b, (((1,), (0,)), ((), ())), preferred_element_type=F32)


def dot_t(a, b):
    return lax.dot_general(a, b, (((1,), (1,)), ((), ())), preferred_element_type=F32)


def t_dot(a, b):
    return lax.dot_general(a, b, (((0,), (0,)), ((), ())), preferred_element_type=F32)


def key_blocks(i):
    if i >= PADBLK:
        return list(range(PADBLK, i + 1))
    return list(range(max(0, i - BAND), i + 1))


SLOTS = {}
for _i in range(NBLK):
    for _j in key_blocks(_i):
        SLOTS[(_i, _j)] = len(SLOTS)
NSLOT = len(SLOTS)


def doc_begin(slot, ends):
    begin = jnp.zeros_like(slot)
    for end in ends:
        begin = jnp.where(slot >= end, end, begin)
    return begin


def doc_ends(doc_ref):
    ends = []
    total = 0
    for d in range(DOCS):
        total = total + doc_ref[0, d]
        ends.append(total)
    return ends


def build_tables(doc_ref, cos_ref, sa_ref, sb_ref):
    ends = doc_ends(doc_ref)
    slot = lax.broadcasted_iota(jnp.int32, (HALF, SLOT), 1)
    freq_index = lax.broadcasted_iota(jnp.int32, (HALF, SLOT), 0)
    position = (slot - doc_begin(slot, ends)).astype(F32)
    freq = jnp.zeros((HALF, SLOT), F32)
    for i in range(HALF):
        freq = jnp.where(freq_index == i, 10000.0 ** (-(2.0 * i) / ROT), freq)
    angle = position * freq
    lane = lax.broadcasted_iota(jnp.int32, (3 * HALF, LANES), 1) % HD
    row = lax.broadcasted_iota(jnp.int32, (3 * HALF, LANES), 0) % HALF
    low = (lane == row).astype(BF16)
    high = (lane == row + HALF).astype(BF16)
    rest = lax.broadcasted_iota(jnp.int32, (SLOT, LANES), 1) % HD >= ROT

    def parts(v):
        a = v.astype(BF16)
        r = v - a.astype(F32)
        b = r.astype(BF16)
        c = (r - b.astype(F32)).astype(BF16)
        return jnp.concatenate([a, b, c], axis=0)

    cos = parts(jnp.cos(angle))
    sine = parts(jnp.sin(angle))
    cos_ref[...] = jnp.where(rest, 1.0, t_dot(cos, low + high))
    sa_ref[...] = -t_dot(sine, low)
    sb_ref[...] = t_dot(sine, high)


def rope(v, cos, sa, sb):
    return v * cos + pltpu.roll(v, LANES - HALF, 1) * sa + pltpu.roll(v, HALF, 1) * sb


def unrope(v, cos, sa, sb):
    return v * cos - pltpu.roll(v, LANES - HALF, 1) * sa - pltpu.roll(v, HALF, 1) * sb


def mlp_kernel(
    heads,
    doc_ref, x_ref, g_ref, ag_ref, as_ref, wq_ref, bq_ref, wk_ref, bk_ref, wv_ref, bv_ref, wo_ref, mg_ref, ms_ref, wu_ref, bu_ref, wd_ref,
    q_ref, kv_ref, dctx_ref, xh_ref, gm_ref, outp_ref, em_ref, gup_ref, gdown_ref, bup_ref, cos_ref, sa_ref, sb_ref,
    ain, min_, hp, hid, dg, dpre, wq, wkv, wo, bq, bkv,
):
    pairs = (heads + 1) // 2
    width = pairs * LANES
    rows = 512
    depth = x_ref.shape[1]
    ff = wu_ref.shape[1]
    build_tables(doc_ref, cos_ref, sa_ref, sb_ref)
    used = heads * HD
    wq[:, :used] = wq_ref[...]
    bq[:, :used] = bq_ref[...]
    wo[:used, :] = wo_ref[...]
    if used < width:
        wq[:, used:] = jnp.zeros((depth, width - used), BF16)
        bq[:, used:] = jnp.zeros((1, width - used), F32)
        wo[used:, :] = jnp.zeros((width - used, depth), BF16)
    wkv[:, :HD] = wk_ref[...]
    wkv[:, HD:] = wv_ref[...]
    bkv[:, :HD] = bk_ref[...]
    bkv[:, HD:] = bv_ref[...]
    gup_ref[...] = jnp.zeros_like(gup_ref)
    gdown_ref[...] = jnp.zeros_like(gdown_ref)
    bup_ref[...] = jnp.zeros_like(bup_ref)

    def chunk(c, carry):
        first = pl.multiple_of(c * rows, rows)
        here = pl.ds(first, rows)

        def norm(r, carry):
            at = pl.ds(pl.multiple_of(first + r * 32, 32), 32)
            to = pl.ds(pl.multiple_of(r * 32, 32), 32)
            v = x_ref[at, :].astype(F32)
            mean = jnp.mean(v, axis=-1, keepdims=True)
            v = v - mean
            inv = lax.rsqrt(jnp.mean(v * v, axis=-1, keepdims=True) + EPS)
            v = v * inv
            xh_ref[at, :] = v.astype(BF16)
            ain[to, :] = (v * ag_ref[...] + as_ref[...]).astype(BF16)
            min_[to, :] = (v * mg_ref[...] + ms_ref[...]).astype(BF16)
            slot = first + r * 32 + lax.broadcasted_iota(jnp.int32, (32, depth), 0)
            gm_ref[at, :] = jnp.where(slot < VALID, g_ref[at, :].astype(F32), 0.0).astype(BF16)
            return carry

        lax.fori_loop(0, rows // 32, norm, 0)
        cos, sa, sb = cos_ref[here, :], sa_ref[here, :], sb_ref[here, :]
        qf = dot(ain[...], wq[...]) + bq[...]
        for p in range(pairs):
            q_ref[p, here, :] = (rope(qf[:, p * LANES : (p + 1) * LANES], cos, sa, sb) * HD**-0.5).astype(BF16)
        kvf = dot(ain[...], wkv[...]) + bkv[...]
        is_key = lax.broadcasted_iota(jnp.int32, (rows, LANES), 1) < HD
        kv_ref[here, :] = jnp.where(is_key, rope(kvf, cos, sa, sb), kvf).astype(BF16)
        hp[...] = dot(min_[...], wu_ref[...])

        def act(r, carry):
            to = pl.ds(pl.multiple_of(r * 16, 16), 16)
            v = hp[to, :] + bu_ref[...]
            cdf = 0.5 * (1.0 + lax.erf(v * (0.5**0.5)))
            pdf = jnp.exp(-0.5 * v * v) * (2.0 * jnp.pi) ** -0.5
            hid[to, :] = (v * cdf).astype(BF16)
            dg[to, :] = (cdf + v * pdf).astype(BF16)
            return carry

        lax.fori_loop(0, rows // 16, act, 0)
        outp_ref[here, :] = dot(hid[...], wd_ref[...]).astype(BF16)
        g = gm_ref[here, :]
        dc = dot_t(g, wo[...]).astype(BF16)
        for p in range(pairs):
            dctx_ref[p, here, :] = dc[:, p * LANES : (p + 1) * LANES]
        hp[...] = dot_t(g, wd_ref[...])

        def back(r, acc):
            to = pl.ds(pl.multiple_of(r * 16, 16), 16)
            v = hp[to, :] * dg[to, :].astype(F32)
            dpre[to, :] = v.astype(BF16)
            return acc + v[:8] + v[8:]

        acc = lax.fori_loop(0, rows // 16, back, jnp.zeros((8, ff), F32))
        bup_ref[...] += jnp.sum(acc, axis=0, keepdims=True)
        em_ref[here, :] = (dot_t(dpre[...], wu_ref[...]) * mg_ref[...]).astype(BF16)
        gup_ref[...] += t_dot(xh_ref[here, :], dpre[...])
        gdown_ref[...] += t_dot(hid[...], g)
        return carry

    lax.fori_loop(0, SLOT // rows, chunk, 0)


def attention_kernel(
    heads,
    doc_ref, q_ref, kv_ref, dctx_ref, cos_ref, sa_ref, sb_ref,
    ctx_ref, dqkv_ref,
    kx, vx, probs, scores, total, left, dq, dk, dv, dcn,
):
    pairs = (heads + 1) // 2
    ends = doc_ends(doc_ref)
    lane = lax.broadcasted_iota(jnp.int32, (BLK, LANES), 1)
    low = lane < HD
    for b in range(NBLK):
        at = pl.ds(b * BLK, BLK)
        kv = kv_ref[at, :].astype(F32)
        vk = pltpu.roll(kv, HD, 1)
        zero = jnp.zeros_like(kv)
        kx[0, at, :] = jnp.where(low, kv, zero).astype(BF16)
        kx[1, at, :] = jnp.where(low, zero, vk).astype(BF16)
        vx[0, at, :LANES] = jnp.where(low, vk, zero).astype(BF16)
        vx[1, at, :LANES] = jnp.where(low, zero, kv).astype(BF16)
        vx[0, at, LANES:] = jnp.where(low, 1.0, 0.0).astype(BF16)
        vx[1, at, LANES:] = jnp.where(low, 0.0, 1.0).astype(BF16)
    dk[...] = jnp.zeros_like(dk)
    dv[...] = jnp.zeros_like(dv)

    for i in range(NBLK):
        at = pl.ds(i * BLK, BLK)
        blocks = key_blocks(i)
        slot = i * BLK + lax.broadcasted_iota(jnp.int32, (BLK, 1), 0)
        begin = doc_begin(slot, ends)
        total[...] = jnp.zeros_like(total)

        def head_fwd(h, carry):
            p, half = h // 2, h % 2
            qb = q_ref[p, at, :]
            peak = jnp.full((BLK, BLK), -1e30, F32)
            for n, j in enumerate(blocks):
                s = dot_t(qb, kx[half, pl.ds(j * BLK, BLK), :])
                key = j * BLK + lax.broadcasted_iota(jnp.int32, (BLK, BLK), 1)
                ok = key >= begin
                if i == j:
                    ok = ok & (key <= slot)
                s = jnp.where(ok, s, -1e30)
                scores[:, n * BLK : (n + 1) * BLK] = s
                peak = jnp.maximum(peak, s)
            top = jnp.max(peak, axis=-1, keepdims=True)
            acc = total[p]
            for n, j in enumerate(blocks):
                e = jnp.exp(scores[:, n * BLK : (n + 1) * BLK] - top).astype(BF16)
                probs[h, SLOTS[(i, j)]] = e
                acc = acc + dot(e, vx[half, pl.ds(j * BLK, BLK), :])
            total[p] = acc
            return carry

        lax.fori_loop(0, heads, head_fwd, 0)
        for p in range(pairs):
            norm = total[p, :, LANES:]
            norm = 1.0 / jnp.where(norm == 0.0, 1.0, norm)
            ctx = total[p, :, :LANES] * norm
            ctx_ref[p, at, :] = ctx.astype(BF16)
            dcs = (dctx_ref[p, at, :].astype(F32) * norm).astype(BF16)
            dcn[p, at, :] = dcs
            prod = dcs.astype(F32) * ctx
            extra = jnp.zeros((BLK, LANES), F32)
            for half, first in ((0, 0), (1, HD)):
                d = -jnp.sum(jnp.where(low if half == 0 else ~low, prod, 0.0), axis=-1, keepdims=True)
                d_top = d.astype(BF16).astype(F32)
                extra = jnp.where(lane == first, d_top, extra)
                extra = jnp.where(lane == first + 1, d - d_top, extra)
            left[p, at, :LANES] = dcs
            left[p, at, LANES:] = extra.astype(BF16)

    dq[...] = jnp.zeros_like(dq)
    for i in range(PADBLK):
        at = pl.ds(i * BLK, BLK)
        blocks = key_blocks(i)

        def head_bwd(h, carry):
            p, half = h // 2, h % 2
            lb = left[p, at, :]
            qb = q_ref[p, at, :]
            dc = dcn[p, at, :]
            acc = dq[p, at, :]
            for j in blocks:
                jat = pl.ds(j * BLK, BLK)
                e = probs[h, SLOTS[(i, j)]]
                ds = (e.astype(F32) * dot_t(lb, vx[half, jat, :])).astype(BF16)
                acc = acc + dot(ds, kx[half, jat, :])
                dk[half, jat, :] += t_dot(ds, qb)
                dv[half, jat, :] += t_dot(e, dc)
            dq[p, at, :] = acc
            return carry

        lax.fori_loop(0, heads, head_bwd, 0)

    for b in range(NBLK):
        at = pl.ds(b * BLK, BLK)
        cos, sa, sb = cos_ref[at, :], sa_ref[at, :], sb_ref[at, :]
        for p in range(pairs):
            dqkv_ref[at, p * LANES : (p + 1) * LANES] = (unrope(dq[p, at, :], cos, sa, sb) * HD**-0.5).astype(BF16)
        keys = dk[0, at, :] + pltpu.roll(dk[1, at, :], HD, 1)
        values = pltpu.roll(dv[0, at, :], HD, 1) + dv[1, at, :]
        both = jnp.where(low, unrope(keys, cos, sa, sb), values)
        dqkv_ref[at, pairs * LANES :] = both.astype(BF16)


VM = pl.BlockSpec(memory_space=pltpu.VMEM)
SM = pl.BlockSpec(memory_space=pltpu.SMEM)


def run_mlp(heads, doc, x_all, g_all, params):
    depth = x_all.shape[1]
    ff = params[-2].shape[1]
    pairs = (heads + 1) // 2
    width = pairs * LANES
    sh = jax.ShapeDtypeStruct
    return pl.pallas_call(
        partial(mlp_kernel, heads),
        out_shape=(
            sh((pairs, SLOT, LANES), BF16), sh((SLOT, LANES), BF16), sh((pairs, SLOT, LANES), BF16),
            sh((SLOT, depth), BF16), sh((SLOT, depth), BF16), sh((SLOT, depth), BF16), sh((SLOT, depth), BF16),
            sh((depth, ff), F32), sh((ff, depth), F32), sh((1, ff), F32),
            sh((SLOT, LANES), F32), sh((SLOT, LANES), F32), sh((SLOT, LANES), F32),
        ),
        in_specs=[SM] + [VM] * 16,
        out_specs=[VM] * 13,
        scratch_shapes=[
            pltpu.VMEM((512, depth), BF16), pltpu.VMEM((512, depth), BF16), pltpu.VMEM((512, ff), F32),
            pltpu.VMEM((512, ff), BF16), pltpu.VMEM((512, ff), BF16), pltpu.VMEM((512, ff), BF16),
            pltpu.VMEM((depth, width), BF16), pltpu.VMEM((depth, LANES), BF16), pltpu.VMEM((width, depth), BF16),
            pltpu.VMEM((1, width), F32), pltpu.VMEM((1, LANES), F32),
        ],
        compiler_params=pltpu.CompilerParams(vmem_limit_bytes=63 * 1024 * 1024),
        name="mlp",
    )(doc, x_all, g_all, *params)


def run_attention(heads, doc, q, kv, dctx, cos, sa, sb):
    pairs = (heads + 1) // 2
    sh = jax.ShapeDtypeStruct
    return pl.pallas_call(
        partial(attention_kernel, heads),
        out_shape=(sh((pairs, SLOT, LANES), BF16), sh((SLOT, (pairs + 1) * LANES), BF16)),
        in_specs=[SM] + [VM] * 6,
        out_specs=[VM] * 2,
        scratch_shapes=[
            pltpu.VMEM((2, SLOT, LANES), BF16), pltpu.VMEM((2, SLOT, 2 * LANES), BF16),
            pltpu.VMEM((heads, NSLOT, BLK, BLK), BF16), pltpu.VMEM((BLK, (BAND + 1) * BLK), F32),
            pltpu.VMEM((pairs, BLK, 2 * LANES), F32), pltpu.VMEM((pairs, SLOT, 2 * LANES), BF16),
            pltpu.VMEM((pairs, SLOT, LANES), F32), pltpu.VMEM((2, SLOT, LANES), F32), pltpu.VMEM((2, SLOT, LANES), F32),
            pltpu.VMEM((pairs, SLOT, LANES), BF16),
        ],
        compiler_params=pltpu.CompilerParams(vmem_limit_bytes=63 * 1024 * 1024),
        name="attention",
    )(doc, q, kv, dctx, cos, sa, sb)


def per_device(
    tokens, doc_lengths, attn_gain, attn_shift, query_weight, query_bias, key_weight, key_bias, value_weight, value_bias,
    out_weight, out_bias, mlp_gain, mlp_shift, up_weight, up_bias, down_weight, down_bias, out_grad,
):
    shard = tokens.shape[0]
    first = lax.axis_index("mp") * shard
    heads = query_weight.shape[1] // HD
    used = heads * HD
    pairs = (heads + 1) // 2
    row = lambda v: v.reshape(1, -1)
    x_all = lax.all_gather(tokens, "mp", axis=0, tiled=True)
    g_all = lax.all_gather(out_grad, "mp", axis=0, tiled=True)
    params = (
        row(attn_gain), row(attn_shift), query_weight, row(query_bias), key_weight, row(key_bias), value_weight, row(value_bias),
        out_weight, row(mlp_gain), row(mlp_shift), up_weight, row(up_bias), down_weight,
    )
    q, kv, dctx, xh, gm, outp, em, gup, gdown, bup, cos, sa, sb = run_mlp(heads, doc_lengths, x_all, g_all, params)
    gup, gdown = lax.optimization_barrier((gup.astype(BF16), gdown.astype(BF16)))
    gup, gdown = lax.psum((gup, gdown), "dp")
    ctx, dqkv = run_attention(heads, doc_lengths, q, kv, dctx, cos, sa, sb)
    ctx = jnp.concatenate([ctx[p] for p in range(pairs)], axis=1)[:, :used]
    branch = dot(ctx, out_weight) + outp.astype(F32)
    branch = lax.psum_scatter(branch.astype(BF16), "mp", scatter_dimension=0, tiled=True)
    gout = t_dot(ctx, gm)
    qkv_weight = jnp.concatenate([query_weight, jnp.zeros((query_weight.shape[0], pairs * LANES - used), BF16), key_weight, value_weight], axis=1)
    e = dot_t(dqkv, qkv_weight) * attn_gain + em.astype(F32)
    e = lax.psum_scatter(e.astype(BF16), "mp", scatter_dimension=0, tiled=True).astype(F32)
    gqkv = t_dot(xh, dqkv)
    bqkv = jnp.sum(dqkv, axis=0, dtype=F32)
    g_sum = jnp.sum(gm, axis=0, dtype=F32)
    split = pairs * LANES
    gq, gout, gkv = lax.psum((gqkv[:, :used].astype(BF16), gout.astype(BF16), gqkv[:, split:].astype(BF16)), "dp")
    vectors = lax.psum(jnp.concatenate([bqkv, g_sum, bup[0]]), "dp")
    gq, gout, gkv, gup, gdown = (v.astype(F32) for v in (gq, gout, gkv, gup, gdown))
    depth = tokens.shape[1]
    bqkv, g_sum, bup = vectors[: split + LANES], vectors[split + LANES : split + LANES + depth], vectors[split + LANES + depth :]
    bq, bkv = bqkv[:used], bqkv[split:]
    wq32, wu32 = query_weight.astype(F32), up_weight.astype(F32)
    kv_weight = jnp.concatenate([key_weight, value_weight], axis=1).astype(F32)
    sums = jnp.concatenate(
        [
            (gkv).reshape(-1),
            bkv,
            jnp.sum(gq * wq32, axis=1) + jnp.sum(gkv * kv_weight, axis=1),
            jnp.sum(bq * wq32, axis=1) + jnp.sum(bkv * kv_weight, axis=1),
            jnp.sum(gup * wu32, axis=1),
            jnp.sum(bup * wu32, axis=1),
        ]
    )
    sums = lax.psum(sums, "mp")
    n = depth * LANES
    gkv, bkv = sums[:n].reshape(depth, LANES), sums[n : n + LANES]
    attn_gain_grad, attn_shift_grad, mlp_gain_grad, mlp_shift_grad = sums[n + LANES :].reshape(4, depth)
    query_weight_grad = attn_gain[:, None] * gq + attn_shift[:, None] * bq
    kv_weight_grad = attn_gain[:, None] * gkv + attn_shift[:, None] * bkv
    up_weight_grad = mlp_gain[:, None] * gup + mlp_shift[:, None] * bup
    x = tokens.astype(F32)
    block_out = (x + branch.astype(F32) + out_bias + down_bias).astype(BF16)
    mean = jnp.mean(x, axis=-1, keepdims=True)
    xc = x - mean
    inv = lax.rsqrt(jnp.mean(xc * xc, axis=-1, keepdims=True) + EPS)
    xn = xc * inv
    slot = first + lax.broadcasted_iota(jnp.int32, (shard, 1), 0)
    g = jnp.where(slot < VALID, out_grad.astype(F32), 0.0)
    dx = inv * (e - jnp.mean(e, axis=-1, keepdims=True) - xn * jnp.mean(e * xn, axis=-1, keepdims=True))
    input_grad = (g + dx).astype(BF16)
    return (
        block_out, input_grad, attn_gain_grad, attn_shift_grad, query_weight_grad, bq, kv_weight_grad[:, :HD], bkv[:HD],
        kv_weight_grad[:, HD:], bkv[HD:], gout, g_sum, mlp_gain_grad, mlp_shift_grad, up_weight_grad, bup, gdown, g_sum,
    )


def solution(mesh):
    rows = P(("dp", "mp"), None)
    placed = (
        rows, P("dp", None), P(), P(), P(None, "mp"), P("mp"), P(), P(), P(), P(), P("mp", None), P(), P(), P(),
        P(None, "mp"), P("mp"), P("mp", None), P(), rows,
    )
    outs = (
        rows, rows, P(), P(), P(None, "mp"), P("mp"), P(), P(), P(), P(), P("mp", None), P(), P(), P(),
        P(None, "mp"), P("mp"), P("mp", None), P(),
    )
    return jax.shard_map(per_device, mesh=mesh, in_specs=placed, out_specs=outs, check_vma=False)
```

```python
from functools import partial

import jax
import jax.numpy as jnp
from jax import lax
from jax.experimental import pallas as pl
from jax.experimental.pallas import tpu as pltpu
from jax.sharding import PartitionSpec as P

HD = 64
ROT = 16
HALF = ROT // 2
SLOT = 2048
VALID = 1792
LONGEST = 1024
DOCS = 4
EPS = 1e-05
BLK = 256
NBLK = SLOT // BLK
BAND = LONGEST // BLK
PADBLK = VALID // BLK
LANES = 128
MP = 4
SHARD = SLOT // MP
RING = 8
EVENTS = 2 * RING - 1
F32 = jnp.float32
BF16 = jnp.bfloat16
MESH = pl.DeviceIdType.MESH


def dot(a, b):
    return lax.dot_general(a, b, (((1,), (0,)), ((), ())), preferred_element_type=F32)


def dot_t(a, b):
    return lax.dot_general(a, b, (((1,), (1,)), ((), ())), preferred_element_type=F32)


def t_dot(a, b):
    return lax.dot_general(a, b, (((0,), (0,)), ((), ())), preferred_element_type=F32)


def key_blocks(i):
    if i >= PADBLK:
        return list(range(PADBLK, i + 1))
    return list(range(max(0, i - BAND), i + 1))


SLOTS = {}
for _i in range(NBLK):
    for _j in key_blocks(_i):
        SLOTS[(_i, _j)] = len(SLOTS)
NSLOT = len(SLOTS)


def doc_begin(slot, ends):
    begin = jnp.zeros_like(slot)
    for end in ends:
        begin = jnp.where(slot >= end, end, begin)
    return begin


def doc_ends(doc_ref):
    ends = []
    total = 0
    for d in range(DOCS):
        total = total + doc_ref[0, d]
        ends.append(total)
    return ends


def build_tables(doc_ref, cos_ref, sine_ref):
    ends = doc_ends(doc_ref)
    slot = lax.broadcasted_iota(jnp.int32, (HALF, SLOT), 1)
    freq_index = lax.broadcasted_iota(jnp.int32, (HALF, SLOT), 0)
    position = (slot - doc_begin(slot, ends)).astype(F32)
    freq = jnp.zeros((HALF, SLOT), F32)
    for i in range(HALF):
        freq = jnp.where(freq_index == i, 10000.0 ** (-(2.0 * i) / ROT), freq)
    angle = position * freq
    lane = lax.broadcasted_iota(jnp.int32, (3 * HALF, LANES), 1) % HD
    row = lax.broadcasted_iota(jnp.int32, (3 * HALF, LANES), 0) % HALF
    low = jnp.where(lane == row, 1.0, 0.0)
    high = jnp.where(lane == row + HALF, 1.0, 0.0)
    rest = lax.broadcasted_iota(jnp.int32, (SLOT, LANES), 1) % HD >= ROT

    def parts(v):
        a = v.astype(BF16)
        r = v - a.astype(F32)
        b = r.astype(BF16)
        c = (r - b.astype(F32)).astype(BF16)
        return jnp.concatenate([a, b, c], axis=0)

    cos_ref[...] = jnp.where(rest, 1.0, t_dot(parts(jnp.cos(angle)), (low + high).astype(BF16)))
    sine_ref[...] = t_dot(parts(jnp.sin(angle)), (high - low).astype(BF16))


def partner(v):
    lane = lax.broadcasted_iota(jnp.int32, v.shape, 1) % HD
    return jnp.where(lane < HALF, pltpu.roll(v, LANES - HALF, 1), pltpu.roll(v, HALF, 1))


def rope(v, cos, sine):
    return v * cos + partner(v) * sine


def unrope(v, cos, sine):
    return v * cos - partner(v) * sine


def top_and_rest(v):
    top = v.astype(BF16)
    return top, (v - top.astype(F32)).astype(BF16)


def rows_of(first, count):
    return pl.ds(pl.multiple_of(first, count), count)


class Ring:
    def __init__(self, source, stage, slots, final, recv, send, place, right, left):
        self.source, self.stage, self.slots, self.final = source, stage, slots, final
        self.recv, self.send, self.place = recv, send, place
        self.to = (right, left)
        self.rows = stage.shape[1]

    def copy(self, way, src, dst, step):
        return pltpu.make_async_remote_copy(
            src_ref=src, dst_ref=dst, send_sem=self.send.at[way], recv_sem=self.recv.at[way, step],
            device_id={"dp": self.to[way]}, device_id_type=MESH,
        )

    def at(self, chunk, way):
        return rows_of((chunk * 2 + way) * self.rows, self.rows)

    def chunk(self, way, back):
        return lax.rem(self.place + 2 * RING - back, RING) if way == 0 else lax.rem(self.place + RING + back, RING)

    def event(self, e):
        last = RING - 1
        for way in range(2):
            stage, slots, source, final = self.stage, self.slots, self.source, self.final

            @pl.when(e == 0)
            def _():
                stage[way] = source[self.at(self.chunk(way, 0), way), :].astype(BF16)
                self.copy(way, stage.at[way], slots.at[way, 0], 0).start()

            @pl.when((e >= 1) & (e <= last))
            def _():
                got = slots.at[way, e - 1]
                self.copy(way, stage.at[way], got, e - 1).wait_recv()
                own = self.at(self.chunk(way, e), way)
                total = (slots[way, e - 1].astype(F32) + source[own, :]).astype(BF16)
                self.copy(way, stage.at[way], got, e - 1).wait_send()

                @pl.when(e < last)
                def _():
                    slots[way, e - 1] = total
                    self.copy(way, got, slots.at[way, e], e).start()

                @pl.when(e == last)
                def _():
                    final[own, :] = total
                    self.copy(way, final.at[own, :], final.at[own, :], e).start()

            @pl.when(e > last)
            def _():
                here = final.at[self.at(self.chunk(way, e - RING), way), :]
                self.copy(way, stage.at[way], here, e - 1).wait_recv()
                self.copy(way, here, here, e - 1).wait_send()

                @pl.when(e < EVENTS - 1)
                def _():
                    self.copy(way, here, here, e).start()


class Scatter:
    def __init__(self, part, mate_in, cross_in, send, recv, m, mate, cross):
        self.part, self.mate_in, self.cross_in, self.send, self.recv = part, mate_in, cross_in, send, recv
        self.m, self.mate, self.cross = m, mate, cross

    def copy(self, src, dst, index, to):
        return pltpu.make_async_remote_copy(
            src_ref=src, dst_ref=dst, send_sem=self.send.at[index], recv_sem=self.recv.at[index],
            device_id={"mp": to}, device_id_type=MESH,
        )

    def to_mate(self, b):
        index = (b // 4) * 2 + b % 2
        return self.copy(self.part.at[pl.ds(b * BLK, BLK), :], self.mate_in.at[index], index, self.mate)

    def to_cross(self, b):
        index = (b // 4) * 2 + b % 2
        return self.copy(self.mate_in.at[index], self.cross_in.at[b % 2], 4 + b % 2, self.cross)

    def mine(self, b):
        return self.m % 2 == (b // 2) % 2

    def offer(self, b):
        @pl.when(jnp.logical_not(self.mine(b)))
        def _():
            self.to_mate(b).start()

    def collect(self, b):
        index = (b // 4) * 2 + b % 2

        @pl.when(self.mine(b))
        def _():
            self.to_mate(b).wait_recv()

            @pl.when(self.m // 2 != b // 4)
            def _():
                def add(r, carry):
                    at = rows_of(r * 32, 32)
                    own = self.part[rows_of(b * BLK + r * 32, 32), :].astype(F32)
                    self.mate_in[index, at, :] = (self.mate_in[index, at, :].astype(F32) + own).astype(BF16)
                    return carry

                lax.fori_loop(0, BLK // 32, add, 0)
                self.to_cross(b).start()

    def total(self, k, at):
        own = self.part[rows_of((2 * self.m + k) * BLK + at, 32), :].astype(F32)
        index = (self.m // 2) * 2 + k
        return own + self.mate_in[index, rows_of(at, 32), :].astype(F32) + self.cross_in[k, rows_of(at, 32), :].astype(F32)

    def arrived(self, k):
        self.copy(self.mate_in.at[0], self.cross_in.at[k], 4 + k, self.cross).wait_recv()

    def drain(self, b):
        @pl.when(jnp.logical_not(self.mine(b)))
        def _():
            self.to_mate(b).wait_send()

        @pl.when(self.mine(b) & (self.m // 2 != b // 4))
        def _():
            self.to_cross(b).wait_send()


def layer_kernel(
    heads,
    doc_ref, tok_hbm, grad_hbm, ag_ref, as_ref, wq_ref, bq_ref, wk_ref, bk_ref, wv_ref, bv_ref, wo_ref, ob_ref, mg_ref, ms_ref,
    wu_hbm, bu_ref, wd_hbm,
    bout_hbm, ingrad_hbm, fdown_hbm, fup_hbm, fout_hbm, fqkv_hbm, kvg_hbm, vec_hbm,
    xs, gm, outp, em, gdown, gup, gout, gqkv, q, kv, dctx, dd, cos, sine, ctx, dqh, dk, dv, dqkv, wqkv, wo, wu, wd, bqkv, gsum,
    own_x, io,
    st_d, sl_d, f_d, st_u, sl_u, f_u, st_o, sl_o, f_o, st_q, sl_q, f_q,
    mo, co, me_, ce, kvx, vecx, kvg,
    loc, ag_send, ag_recv, rr, rs_, so_s, so_r, se_s, se_r, bf_s, bf_r,
):
    pairs = (heads + 1) // 2
    width = pairs * LANES
    used = heads * HD
    depth = tok_hbm.shape[1]
    ff = wu.shape[1]
    m = lax.axis_index("mp")
    d = lax.axis_index("dp")
    mate = m + 1 - 2 * (m % 2)
    cross = (m + 2) % MP
    far = (mate + 2) % MP
    inner, outer = d % RING, d // RING
    place = jnp.where(inner % 2 == 0, inner // 2, RING - 1 - inner // 2)

    def seat(p):
        return outer * RING + jnp.where(p < RING // 2, 2 * p, 2 * (RING - 1 - p) + 1)

    right, left = seat((place + 1) % RING), seat((place + RING - 1) % RING)

    local = [
        pltpu.make_async_copy(tok_hbm, xs.at[rows_of(m * SHARD, SHARD), :], loc.at[0]),
        pltpu.make_async_copy(wu_hbm, wu, loc.at[1]),
        pltpu.make_async_copy(wd_hbm, wd, loc.at[2]),
        pltpu.make_async_copy(tok_hbm, own_x, loc.at[3]),
    ]
    for c in local:
        c.start()
    local_g = [
        pltpu.make_async_copy(grad_hbm.at[pl.ds(k * BLK, BLK), :], gm.at[rows_of(m * SHARD + k * BLK, BLK), :], loc.at[4 + k])
        for k in range(2)
    ]

    def valid(shard, k):
        return 2 * shard + k < PADBLK

    for k in range(2):
        @pl.when(valid(m, k))
        def _():
            local_g[k].start()
    gm[VALID:, :] = jnp.zeros((SLOT - VALID, depth), BF16)

    barrier = pltpu.get_barrier_semaphore()
    for to in ({"mp": mate}, {"mp": cross}, {"dp": right}, {"dp": left}):
        pl.semaphore_signal(barrier, inc=1, device_id=to, device_id_type=MESH)
    pl.semaphore_wait(barrier, 4)

    def send(src, dst, index, to):
        return pltpu.make_async_remote_copy(
            src_ref=src, dst_ref=dst, send_sem=ag_send.at[index], recv_sem=ag_recv.at[index], device_id={"mp": to}, device_id_type=MESH
        )

    def half(ref, shard, k):
        return ref.at[rows_of(shard * SHARD + k * BLK, BLK), :]

    def x_cross(shard, k):
        return send(tok_hbm.at[pl.ds(k * BLK, BLK), :], half(xs, shard, k), k, cross)

    def x_mate(shard, k):
        return send(tok_hbm.at[pl.ds(k * BLK, BLK), :], half(xs, shard, k), 2 + k, mate)

    def g_cross(shard, k):
        return send(grad_hbm.at[pl.ds(k * BLK, BLK), :], half(gm, shard, k), 4 + k, cross)

    def g_mate(shard, k):
        return send(grad_hbm.at[pl.ds(k * BLK, BLK), :], half(gm, shard, k), 6 + k, mate)

    def x_pass(shard, k):
        return send(half(xs, shard, k), half(xs, shard, k), 8 + k, mate)

    def g_pass(shard, k):
        return send(half(gm, shard, k), half(gm, shard, k), 10 + k, mate)

    for k in range(2):
        x_cross(m, k).start()
    for k in range(2):
        x_mate(m, k).start()
    for k in range(2):
        @pl.when(valid(m, k))
        def _():
            g_mate(m, k).start()
    for k in range(2):
        @pl.when(valid(m, k))
        def _():
            g_cross(m, k).start()

    build_tables(doc_ref, cos, sine)
    wqkv[:, :used] = wq_ref[...]
    bqkv[:, :used] = bq_ref[...]
    wo[:used, :] = wo_ref[...]
    if used < width:
        wqkv[:, used:width] = jnp.zeros((depth, width - used), BF16)
        bqkv[:, used:width] = jnp.zeros((1, width - used), F32)
        wo[used:, :] = jnp.zeros((width - used, depth), BF16)
    wqkv[:, width : width + HD] = wk_ref[...]
    wqkv[:, width + HD :] = wv_ref[...]
    bqkv[:, width : width + HD] = bk_ref[...]
    bqkv[:, width + HD :] = bv_ref[...]
    gup[...] = jnp.zeros_like(gup)
    gdown[...] = jnp.zeros_like(gdown)
    gout[...] = jnp.zeros_like(gout)
    gsum[...] = jnp.zeros_like(gsum)
    dqkv[VALID:, :] = jnp.zeros((SLOT - VALID, width + LANES), BF16)

    def feed_forward(ain, min_, hp, hid, dg, dpre):
        def forward(c, slot):
            first = pl.multiple_of(c * SHARD, SHARD)
            here = pl.ds(first, SHARD)

            def norm(r, carry):
                at = rows_of(first + r * 32, 32)
                to = rows_of(r * 32, 32)
                v = xs[at, :].astype(F32)
                v = v - jnp.mean(v, axis=-1, keepdims=True)
                v = v * lax.rsqrt(jnp.mean(v * v, axis=-1, keepdims=True) + EPS)
                xs[at, :] = v.astype(BF16)
                ain[to, :] = (v * ag_ref[...] + as_ref[...]).astype(BF16)
                min_[to, :] = (v * mg_ref[...] + ms_ref[...]).astype(BF16)
                return carry

            lax.fori_loop(0, SHARD // 32, norm, 0)
            ct, st = cos[here, :], sine[here, :]
            qf = dot(ain[...], wqkv[:, :width]) + bqkv[:, :width]
            for p in range(pairs):
                q[p, here, :] = (rope(qf[:, p * LANES : (p + 1) * LANES], ct, st) * HD**-0.5).astype(BF16)
            kvf = dot(ain[...], wqkv[:, width:]) + bqkv[:, width:]
            is_key = lax.broadcasted_iota(jnp.int32, (SHARD, LANES), 1) < HD
            kv[here, :] = jnp.where(is_key, rope(kvf, ct, st), kvf).astype(BF16)
            hp[...] = dot(min_[...], wu[...])

            def act(r, carry):
                to = rows_of(r * 16, 16)
                v = hp[to, :] + bu_ref[...]
                cdf = 0.5 * (1.0 + lax.erf(v * (0.5**0.5)))
                pdf = jnp.exp(-0.5 * v * v) * (2.0 * jnp.pi) ** -0.5
                hid[slot, to, :] = (v * cdf).astype(BF16)
                dg[slot, to, :] = (cdf + v * pdf).astype(BF16)
                return carry

            lax.fori_loop(0, SHARD // 16, act, 0)
            outp[here, :] = dot(hid[slot], wd[...]).astype(BF16)

        def backward(c, slot):
            first = pl.multiple_of(c * SHARD, SHARD)
            here = pl.ds(first, SHARD)
            g = gm[here, :]
            dc = dot_t(g, wo[...]).astype(BF16)
            for p in range(pairs):
                dctx[p, here, :] = dc[:, p * LANES : (p + 1) * LANES]
            hp[...] = dot_t(g, wd[...])

            def back(r, carry):
                acc, gacc = carry
                to = rows_of(r * 16, 16)
                v = hp[to, :] * dg[slot, to, :].astype(F32)
                dpre[to, :] = v.astype(BF16)
                gv = gm[rows_of(first + r * 16, 16), :].astype(F32)
                return acc + v[:8] + v[8:], gacc + gv[:8] + gv[8:]

            acc, gacc = lax.fori_loop(0, SHARD // 16, back, (jnp.zeros((8, ff), F32), jnp.zeros((8, depth), F32)))
            gsum[:8, :] += gacc
            gsum[8:, :] += acc
            em[here, :] = (dot_t(dpre[...], wu[...]) * mg_ref[...]).astype(BF16)
            gup[...] += t_dot(xs[here, :], dpre[...])
            gdown[...] += t_dot(hid[slot], g)

        def step(s, carry):
            early = s < 4
            which = jnp.where(early, s // 2, 2 + s % 2)
            is_forward = jnp.where(early, s % 2 == 0, s < 6)
            shard = jnp.where(which == 0, m, jnp.where(which == 1, mate, jnp.where(which == 2, cross, far)))

            @pl.when(s == 0)
            def _():
                for c in local:
                    c.wait()

            @pl.when(s == 1)
            def _():
                for k in range(2):
                    @pl.when(valid(m, k))
                    def _():
                        local_g[k].wait()

            @pl.when(s == 2)
            def _():
                for k in range(2):
                    x_mate(mate, k).wait_recv()

            @pl.when(s == 3)
            def _():
                for k in range(2):
                    x_cross(cross, k).wait_recv()
                    x_pass(cross, k).start()
                for k in range(2):
                    @pl.when(valid(mate, k))
                    def _():
                        g_mate(mate, k).wait_recv()

            @pl.when(s == 5)
            def _():
                for k in range(2):
                    x_pass(far, k).wait_recv()

            @pl.when(s == 4)
            def _():
                for k in range(2):
                    x_pass(cross, k).wait_send()

            @pl.when(s == 6)
            def _():
                for k in range(2):
                    @pl.when(valid(cross, k))
                    def _():
                        g_cross(cross, k).wait_recv()
                        g_pass(cross, k).start()

            @pl.when(s == 7)
            def _():
                for k in range(2):
                    @pl.when(valid(far, k))
                    def _():
                        g_pass(far, k).wait_recv()

            @pl.when(is_forward)
            def _():
                forward(shard, which % 2)

            @pl.when(jnp.logical_not(is_forward))
            def _():
                backward(shard, which % 2)

            return carry

        lax.fori_loop(0, 8, step, 0)

    sh16 = pltpu.VMEM((SHARD, depth), BF16)
    pl.run_scoped(
        feed_forward, sh16, sh16, pltpu.VMEM((SHARD, ff), F32), pltpu.VMEM((2, SHARD, ff), BF16), pltpu.VMEM((2, SHARD, ff), BF16),
        pltpu.VMEM((SHARD, ff), BF16),
    )
    for k in range(2):
        x_cross(m, k).wait_send()
        x_mate(m, k).wait_send()

        @pl.when(valid(m, k))
        def _():
            g_cross(m, k).wait_send()
            g_mate(m, k).wait_send()

        @pl.when(valid(cross, k))
        def _():
            g_pass(cross, k).wait_send()

    gout[used : used + 8, :] = jnp.concatenate(
        [jnp.sum(gsum[:8, :], axis=0, keepdims=True), jnp.sum(gsum[8:, :], axis=0, keepdims=True), jnp.zeros((6, depth), F32)], axis=0
    )
    ring = lambda n, *refs: Ring(*refs, rr.at[n], rs_.at[n], place, right, left)
    ring_d = ring(0, gdown, st_d, sl_d, f_d)
    ring_u = ring(1, gup, st_u, sl_u, f_u)
    ring_o = ring(2, gout, st_o, sl_o, f_o)
    ring_q = ring(3, gqkv, st_q, sl_q, f_q)
    scat_o = Scatter(outp, mo, co, so_s, so_r, m, mate, cross)
    scat_e = Scatter(em, me_, ce, se_s, se_r, m, mate, cross)
    ends = doc_ends(doc_ref)
    lane = lax.broadcasted_iota(jnp.int32, (BLK, LANES), 1)
    low = lane < HD
    fwd_steps = NBLK * heads
    bwd_steps = PADBLK * heads
    steps = fwd_steps + bwd_steps

    def attention(kx, vx, probs, scores, total):
        for b in range(NBLK):
            at = pl.ds(b * BLK, BLK)
            v = kv[at, :].astype(F32)
            t = pltpu.roll(v, HD, 1)
            kx[at, :] = jnp.where(low, v, t).astype(BF16)
            vx[at, :LANES] = jnp.where(low, t, v).astype(BF16)
            vx[at, LANES:] = jnp.ones((BLK, LANES), BF16)
        dk[...] = jnp.zeros_like(dk)
        dv[...] = jnp.zeros_like(dv)

        def head_lanes(ref, p, at, side):
            return jnp.where(lane // HD == side, ref[p, at, :].astype(F32), 0.0).astype(BF16)

        def forward(i, h):
            at = pl.ds(i * BLK, BLK)
            blocks = key_blocks(i)
            slot = i * BLK + lax.broadcasted_iota(jnp.int32, (BLK, 1), 0)
            begin = doc_begin(slot, ends)
            qb = head_lanes(q, h // 2, at, h % 2)
            peak = jnp.full((BLK, BLK), -1e30, F32)
            for n, j in enumerate(blocks):
                s = dot_t(qb, kx[pl.ds(j * BLK, BLK), :])
                key = j * BLK + lax.broadcasted_iota(jnp.int32, (BLK, BLK), 1)
                ok = key >= begin
                if i == j:
                    ok = ok & (key <= slot)
                s = jnp.where(ok, s, -1e30)
                scores[:, n * BLK : (n + 1) * BLK] = s
                peak = jnp.maximum(peak, s)
            top = jnp.max(peak, axis=-1, keepdims=True)
            acc = jnp.zeros((BLK, 2 * LANES), F32)
            for n, j in enumerate(blocks):
                e = jnp.exp(scores[:, n * BLK : (n + 1) * BLK] - top).astype(BF16)
                probs[h, SLOTS[(i, j)]] = e
                acc = acc + dot(e, vx[pl.ds(j * BLK, BLK), :])
            total[h] = acc

            @pl.when(h == heads - 1)
            def _():
                extra = jnp.zeros((BLK, LANES), F32)
                context = []
                for p in range(pairs):
                    full = 2 * p + 1 < heads
                    norm = jnp.where(low, total[2 * p, :, LANES:], total[2 * p + 1, :, LANES:] if full else 1.0)
                    c = jnp.where(low, total[2 * p, :, :LANES], total[2 * p + 1, :, :LANES] if full else 0.0)
                    norm = 1.0 / norm
                    c = c * norm
                    context.append(c.astype(BF16))
                    ctx[at, p * LANES : (p + 1) * LANES] = context[p]
                    if i < PADBLK:
                        dcs = (dctx[p, at, :].astype(F32) * norm).astype(BF16)
                        dctx[p, at, :] = dcs
                        prod = dcs.astype(F32) * c
                        for side in range(2 if full else 1):
                            first = 2 * (2 * p + side)
                            r = -jnp.sum(jnp.where(low if side == 0 else ~low, prod, 0.0), axis=-1, keepdims=True)
                            r_top = r.astype(BF16).astype(F32)
                            extra = jnp.where(lane == first, r_top, jnp.where(lane == first + 1, r - r_top, extra))
                if i < PADBLK:
                    dd[at, :] = extra.astype(BF16)
                outp[at, :] = (dot(jnp.concatenate(context, axis=1), wo[...]) + outp[at, :].astype(F32)).astype(BF16)
                scat_o.offer(i)
                if i > 0:
                    scat_o.collect(i - 1)

        def backward(i, h):
            at = pl.ds(i * BLK, BLK)
            dc = head_lanes(dctx, h // 2, at, h % 2)
            rest = jnp.where(lane // 2 == h, dd[at, :].astype(F32), 0.0).astype(BF16)
            lhs = jnp.concatenate([dc, rest], axis=1)
            qb = head_lanes(q, h // 2, at, h % 2)
            acc = jnp.zeros((BLK, LANES), F32)
            for j in key_blocks(i):
                jat = pl.ds(j * BLK, BLK)
                e = probs[h, SLOTS[(i, j)]]
                ds = (e.astype(F32) * dot_t(lhs, vx[jat, :])).astype(BF16)
                acc = acc + dot(ds, kx[jat, :])
                dk[jat, :] += t_dot(ds, qb)
                dv[jat, :] += t_dot(e, dc)
            dqh[h] = acc

            @pl.when(h == heads - 1)
            def _():
                ct, st = cos[at, :], sine[at, :]
                for p in range(pairs):
                    full = 2 * p + 1 < heads
                    v = jnp.where(low, dqh[2 * p], dqh[2 * p + 1] if full else 0.0)
                    dqkv[at, p * LANES : (p + 1) * LANES] = (unrope(v, ct, st) * HD**-0.5).astype(BF16)
                keys = dk[at, :]
                values = dv[at, :]
                keys = keys + pltpu.roll(keys, HD, 1)
                values = values + pltpu.roll(values, HD, 1)
                dqkv[at, width:] = jnp.where(low, unrope(keys, ct, st), values).astype(BF16)
                em[at, :] = (dot_t(dqkv[at, :], wqkv[...]) * ag_ref[...] + em[at, :].astype(F32)).astype(BF16)
                scat_e.offer(i)
                if i < PADBLK - 1:
                    scat_e.collect(i + 1)

        def events(r, t, begin, count):
            lo = jnp.maximum(t - begin, 0) * EVENTS // count
            hi = jnp.minimum(jnp.maximum(t + 1 - begin, 0) * EVENTS // count, EVENTS)

            @pl.when(lo < hi)
            def _():
                r.event(lo)

        def step(t, carry):
            events(ring_d, t, 0, steps)
            events(ring_u, t, -1, steps)

            @pl.when(t < fwd_steps)
            def _():
                lax.switch(t // heads, [partial(forward, i) for i in range(NBLK)], t % heads)

            @pl.when(t == fwd_steps)
            def _():
                scat_o.collect(NBLK - 1)
                gout[:used, :] = t_dot(ctx[...], gm[...])[:used, :]

            @pl.when(t >= fwd_steps)
            def _():
                events(ring_o, t, fwd_steps + 1, EVENTS)
                lax.switch((t - fwd_steps) // heads, [partial(backward, i) for i in reversed(range(PADBLK))], (t - fwd_steps) % heads)

            return carry

        lax.fori_loop(0, steps, step, 0)

    pl.run_scoped(
        attention, pltpu.VMEM((SLOT, LANES), BF16), pltpu.VMEM((SLOT, 2 * LANES), BF16), pltpu.VMEM((heads, NSLOT, BLK, BLK), BF16),
        pltpu.VMEM((BLK, (BAND + 1) * BLK), F32), pltpu.VMEM((heads, BLK, 2 * LANES), F32),
    )

    out_down = pltpu.make_async_copy(f_d, fdown_hbm, loc.at[0])
    out_up = pltpu.make_async_copy(f_u, fup_hbm, loc.at[1])
    out_out = pltpu.make_async_copy(f_o, fout_hbm, loc.at[2])
    out_down.start()
    out_up.start()
    out_out.start()
    scat_e.collect(0)
    grads = t_dot(xs[:VALID, :], dqkv[:VALID, :])
    gqkv[...] = grads
    sums = jnp.sum(dqkv[:VALID, :].astype(F32), axis=0, keepdims=True)
    for piece in range((width + LANES) // HD):
        part = sums[:, piece // 2 * LANES : piece // 2 * LANES + LANES]
        part = jnp.broadcast_to(part, (8, LANES))
        if piece % 2 == 0:
            part = pltpu.roll(part, HD, 1)
        gqkv[piece * 8 : piece * 8 + 8, used:width] = part[:, HD:]
    ring_q.event(0)

    for k in range(2):
        scat_o.arrived(k)

        def finish_out(r, carry):
            at = pl.multiple_of(r * 32, 32)
            v = own_x[rows_of(k * BLK + at, 32), :].astype(F32) + scat_o.total(k, at) + ob_ref[...]
            io[rows_of(k * BLK + at, 32), :] = v.astype(BF16)
            return carry

        lax.fori_loop(0, BLK // 32, finish_out, 0)
    out_block = pltpu.make_async_copy(io, bout_hbm, loc.at[3])
    out_block.start()

    def tail(e, carry):
        ring_q.event(e)
        return carry

    lax.fori_loop(1, EVENTS, tail, 0)
    out_block.wait()
    for k in range(2):
        @pl.when(valid(m, k))
        def _():
            scat_e.arrived(k)

            def finish_in(r, carry):
                at = pl.multiple_of(r * 32, 32)
                v = own_x[rows_of(k * BLK + at, 32), :].astype(F32)
                v = v - jnp.mean(v, axis=-1, keepdims=True)
                inv = lax.rsqrt(jnp.mean(v * v, axis=-1, keepdims=True) + EPS)
                v = v * inv
                e = scat_e.total(k, at)
                e = inv * (e - jnp.mean(e, axis=-1, keepdims=True) - v * jnp.mean(e * v, axis=-1, keepdims=True))
                g = gm[rows_of((2 * m + k) * BLK + at, 32), :].astype(F32)
                io[rows_of(k * BLK + at, 32), :] = (e + g).astype(BF16)
                return carry

            lax.fori_loop(0, BLK // 32, finish_in, 0)

        @pl.when(jnp.logical_not(valid(m, k)))
        def _():
            io[pl.ds(k * BLK, BLK), :] = jnp.zeros((BLK, depth), BF16)
    out_in = pltpu.make_async_copy(io, ingrad_hbm, loc.at[4])
    out_in.start()
    out_q = pltpu.make_async_copy(f_q, fqkv_hbm, loc.at[3])
    out_q.start()

    ones = jnp.ones((8, 2 * LANES), BF16)

    def row_sums(weight, grad, n):
        acc = jnp.zeros((8, depth), F32)
        for c in range(0, n, LANES):
            for part in top_and_rest(weight[:, c : c + LANES].astype(F32) * grad[:, c : c + LANES].astype(F32)):
                acc = acc + dot_t(ones[:, :LANES], part)
        return acc[:1]

    def times(vector, weight):
        acc = jnp.zeros((8, depth), F32)
        for part in top_and_rest(jnp.broadcast_to(vector, (8, vector.shape[1]))):
            acc = acc + dot_t(part, weight[...])
        return acc[:1]

    lane_row = lax.broadcasted_iota(jnp.int32, (1, LANES), 1)
    biases = []
    for c in range((width + LANES) // LANES):
        a = f_q[16 * c : 16 * c + 16, width - LANES : width].astype(F32)
        first, second = pltpu.roll(a[:8], HD, 1)[:1], a[8:9]
        biases.append(jnp.where(lane_row < HD, first, second))
    up_bias = f_o[used : used + 16, :].astype(F32)[1:2]
    vecx[0] = jnp.concatenate(
        [
            row_sums(wqkv, f_q, width + LANES),
            times(jnp.concatenate(biases, axis=1), wqkv),
            row_sums(wu, f_u, ff),
            times(up_bias, wu),
            jnp.concatenate([biases[-1], jnp.zeros((1, depth - LANES), F32)], axis=1),
            jnp.zeros((3, depth), F32),
        ],
        axis=0,
    )
    kvx[0] = f_q[:, width:]

    def swap(stage, to):
        def one(ref, index):
            return pltpu.make_async_remote_copy(
                src_ref=ref.at[2 * stage], dst_ref=ref.at[2 * stage + 1], send_sem=bf_s.at[index], recv_sem=bf_r.at[index],
                device_id={"mp": to}, device_id_type=MESH,
            )

        return one(kvx, 2 * stage), one(vecx, 2 * stage + 1)

    for stage, to in ((0, mate), (1, cross)):
        both = swap(stage, to)
        for c in both:
            c.start()
        for c in both:
            c.wait()
        a, b = 2 * stage, 2 * stage + 1
        kv_sum = kvx[a].astype(F32) + kvx[b].astype(F32)
        vec_sum = vecx[a] + vecx[b]
        if stage == 0:
            kvx[2] = kv_sum.astype(BF16)
            vecx[2] = vec_sum
        else:
            kvg[...] = kv_sum
            vecx[4] = vec_sum
    finals = [pltpu.make_async_copy(kvg, kvg_hbm, loc.at[5]), pltpu.make_async_copy(vecx.at[4], vec_hbm, loc.at[6])]
    for c in finals:
        c.start()
    for b in range(NBLK):
        scat_o.drain(b)
        if b < PADBLK:
            scat_e.drain(b)
    for c in finals + [out_down, out_up, out_out, out_q, out_in]:
        c.wait()


VM = pl.BlockSpec(memory_space=pltpu.VMEM)
SM = pl.BlockSpec(memory_space=pltpu.SMEM)
ANY = pl.BlockSpec(memory_space=pl.ANY)


def run_layer(heads, doc, tokens, grads, small, wu, bu, wd):
    depth = tokens.shape[1]
    ff = wu.shape[1]
    pairs = (heads + 1) // 2
    width = pairs * LANES
    wide = width + LANES
    sh = jax.ShapeDtypeStruct
    vm = pltpu.VMEM
    dma = pltpu.SemaphoreType.DMA

    def ring_refs(rows, columns):
        half = rows // (2 * RING)
        return [vm((2, half, columns), BF16), vm((2, RING - 1, half, columns), BF16), vm((rows, columns), BF16)]

    scratch = [
        vm((SLOT, depth), BF16), vm((SLOT, depth), BF16), vm((SLOT, depth), BF16), vm((SLOT, depth), BF16),
        vm((ff, depth), F32), vm((depth, ff), F32), vm((width, depth), F32), vm((depth, wide), F32),
        vm((pairs, SLOT, LANES), BF16), vm((SLOT, LANES), BF16), vm((pairs, SLOT, LANES), BF16), vm((SLOT, LANES), BF16),
        vm((SLOT, LANES), F32), vm((SLOT, LANES), F32), vm((SLOT, width), BF16), vm((heads, BLK, LANES), F32),
        vm((SLOT, LANES), F32), vm((SLOT, LANES), F32), vm((SLOT, wide), BF16), vm((depth, wide), BF16), vm((width, depth), BF16),
        vm((depth, ff), BF16), vm((ff, depth), BF16), vm((1, wide), F32), vm((16, depth), F32),
        vm((SHARD, depth), BF16), vm((SHARD, depth), BF16),
        *ring_refs(ff, depth), *ring_refs(depth, ff), *ring_refs(width, depth), *ring_refs(depth, wide),
        vm((4, BLK, depth), BF16), vm((2, BLK, depth), BF16), vm((4, BLK, depth), BF16), vm((2, BLK, depth), BF16),
        vm((4, depth, LANES), BF16), vm((5, 8, depth), F32), vm((depth, LANES), F32),
        dma((8,)), dma((12,)), dma((12,)), dma((4, 2, EVENTS - 1)), dma((4, 2)), dma((6,)), dma((6,)), dma((6,)), dma((6,)),
        dma((4,)), dma((4,)),
    ]
    return pl.pallas_call(
        partial(layer_kernel, heads),
        out_shape=(
            sh((SHARD, depth), BF16), sh((SHARD, depth), BF16), sh((ff, depth), BF16), sh((depth, ff), BF16), sh((width, depth), BF16),
            sh((depth, wide), BF16), sh((depth, LANES), F32), sh((8, depth), F32),
        ),
        in_specs=[SM, ANY, ANY] + [VM] * 12 + [ANY, VM, ANY],
        out_specs=[ANY] * 8,
        scratch_shapes=scratch,
        compiler_params=pltpu.CompilerParams(vmem_limit_bytes=67043328, collective_id=0, has_side_effects=True),
        name="layer",
    )(doc, tokens, grads, *small, wu, bu, wd)


def per_device(
    ways,
    tokens, doc_lengths, attn_gain, attn_shift, query_weight, query_bias, key_weight, key_bias, value_weight, value_bias,
    out_weight, out_bias, mlp_gain, mlp_shift, up_weight, up_bias, down_weight, down_bias, out_grad,
):
    heads = query_weight.shape[1] // HD
    used = heads * HD
    pairs = (heads + 1) // 2
    width = pairs * LANES
    row = lambda v: v.reshape(1, -1)
    small = (
        row(attn_gain), row(attn_shift), query_weight, row(query_bias), key_weight, row(key_bias), value_weight, row(value_bias),
        out_weight, row(out_bias + down_bias), row(mlp_gain), row(mlp_shift),
    )
    block_out, input_grad, gdown, gup, gout, gqkv, gkv, vectors = run_layer(
        heads, doc_lengths, tokens, out_grad, small, up_weight, row(up_bias), down_weight
    )
    gdown, gup, gout, gqkv = (v.astype(F32) for v in (gdown, gup, gout, gqkv))
    if ways > RING:
        groups = [[i + RING * o for o in range(ways // RING)] for i in range(RING)]
        gdown, gup, gout, gqkv, gkv, vectors = lax.psum((gdown, gup, gout, gqkv, gkv, vectors), "dp", axis_index_groups=groups)
    biases = gqkv[: 8 * heads : 8, used:width].reshape(used)
    kv_bias = vectors[4, :LANES]
    g_sum, bup = gout[used], gout[used + 1]
    query_weight_grad = attn_gain[:, None] * gqkv[:, :used] + attn_shift[:, None] * biases
    kv_weight_grad = attn_gain[:, None] * gkv + attn_shift[:, None] * kv_bias
    up_weight_grad = mlp_gain[:, None] * gup + mlp_shift[:, None] * bup
    return (
        block_out, input_grad, vectors[0], vectors[1], query_weight_grad, biases, kv_weight_grad[:, :HD], kv_bias[:HD],
        kv_weight_grad[:, HD:], kv_bias[HD:], gout[:used], g_sum, vectors[2], vectors[3], up_weight_grad, bup, gdown, g_sum,
    )


def solution(mesh):
    rows = P(("dp", "mp"), None)
    placed = (
        rows, P("dp", None), P(), P(), P(None, "mp"), P("mp"), P(), P(), P(), P(), P("mp", None), P(), P(), P(),
        P(None, "mp"), P("mp"), P("mp", None), P(), rows,
    )
    outs = (
        rows, rows, P(), P(), P(None, "mp"), P("mp"), P(), P(), P(), P(), P("mp", None), P(), P(), P(),
        P(None, "mp"), P("mp"), P("mp", None), P(),
    )
    return jax.shard_map(partial(per_device, mesh.shape["dp"]), mesh=mesh, in_specs=placed, out_specs=outs, check_vma=False)
```

```python
from functools import partial

import jax
import jax.numpy as jnp
from jax import lax
from jax.experimental import pallas as pl
from jax.experimental.pallas import tpu as pltpu
from jax.sharding import PartitionSpec as P

HD = 64
ROT = 16
HALF = ROT // 2
SLOT = 2048
VALID = 1792
LONGEST = 1024
DOCS = 4
BIG = 1e30
EPS = 1e-05
BLK = 256
NBLK = SLOT // BLK
BAND = LONGEST // BLK
PADBLK = VALID // BLK
LANES = 128
MP = 4
SHARD = SLOT // MP
RING = 8
EVENTS = RING + 1
F32 = jnp.float32
BF16 = jnp.bfloat16
MESH = pl.DeviceIdType.MESH


def dot(a, b):
    return lax.dot_general(a, b, (((1,), (0,)), ((), ())), preferred_element_type=F32)


def dot_t(a, b):
    return lax.dot_general(a, b, (((1,), (1,)), ((), ())), preferred_element_type=F32)


def t_dot(a, b):
    return lax.dot_general(a, b, (((0,), (0,)), ((), ())), preferred_element_type=F32)


def key_blocks(i):
    if i >= PADBLK:
        return list(range(PADBLK, i + 1))
    return list(range(max(0, i - BAND), i + 1))


SLOTS = {}
for _i in range(NBLK):
    for _j in key_blocks(_i):
        SLOTS[(_i, _j)] = len(SLOTS)
NSLOT = len(SLOTS)
KV_ROW, Q_ROW = 256, 384


def doc_begin(slot, ends):
    begin = jnp.zeros_like(slot)
    for end in ends:
        begin = jnp.where(slot >= end, end, begin)
    return begin


def doc_ends(doc_ref):
    ends = []
    total = 0
    for d in range(DOCS):
        total = total + doc_ref[0, d]
        ends.append(total)
    return ends


def build_tables(doc_ref, cos_ref, sine_ref):
    ends = doc_ends(doc_ref)
    slot = lax.broadcasted_iota(jnp.int32, (HALF, SLOT), 1)
    freq_index = lax.broadcasted_iota(jnp.int32, (HALF, SLOT), 0)
    position = (slot - doc_begin(slot, ends)).astype(F32)
    freq = jnp.zeros((HALF, SLOT), F32)
    for i in range(HALF):
        freq = jnp.where(freq_index == i, 10000.0 ** (-(2.0 * i) / ROT), freq)
    angle = position * freq
    lane = lax.broadcasted_iota(jnp.int32, (3 * HALF, LANES), 1) % HD
    row = lax.broadcasted_iota(jnp.int32, (3 * HALF, LANES), 0) % HALF
    low = jnp.where(lane == row, 1.0, 0.0)
    high = jnp.where(lane == row + HALF, 1.0, 0.0)
    rest = lax.broadcasted_iota(jnp.int32, (SLOT, LANES), 1) % HD >= ROT

    def parts(v):
        a = v.astype(BF16)
        r = v - a.astype(F32)
        b = r.astype(BF16)
        c = (r - b.astype(F32)).astype(BF16)
        return jnp.concatenate([a, b, c], axis=0)

    cos_ref[...] = jnp.where(rest, 1.0, t_dot(parts(jnp.cos(angle)), (low + high).astype(BF16)))
    sine_ref[...] = t_dot(parts(jnp.sin(angle)), (high - low).astype(BF16))


def partner(v):
    lane = lax.broadcasted_iota(jnp.int32, v.shape, 1) % HD
    return jnp.where(lane < HALF, pltpu.roll(v, LANES - HALF, 1), pltpu.roll(v, HALF, 1))


def rope(v, cos, sine):
    return v * cos + partner(v) * sine


def unrope(v, cos, sine):
    return v * cos - partner(v) * sine


def top_and_rest(v):
    top = v.astype(BF16)
    return top, (v - top.astype(F32)).astype(BF16)


def rows_of(first, count):
    return pl.ds(pl.multiple_of(first, count), count)


class Rings:
    CHAINS = ((0, 4, 0), (1, 3, 0), (0, 3, 1), (1, 4, 1))

    def __init__(self, source, stage, slots, final, recv, send, place, right, left):
        self.source, self.stage, self.slots, self.final = source, stage, slots, final
        self.recv, self.send, self.place = recv, send, place
        self.to = (right, left)
        self.rows, self.lanes = stage.shape[2], stage.shape[3]

    def copy(self, r, chain, src, dst, step):
        return pltpu.make_async_remote_copy(
            src_ref=src, dst_ref=dst, send_sem=self.send.at[r, chain], recv_sem=self.recv.at[r, chain, step],
            device_id={"dp": self.to[self.CHAINS[chain][0]]}, device_id_type=MESH,
        )

    def at(self, r, ahead):
        chunk = lax.rem(self.place + 2 * RING + ahead, RING)
        return rows_of((r * RING + chunk) * self.rows, self.rows)

    def event(self, r, e):
        stage, slots, source, final = self.stage, self.slots, self.source, self.final
        for chain, (left, hops, side) in enumerate(self.CHAINS):
            sign = -1 if left else 1
            lanes = pl.ds(side * self.lanes, self.lanes)
            own = self.at(r, sign * (hops - e))

            @pl.when(e == 0)
            def _():
                stage[r, chain] = source[own, lanes].astype(BF16)
                self.copy(r, chain, stage.at[r, chain], slots.at[r, chain, 0], 0).start()

            @pl.when((e >= 1) & (e < hops))
            def _():
                got = slots.at[r, chain, e - 1]
                self.copy(r, chain, stage.at[r, chain], got, e - 1).wait_recv()
                slots[r, chain, e - 1] = (slots[r, chain, e - 1].astype(F32) + source[own, lanes]).astype(BF16)
                self.copy(r, chain, stage.at[r, chain], got, e - 1).wait_send()
                self.copy(r, chain, got, slots.at[r, chain, e], e).start()

        @pl.when(e == 4)
        def _():
            self.settle(r)
            self.release(r)

        for chain, (left, hops, side) in enumerate(self.CHAINS):
            sign = -1 if left else 1
            here = final.at[self.at(r, sign * (4 - e)), pl.ds(side * self.lanes, self.lanes)]

            @pl.when((e > 4) & (e <= 4 + hops))
            def _():
                self.copy(r, chain, stage.at[r, chain], here, e - 1).wait_recv()
                self.copy(r, chain, here, here, e - 1).wait_send()

            @pl.when((e > 4) & (e < 4 + hops))
            def _():
                self.copy(r, chain, here, here, e).start()

    def settle(self, r):
        for chain, (left, hops, side) in enumerate(self.CHAINS):
            got = self.slots.at[r, chain, hops - 1]
            self.copy(r, chain, self.stage.at[r, chain], got, hops - 1).wait_recv()
            self.copy(r, chain, self.stage.at[r, chain], got, hops - 1).wait_send()
        mine = self.at(r, 0)
        for side in range(2):
            lanes = pl.ds(side * self.lanes, self.lanes)
            pair = [self.slots[r, c, self.CHAINS[c][1] - 1].astype(F32) for c in (2 * side, 2 * side + 1)]
            self.final[mine, lanes] = (self.source[mine, lanes] + pair[0] + pair[1]).astype(BF16)

    def release(self, r):
        for chain, (left, hops, side) in enumerate(self.CHAINS):
            here = self.final.at[self.at(r, 0), pl.ds(side * self.lanes, self.lanes)]
            self.copy(r, chain, here, here, 4).start()


class Scatter:
    def __init__(self, part, mate_in, cross_in, send, recv, m, mate, cross):
        self.part, self.mate_in, self.cross_in, self.send, self.recv = part, mate_in, cross_in, send, recv
        self.m, self.mate, self.cross = m, mate, cross

    def copy(self, src, dst, index, to):
        return pltpu.make_async_remote_copy(
            src_ref=src, dst_ref=dst, send_sem=self.send.at[index], recv_sem=self.recv.at[index],
            device_id={"mp": to}, device_id_type=MESH,
        )

    def to_mate(self, b):
        index = (b // 4) * 2 + b % 2
        return self.copy(self.part.at[pl.ds(b * BLK, BLK), :], self.mate_in.at[index], index, self.mate)

    def to_cross(self, b):
        index = (b // 4) * 2 + b % 2
        return self.copy(self.mate_in.at[index], self.cross_in.at[b % 2], 4 + b % 2, self.cross)

    def mine(self, b):
        return self.m % 2 == (b // 2) % 2

    def offer(self, b):
        @pl.when(jnp.logical_not(self.mine(b)))
        def _():
            self.to_mate(b).start()

    def collect(self, b):
        index = (b // 4) * 2 + b % 2

        @pl.when(self.mine(b))
        def _():
            self.to_mate(b).wait_recv()

            @pl.when(self.m // 2 != b // 4)
            def _():
                def add(r, carry):
                    at = rows_of(r * 32, 32)
                    own = self.part[rows_of(b * BLK + r * 32, 32), :].astype(F32)
                    self.mate_in[index, at, :] = (self.mate_in[index, at, :].astype(F32) + own).astype(BF16)
                    return carry

                lax.fori_loop(0, BLK // 32, add, 0)
                self.to_cross(b).start()

    def total(self, k, at):
        own = self.part[rows_of((2 * self.m + k) * BLK + at, 32), :].astype(F32)
        index = (self.m // 2) * 2 + k
        return own + self.mate_in[index, rows_of(at, 32), :].astype(F32) + self.cross_in[k, rows_of(at, 32), :].astype(F32)

    def arrived(self, k):
        self.copy(self.mate_in.at[0], self.cross_in.at[k], 4 + k, self.cross).wait_recv()

    def drain(self, b):
        @pl.when(jnp.logical_not(self.mine(b)))
        def _():
            self.to_mate(b).wait_send()

        @pl.when(self.mine(b) & (self.m // 2 != b // 4))
        def _():
            self.to_cross(b).wait_send()


def layer_kernel(
    heads,
    doc_ref, tok_hbm, grad_hbm, ag_in, as_in, wq_ref, bq_in, wk_ref, bk_in, wv_ref, bv_in, wo_ref, ob_in, db_in, mg_in, ms_in,
    wu_hbm, bu_in, wd_hbm,
    bout_hbm, ingrad_hbm, fa_hbm, fb_hbm,
    xs, gm, outp, em, ga, gb, q, qt, kx, vx, dctx, dct, left_in, cos, sine, ctx, dqh, dkv, dqkv, wqkv, wo, wu, wd, bqkv, gsum, rows_in,
    own_x, io,
    st_a, sl_a, f_a, st_b, sl_b, f_b,
    mo, co, me_, ce, swap,
    loc, ag_send, ag_recv, ra_r, ra_s, rb_r, rb_s, so_s, so_r, se_s, se_r, bf_s, bf_r,
):
    pairs = (heads + 1) // 2
    width = pairs * LANES
    used = heads * HD
    depth = tok_hbm.shape[1]
    ff = wu.shape[1]
    misc = Q_ROW + used
    m = lax.axis_index("mp")
    d = lax.axis_index("dp")
    mate = m + 1 - 2 * (m % 2)
    cross = (m + 2) % MP
    far = (mate + 2) % MP
    inner, outer = d % RING, d // RING
    place = jnp.where(inner % 2 == 0, inner // 2, RING - 1 - inner // 2)

    def seat(p):
        return outer * RING + jnp.where(p < RING // 2, 2 * p, 2 * (RING - 1 - p) + 1)

    right, left = seat((place + 1) % RING), seat((place + RING - 1) % RING)
    rings_a = Rings(ga, st_a, sl_a, f_a, ra_r, ra_s, place, right, left)
    rings_b = Rings(gb, st_b, sl_b, f_b, rb_r, rb_s, place, right, left)

    local = [
        pltpu.make_async_copy(tok_hbm, xs.at[rows_of(m * SHARD, SHARD), :], loc.at[0]),
        pltpu.make_async_copy(wu_hbm, wu, loc.at[1]),
        pltpu.make_async_copy(wd_hbm, wd, loc.at[2]),
        pltpu.make_async_copy(tok_hbm, own_x, loc.at[3]),
    ]
    for c in local:
        c.start()
    local_g = [
        pltpu.make_async_copy(grad_hbm.at[pl.ds(k * BLK, BLK), :], gm.at[rows_of(m * SHARD + k * BLK, BLK), :], loc.at[4 + k])
        for k in range(2)
    ]

    def valid(shard, k):
        return 2 * shard + k < PADBLK

    for k in range(2):
        @pl.when(valid(m, k))
        def _():
            local_g[k].start()
    gm[VALID:, :] = jnp.zeros((SLOT - VALID, depth), BF16)

    barrier = pltpu.get_barrier_semaphore()
    for to in ({"mp": mate}, {"mp": cross}, {"dp": right}, {"dp": left}):
        pl.semaphore_signal(barrier, inc=1, device_id=to, device_id_type=MESH)
    pl.semaphore_wait(barrier, 4)

    def send(src, dst, index, to):
        return pltpu.make_async_remote_copy(
            src_ref=src, dst_ref=dst, send_sem=ag_send.at[index], recv_sem=ag_recv.at[index], device_id={"mp": to}, device_id_type=MESH
        )

    def half(ref, shard, k):
        return ref.at[rows_of(shard * SHARD + k * BLK, BLK), :]

    def x_cross(shard, k):
        return send(tok_hbm.at[pl.ds(k * BLK, BLK), :], half(xs, shard, k), k, cross)

    def x_mate(shard, k):
        return send(tok_hbm.at[pl.ds(k * BLK, BLK), :], half(xs, shard, k), 2 + k, mate)

    def g_cross(shard, k):
        return send(grad_hbm.at[pl.ds(k * BLK, BLK), :], half(gm, shard, k), 4 + k, cross)

    def g_mate(shard, k):
        return send(grad_hbm.at[pl.ds(k * BLK, BLK), :], half(gm, shard, k), 6 + k, mate)

    def x_pass(shard, k):
        return send(half(xs, shard, k), half(xs, shard, k), 8 + k, mate)

    def g_pass(shard, k):
        return send(half(gm, shard, k), half(gm, shard, k), 10 + k, mate)

    for k in range(2):
        x_cross(m, k).start()
    for k in range(2):
        x_mate(m, k).start()
    for k in range(2):
        @pl.when(valid(m, k))
        def _():
            g_mate(m, k).start()
    build_tables(doc_ref, cos, sine)
    for n, ref in enumerate((ag_in, as_in, mg_in, ms_in, bu_in)):
        rows_in[n : n + 1, :] = ref[...].reshape(1, depth)
    ag_row, as_row, mg_row, ms_row, bu_row = (rows_in.at[n : n + 1, :] for n in range(5))
    rows_in[5:6, :] = ob_in[...].reshape(1, depth) + db_in[...].reshape(1, depth)
    wqkv[:used, :] = wq_ref[...]
    bqkv[:, :used] = bq_in[...].reshape(1, used)
    wo[:used, :] = wo_ref[...]
    if used < width:
        wqkv[used:width, :] = jnp.zeros((width - used, depth), BF16)
        bqkv[:, used:width] = jnp.zeros((1, width - used), F32)
        wo[used:, :] = jnp.zeros((width - used, depth), BF16)
    wqkv[width : width + HD, :] = wk_ref[...]
    wqkv[width + HD :, :] = wv_ref[...]
    bqkv[:, width : width + HD] = bk_in[...].reshape(1, HD)
    bqkv[:, width + HD :] = bv_in[...].reshape(1, HD)
    ga[...] = jnp.zeros_like(ga)
    gb[...] = jnp.zeros_like(gb)
    gsum[...] = jnp.zeros_like(gsum)
    dqkv[VALID:, :] = jnp.zeros((SLOT - VALID, width + LANES), BF16)
    fwd_steps = NBLK * heads
    bwd_steps = PADBLK * heads
    steps = fwd_steps + bwd_steps
    lead = MP
    down_at, up_at = pl.ds(0, ff), pl.ds(ff, depth)

    def times(vector, weight, product):
        acc = jnp.zeros((8, depth), F32)
        for part in top_and_rest(jnp.broadcast_to(vector, (8, vector.shape[1]))):
            acc = acc + product(part, weight[...])
        return acc[:1]

    def early_rings(t):
        total = 4 * EVENTS
        hooks = lead + steps

        def one(n, carry):
            rings_a.event(n % 4, n // 4)
            return carry

        lax.fori_loop(t * total // hooks, (t + 1) * total // hooks, one, 0)

    def feed_forward(ain, min_, hp, hid, dg):
        def forward(c, which):
            half = which % 2
            first = pl.multiple_of(c * SHARD, SHARD)
            here = pl.ds(first, SHARD)

            def norm(r, carry):
                at = rows_of(first + r * 32, 32)
                to = rows_of(r * 32, 32)
                v = xs[at, :].astype(F32)
                v = v - jnp.mean(v, axis=-1, keepdims=True)
                v = v * lax.rsqrt(jnp.mean(v * v, axis=-1, keepdims=True) + EPS)
                xs[at, :] = v.astype(BF16)
                ain[to, :] = (v * ag_row[...] + as_row[...]).astype(BF16)
                min_[to, :] = (v * mg_row[...] + ms_row[...]).astype(BF16)
                return carry

            lax.fori_loop(0, SHARD // 32, norm, 0)
            ct, st = cos[here, :], sine[here, :]
            qf = dot_t(ain[...], wqkv[:width, :]) + bqkv[:, :width]
            slot = first + lax.broadcasted_iota(jnp.int32, (SHARD, LANES), 0)
            lane = lax.broadcasted_iota(jnp.int32, (SHARD, LANES), 1)
            low = lane < HD
            doc = jnp.zeros((SHARD, LANES), jnp.int32)
            for end in doc_ends(doc_ref):
                doc = jnp.where(slot >= end, doc + 1, doc)
            same = lane % HD == doc
            mark = jnp.where(same, -BIG, 0.0)
            for p in range(pairs):
                v = rope(qf[:, p * LANES : (p + 1) * LANES], ct, st) * HD**-0.5
                qt[p * LANES : (p + 1) * LANES, here] = jnp.transpose(v).astype(BF16)
                q[2 * p, here, :] = jnp.where(low, v, mark).astype(BF16)
                if 2 * p + 1 < heads:
                    q[2 * p + 1, here, :] = jnp.where(low, mark, v).astype(BF16)
            kvf = dot_t(ain[...], wqkv[width:, :]) + bqkv[:, width:]
            keys = rope(kvf, ct, st)
            other = jnp.where(same | (lane % HD > DOCS), 0.0, 1.0)
            kx[0, here, :] = jnp.where(low, keys, other).astype(BF16)
            kx[1, here, :] = jnp.where(low, other, pltpu.roll(keys, HD, 1)).astype(BF16)
            vx[0, here, :] = jnp.where(low, pltpu.roll(kvf, HD, 1), 1.0).astype(BF16)
            vx[1, here, :] = jnp.where(low, 1.0, kvf).astype(BF16)
            hp[...] = dot(min_[...], wu[...])

            def act(r, carry):
                to = rows_of(r * 16, 16)
                v = hp[to, :] + bu_row[...]
                cdf = 0.5 * (1.0 + lax.erf(v * (0.5**0.5)))
                pdf = jnp.exp(-0.5 * v * v) * (2.0 * jnp.pi) ** -0.5
                hid[half, to, :] = (v * cdf).astype(BF16)
                dg[which, to, :] = (cdf + v * pdf).astype(BF16)
                return carry

            lax.fori_loop(0, SHARD // 16, act, 0)
            outp[here, :] = dot(hid[half], wd[...]).astype(BF16)

        def backward(c, which):
            first = pl.multiple_of(c * SHARD, SHARD)
            here = pl.ds(first, SHARD)
            g = gm[here, :]
            hp[...] = dot_t(g, wd[...])

            def back(r, carry):
                acc, gacc = carry
                to = rows_of(r * 16, 16)
                v = hp[to, :] * dg[which, to, :].astype(F32)
                dg[which, to, :] = v.astype(BF16)
                gv = gm[rows_of(first + r * 16, 16), :].astype(F32)
                return acc + v[:8] + v[8:], gacc + gv[:8] + gv[8:]

            acc, gacc = lax.fori_loop(0, SHARD // 16, back, (jnp.zeros((8, ff), F32), jnp.zeros((8, depth), F32)))
            gsum[:8, :] += gacc
            gsum[8:, :] += acc
            ga[down_at, :] += t_dot(hid[which % 2], g)
            ga[up_at, :] += t_dot(xs[here, :], dg[which])

        def shard_of(which):
            return jnp.where(which == 0, m, jnp.where(which == 1, mate, jnp.where(which == 2, cross, far)))

        def after(which, hook):
            hook(0)
            here = rows_of(shard_of(which) * SHARD, SHARD)
            em[here, :] = (dot_t(dg[which], wu[...]) * mg_row[...]).astype(BF16)
            hook(1)
            dc = dot_t(gm[here, :], wo[...]).astype(BF16)
            for p in range(pairs):
                dctx[p, here, :] = dc[:, p * LANES : (p + 1) * LANES]

        def step(s, carry):
            early = s < 4
            which = jnp.where(early, s // 2, 2 + s % 2)
            is_forward = jnp.where(early, s % 2 == 0, s < 6)
            shard = shard_of(which)

            @pl.when(s == 0)
            def _():
                for c in local:
                    c.wait()

            @pl.when(s == 1)
            def _():
                for k in range(2):
                    @pl.when(valid(m, k))
                    def _():
                        local_g[k].wait()

            @pl.when(s == 2)
            def _():
                for k in range(2):
                    x_mate(mate, k).wait_recv()

            @pl.when(s == 3)
            def _():
                for k in range(2):
                    x_cross(m, k).wait_send()

                    @pl.when(valid(m, k))
                    def _():
                        g_cross(m, k).start()

                for k in range(2):
                    x_cross(cross, k).wait_recv()
                    x_pass(cross, k).start()
                for k in range(2):
                    @pl.when(valid(mate, k))
                    def _():
                        g_mate(mate, k).wait_recv()

            @pl.when(s == 5)
            def _():
                for k in range(2):
                    x_pass(far, k).wait_recv()

            @pl.when(s == 4)
            def _():
                for k in range(2):
                    x_pass(cross, k).wait_send()

            @pl.when(s == 6)
            def _():
                def ahead(which, carry):
                    after(which, lambda n: None)
                    return carry

                lax.fori_loop(0, 2, ahead, 0)
                for k in range(2):
                    @pl.when(valid(cross, k))
                    def _():
                        g_cross(cross, k).wait_recv()
                        g_pass(cross, k).start()

            @pl.when(s == 7)
            def _():
                for k in range(2):
                    @pl.when(valid(far, k))
                    def _():
                        g_pass(far, k).wait_recv()

            @pl.when(is_forward)
            def _():
                forward(shard, which)

            @pl.when(jnp.logical_not(is_forward))
            def _():
                backward(shard, which)

            return carry

        lax.fori_loop(0, 8, step, 0)
        up_bias = jnp.sum(gsum[8:, :], axis=0, keepdims=True)
        gb[used : used + 8, :] = jnp.concatenate(
            [jnp.sum(gsum[:8, :], axis=0, keepdims=True), up_bias, jnp.zeros((6, depth), F32)], axis=0
        )
        ones = jnp.ones((8, LANES), BF16)
        gain = jnp.zeros((8, depth), F32)
        for c in range(0, ff, LANES):
            for part in top_and_rest(wu[:, c : c + LANES].astype(F32) * ga[up_at, c : c + LANES]):
                gain = gain + dot_t(ones, part)
        gb[misc + 11 : misc + 12, :] = gain[:1]
        gb[misc + 12 : misc + 13, :] = times(up_bias, wu, dot_t)

        def behind(which, carry):
            after(which, lambda n: early_rings(2 * (which - 2) + n))
            return carry

        lax.fori_loop(2, MP, behind, 0)

    sh16 = pltpu.VMEM((SHARD, depth), BF16)
    pl.run_scoped(
        feed_forward, sh16, sh16, pltpu.VMEM((SHARD, ff), F32), pltpu.VMEM((2, SHARD, ff), BF16), pltpu.VMEM((MP, SHARD, ff), BF16),
    )
    for k in range(2):
        x_mate(m, k).wait_send()

        @pl.when(valid(m, k))
        def _():
            g_cross(m, k).wait_send()
            g_mate(m, k).wait_send()

        @pl.when(valid(cross, k))
        def _():
            g_pass(cross, k).wait_send()

    scat_o = Scatter(outp, mo, co, so_s, so_r, m, mate, cross)
    scat_e = Scatter(em, me_, ce, se_s, se_r, m, mate, cross)
    ends = doc_ends(doc_ref)
    lane = lax.broadcasted_iota(jnp.int32, (BLK, LANES), 1)
    low = lane < HD

    def attention(probs, scores, total):
        dkv[...] = jnp.zeros_like(dkv)
        causal = lax.broadcasted_iota(jnp.int32, (BLK, BLK), 1) <= lax.broadcasted_iota(jnp.int32, (BLK, BLK), 0)

        def forward(i, h):
            at = pl.ds(i * BLK, BLK)
            blocks = key_blocks(i)
            qb = q[h, at, :]
            half = h % 2
            peak = None
            for n, j in enumerate(blocks):
                s = dot_t(qb, kx[half, pl.ds(j * BLK, BLK), :])
                if i == j:
                    s = jnp.where(causal, s, -BIG)
                scores[:, n * BLK : (n + 1) * BLK] = s
                peak = s if peak is None else jnp.maximum(peak, s)
            top = jnp.max(peak, axis=-1, keepdims=True)
            acc = jnp.zeros((BLK, LANES), F32)
            for n, j in enumerate(blocks):
                e = jnp.exp(scores[:, n * BLK : (n + 1) * BLK] - top).astype(BF16)
                probs[h, SLOTS[(i, j)]] = e
                acc = acc + dot(e, vx[half, pl.ds(j * BLK, BLK), :])
            total[h] = acc

            @pl.when(h == heads - 1)
            def _():
                context = []
                for p in range(pairs):
                    full = 2 * p + 1 < heads
                    first, second = total[2 * p], total[2 * p + 1] if full else None
                    norm = jnp.where(low, pltpu.roll(first, HD, 1), pltpu.roll(second, HD, 1) if full else 1.0)
                    norm = 1.0 / norm
                    c = jnp.where(low, first, second if full else 0.0) * norm
                    context.append(c.astype(BF16))
                    ctx[at, p * LANES : (p + 1) * LANES] = context[p]
                    if i < PADBLK:
                        scaled = dctx[p, at, :].astype(F32) * norm
                        dcs = scaled.astype(BF16).astype(F32)
                        dct[p * LANES : (p + 1) * LANES, at] = jnp.transpose(dcs).astype(BF16)
                        prod = dcs * c
                        for side in range(2 if full else 1):
                            inside = low if side == 0 else ~low
                            r = -jnp.sum(jnp.where(inside, prod, 0.0), axis=-1, keepdims=True)
                            r_top = r.astype(BF16).astype(F32)
                            extra = jnp.where(lane % HD == 0, r_top, jnp.where(lane % HD == 1, r - r_top, 0.0))
                            left_in[2 * p + side, at, :] = jnp.where(inside, dcs, extra).astype(BF16)
                outp[at, :] = (dot(jnp.concatenate(context, axis=1), wo[...]) + outp[at, :].astype(F32)).astype(BF16)
                scat_o.offer(i)
                if i > 0:
                    scat_o.collect(i - 1)

        def backward(i, h):
            at = pl.ds(i * BLK, BLK)
            half = h % 2
            lhs = left_in[h, at, :]
            mine = rows_of(h * HD, HD)
            q_turned, d_turned = qt[mine, at], dct[mine, at]
            acc = jnp.zeros((BLK, LANES), F32)
            for j in key_blocks(i):
                jat = pl.ds(j * BLK, BLK)
                e = probs[h, SLOTS[(i, j)]]
                ds = (e.astype(F32) * dot_t(lhs, vx[half, jat, :])).astype(BF16)
                acc = acc + dot(ds, kx[half, jat, :])
                dkv[:HD, jat] += dot(q_turned, ds)
                dkv[HD:, jat] += dot(d_turned, e)
            dqh[h] = acc

            @pl.when(h == heads - 1)
            def _():
                ct, st = cos[at, :], sine[at, :]
                for p in range(pairs):
                    full = 2 * p + 1 < heads
                    v = jnp.where(low, dqh[2 * p], dqh[2 * p + 1] if full else 0.0)
                    dqkv[at, p * LANES : (p + 1) * LANES] = (unrope(v, ct, st) * HD**-0.5).astype(BF16)
                v = jnp.transpose(dkv[:, at])
                dqkv[at, width:] = jnp.where(low, unrope(v, ct, st), v).astype(BF16)
                em[at, :] = (dot(dqkv[at, :], wqkv[...]) * ag_row[...] + em[at, :].astype(F32)).astype(BF16)
                scat_e.offer(i)
                if i < PADBLK - 1:
                    scat_e.collect(i + 1)

        def out_rings(n):
            @pl.when(n < 2 * EVENTS)
            def _():
                rings_b.event(n % 2, n // 2)

        def step(t, carry):
            early_rings(lead + t)

            @pl.when(t < fwd_steps)
            def _():
                lax.switch(t // heads, [partial(forward, i) for i in range(NBLK)], t % heads)

            @pl.when(t == fwd_steps)
            def _():
                scat_o.collect(NBLK - 1)
                gb[:used, :] = t_dot(ctx[...], gm[...])[:used, :]

            @pl.when(t >= fwd_steps)
            def _():
                out_rings(t - fwd_steps)
                lax.switch((t - fwd_steps) // heads, [partial(backward, i) for i in reversed(range(PADBLK))], (t - fwd_steps) % heads)

            return carry

        lax.fori_loop(0, steps, step, 0)

    pl.run_scoped(
        attention, pltpu.VMEM((heads, NSLOT, BLK, BLK), BF16), pltpu.VMEM((BLK, (BAND + 1) * BLK), F32),
        pltpu.VMEM((heads, BLK, LANES), F32),
    )

    out_a = pltpu.make_async_copy(f_a, fa_hbm, loc.at[0])
    out_a.start()
    scat_e.collect(0)
    rows = VALID
    gb[KV_ROW : KV_ROW + LANES, :] = t_dot(dqkv[:rows, width:], xs[:rows, :])
    gb[Q_ROW:misc, :] = t_dot(dqkv[:rows, :width], xs[:rows, :])[:used, :]
    sums = jnp.sum(dqkv[:rows, :].astype(F32), axis=0, keepdims=True)
    gb[misc : misc + 1, : width + LANES] = sums
    gb[misc + 8 : misc + 9, :LANES] = sums[:, width:]
    gain = jnp.sum(wqkv[:used, :].astype(F32) * gb[Q_ROW:misc, :], axis=0, keepdims=True)
    gb[misc + 9 : misc + 10, :] = gain + jnp.sum(
        wqkv[width:, :].astype(F32) * gb[KV_ROW : KV_ROW + LANES, :], axis=0, keepdims=True
    )
    gb[misc + 10 : misc + 11, :] = times(sums, wqkv, dot)

    def tail(n, carry):
        rings_b.event(2 + n % 3, n // 3)
        return carry

    def advance(first, last):
        lax.fori_loop(3 * first, 3 * last, tail, 0)

    advance(0, 1)
    for k in range(2):
        scat_o.arrived(k)

        def finish_out(r, carry):
            at = pl.multiple_of(r * 32, 32)
            v = own_x[rows_of(k * BLK + at, 32), :].astype(F32) + scat_o.total(k, at) + rows_in[5:6, :]
            io[rows_of(k * BLK + at, 32), :] = v.astype(BF16)
            return carry

        lax.fori_loop(0, BLK // 32, finish_out, 0)
    out_block = pltpu.make_async_copy(io, bout_hbm, loc.at[1])
    out_block.start()
    advance(1, 4)

    rings_b.settle(2)
    rings_b.settle(4)
    swap[0, :16, :] = f_b[rings_b.at(2, 0), :]
    swap[0, 16:, :] = f_b[rings_b.at(4, 0), :]

    def exchange(stage, to):
        copy = pltpu.make_async_remote_copy(
            src_ref=swap.at[2 * stage], dst_ref=swap.at[2 * stage + 1], send_sem=bf_s.at[stage], recv_sem=bf_r.at[stage],
            device_id={"mp": to}, device_id_type=MESH,
        )
        copy.start()
        return copy

    copy = exchange(0, mate)
    rings_b.event(3, 4)
    copy.wait()
    swap[2] = (swap[0].astype(F32) + swap[1].astype(F32)).astype(BF16)
    exchange(1, cross).wait()
    both = swap[2].astype(F32) + swap[3].astype(F32)
    f_b[rings_b.at(2, 0), :] = both[:16].astype(BF16)
    last = lax.broadcasted_iota(jnp.int32, (16, depth), 0) >= jnp.where(place == used // 16 % RING, 8, 16)
    f_b[rings_b.at(4, 0), :] = jnp.where(last, both[16:], swap[0, 16:, :].astype(F32)).astype(BF16)
    rings_b.release(2)
    rings_b.release(4)
    advance(5, 6)
    for k in range(2):
        @pl.when(valid(m, k))
        def _():
            scat_e.arrived(k)

            def finish_in(r, carry):
                at = pl.multiple_of(r * 32, 32)
                v = own_x[rows_of(k * BLK + at, 32), :].astype(F32)
                v = v - jnp.mean(v, axis=-1, keepdims=True)
                inv = lax.rsqrt(jnp.mean(v * v, axis=-1, keepdims=True) + EPS)
                v = v * inv
                e = scat_e.total(k, at)
                e = inv * (e - jnp.mean(e, axis=-1, keepdims=True) - v * jnp.mean(e * v, axis=-1, keepdims=True))
                g = gm[rows_of((2 * m + k) * BLK + at, 32), :].astype(F32)
                own_x[rows_of(k * BLK + at, 32), :] = (e + g).astype(BF16)
                return carry

            lax.fori_loop(0, BLK // 32, finish_in, 0)

        @pl.when(jnp.logical_not(valid(m, k)))
        def _():
            own_x[pl.ds(k * BLK, BLK), :] = jnp.zeros((BLK, depth), BF16)
    out_in = pltpu.make_async_copy(own_x, ingrad_hbm, loc.at[2])
    out_in.start()
    advance(6, EVENTS)
    out_b = pltpu.make_async_copy(f_b, fb_hbm, loc.at[3])
    out_b.start()

    for b in range(NBLK):
        scat_o.drain(b)
        if b < PADBLK:
            scat_e.drain(b)
    for c in (out_a, out_b, out_block, out_in):
        c.wait()


VM = pl.BlockSpec(memory_space=pltpu.VMEM)
SM = pl.BlockSpec(memory_space=pltpu.SMEM)
ANY = pl.BlockSpec(memory_space=pl.ANY)


def run_layer(heads, doc, tokens, grads, small, wu, bu, wd):
    depth = tokens.shape[1]
    ff = wu.shape[1]
    pairs = (heads + 1) // 2
    width = pairs * LANES
    wide = width + LANES
    sh = jax.ShapeDtypeStruct
    vm = pltpu.VMEM
    dma = pltpu.SemaphoreType.DMA
    a_rows, b_rows = ff + depth, KV_ROW + 384

    def ring_refs(rows, count):
        chunk = rows // (count * RING)
        return [vm((count, 4, chunk, depth // 2), BF16), vm((count, 4, 4, chunk, depth // 2), BF16), vm((rows, depth), BF16)]

    scratch = [
        vm((SLOT, depth), BF16), vm((SLOT, depth), BF16), vm((SLOT, depth), BF16), vm((SLOT, depth), BF16),
        vm((a_rows, depth), F32), vm((b_rows, depth), F32),
        vm((heads, SLOT, LANES), BF16), vm((width, SLOT), BF16), vm((2, SLOT, LANES), BF16), vm((2, SLOT, LANES), BF16),
        vm((pairs, SLOT, LANES), BF16), vm((width, VALID), BF16), vm((heads, VALID, LANES), BF16),
        vm((SLOT, LANES), F32), vm((SLOT, LANES), F32), vm((SLOT, width), BF16), vm((heads, BLK, LANES), F32),
        vm((LANES, VALID), F32), vm((SLOT, wide), BF16), vm((wide, depth), BF16), vm((width, depth), BF16),
        vm((depth, ff), BF16), vm((ff, depth), BF16), vm((1, wide), F32), vm((16, depth), F32), vm((8, depth), F32),
        vm((SHARD, depth), BF16), vm((SHARD, depth), BF16),
        *ring_refs(a_rows, 4), *ring_refs(b_rows, 5),
        vm((4, BLK, depth), BF16), vm((2, BLK, depth), BF16), vm((4, BLK, depth), BF16), vm((2, BLK, depth), BF16),
        vm((4, 32, depth), BF16),
        dma((8,)), dma((12,)), dma((12,)), dma((4, 4, 8)), dma((4, 4)), dma((5, 4, 8)), dma((5, 4)),
        dma((6,)), dma((6,)), dma((6,)), dma((6,)), dma((2,)), dma((2,)),
    ]
    return pl.pallas_call(
        partial(layer_kernel, heads),
        out_shape=(
            sh((SHARD, depth), BF16), sh((SHARD, depth), BF16), sh((a_rows, depth), BF16), sh((b_rows, depth), BF16),
        ),
        in_specs=[SM, ANY, ANY] + [VM] * 13 + [ANY, VM, ANY],
        out_specs=[ANY] * 4,
        scratch_shapes=scratch,
        compiler_params=pltpu.CompilerParams(vmem_limit_bytes=67043328, collective_id=0, has_side_effects=True),
        name="layer",
    )(doc, tokens, grads, *small, wu, bu, wd)


def final_kernel(
    heads, ff,
    bout_hbm, ingrad_hbm, fa_hbm, fb_hbm, ag_in, as_in, mg_in, ms_in,
    bout_out, ingrad_out, attn_gain, attn_shift, qw_out, qb_out, kw_out, kb_out, vw_out, vb_out, ow_out, ob_out,
    mlp_gain, mlp_shift, uw_out, ub_out, dw_out, db_out,
    blocks, fa, fb, up, down, out, qw, kw, vw, turned, sem,
):
    depth = fa.shape[1]
    used = heads * HD
    pairs = (heads + 1) // 2
    width = pairs * LANES
    misc = Q_ROW + used
    loads = [
        pltpu.make_async_copy(fa_hbm.at[pl.ds(ff, depth), :], fa.at[pl.ds(ff, depth), :], sem.at[0]),
        pltpu.make_async_copy(fb_hbm, fb, sem.at[1]),
        pltpu.make_async_copy(fa_hbm.at[pl.ds(0, ff), :], fa.at[pl.ds(0, ff), :], sem.at[2]),
        pltpu.make_async_copy(bout_hbm, blocks.at[0], sem.at[3]),
        pltpu.make_async_copy(ingrad_hbm, blocks.at[1], sem.at[4]),
    ]
    for c in loads:
        c.start()
    row = lambda ref: ref[...].reshape(1, depth)
    ag, as_, mg, ms = row(ag_in), row(as_in), row(mg_in), row(ms_in)
    turned[...] = jnp.transpose(jnp.concatenate([mg, ms, jnp.zeros((6, depth), F32)], axis=0))
    loads[1].wait()
    extra = fb[used : used + 16, :].astype(F32)
    g_sum, up_bias = extra[:1], extra[1:2]
    ob_out[...] = g_sum.reshape(depth)
    db_out[...] = g_sum.reshape(depth)
    ub_out[...] = up_bias.reshape(ff)
    last = fb[misc : misc + 16, :].astype(F32)
    for n, ref in enumerate((attn_gain, attn_shift, mlp_gain, mlp_shift)):
        ref[...] = last[9 + n : 10 + n].reshape(depth)
    kv_bias = last[8:9, :LANES]
    kb_out[...] = kv_bias[:, :HD].reshape(HD)
    vb_out[...] = kv_bias[:, HD:].reshape(HD)
    biases = last[:1, :width]
    qb_out[...] = biases[:, :used].reshape(used)
    loads[0].wait()
    stores = []

    def store(src, dst):
        copy = pltpu.make_async_copy(src, dst, sem.at[5 + len(stores)])
        copy.start()
        stores.append(copy)

    piece = depth // 4
    for n in range(4):
        def scale(r, carry):
            at = rows_of(n * piece + r * 32, 32)
            v = fa[rows_of(ff + n * piece + r * 32, 32), :].astype(F32)
            up[at, :] = v * turned[at, 0:1] + turned[at, 1:2] * up_bias
            return carry

        lax.fori_loop(0, piece // 32, scale, 0)
        store(up.at[pl.ds(n * piece, piece), :], uw_out.at[pl.ds(n * piece, piece), :])
    for n in (3, 4):
        loads[n].wait()
    store(blocks.at[0], bout_out)
    store(blocks.at[1], ingrad_out)
    loads[2].wait()
    piece = ff // 4
    for n in range(4):
        def widen(r, carry):
            at = rows_of(n * piece + r * 32, 32)
            down[at, :] = fa[at, :].astype(F32)
            return carry

        lax.fori_loop(0, piece // 32, widen, 0)
        store(down.at[pl.ds(n * piece, piece), :], dw_out.at[pl.ds(n * piece, piece), :])
    out[...] = fb[:used, :].astype(F32)
    store(out, ow_out)

    def outer(vector, other):
        a, b = top_and_rest(vector)
        c, e = top_and_rest(other)
        return t_dot(jnp.concatenate([a, a, b, b], axis=0), jnp.concatenate([c, e, c, e], axis=0))

    qw[...] = fb[Q_ROW:misc, :].astype(F32) * ag + outer(biases[:, :used], as_)
    store(qw, qw_out)
    kv = fb[KV_ROW : KV_ROW + LANES, :].astype(F32) * ag + outer(kv_bias, as_)
    kw[...] = kv[:HD]
    vw[...] = kv[HD:]
    store(kw, kw_out)
    store(vw, vw_out)
    for c in stores:
        c.wait()


def run_final(heads, ff, block_out, input_grad, fa, fb, gains):
    shard, depth = block_out.shape
    used = heads * HD
    sh = jax.ShapeDtypeStruct
    vm = pltpu.VMEM
    line = lambda n: sh((n,), F32)
    return pl.pallas_call(
        partial(final_kernel, heads, ff),
        out_shape=(
            sh((shard, depth), BF16), sh((shard, depth), BF16), line(depth), line(depth), sh((used, depth), F32), line(used),
            sh((HD, depth), F32), line(HD), sh((HD, depth), F32), line(HD), sh((used, depth), F32), line(depth),
            line(depth), line(depth), sh((depth, ff), F32), line(ff), sh((ff, depth), F32), line(depth),
        ),
        in_specs=[ANY] * 4 + [VM] * 4,
        out_specs=[ANY, ANY, VM, VM, ANY, VM, ANY, VM, ANY, VM, ANY, VM, VM, VM, ANY, VM, ANY, VM],
        scratch_shapes=[
            vm((2, shard, depth), BF16), vm(fa.shape, fa.dtype), vm(fb.shape, fb.dtype), vm((depth, ff), F32), vm((ff, depth), F32),
            vm((used, depth), F32), vm((used, depth), F32), vm((HD, depth), F32), vm((HD, depth), F32), vm((depth, 8), F32),
            pltpu.SemaphoreType.DMA((24,)),
        ],
        compiler_params=pltpu.CompilerParams(vmem_limit_bytes=67043328),
        name="final",
    )(block_out, input_grad, fa, fb, *gains)


def per_device(
    ways,
    tokens, doc_lengths, attn_gain, attn_shift, query_weight, query_bias, key_weight, key_bias, value_weight, value_bias,
    out_weight, out_bias, mlp_gain, mlp_shift, up_weight, up_bias, down_weight, down_bias, out_grad,
):
    heads = query_weight.shape[1] // HD
    small = (
        attn_gain, attn_shift, query_weight.T, query_bias, key_weight.T, key_bias, value_weight.T, value_bias,
        out_weight, out_bias, down_bias, mlp_gain, mlp_shift,
    )
    block_out, input_grad, fa, fb = run_layer(
        heads, doc_lengths, tokens, out_grad, small, up_weight, up_bias, down_weight
    )
    if ways > RING:
        groups = [[i + RING * o for o in range(ways // RING)] for i in range(RING)]
        fa, fb = lax.psum((fa.astype(F32), fb.astype(F32)), "dp", axis_index_groups=groups)
    (
        block_out, input_grad, attn_gain_grad, attn_shift_grad, qw, qb, kw, kb, vw, vb, ow, ob, mlp_gain_grad, mlp_shift_grad,
        uw, ub, dw, db,
    ) = run_final(
        heads, up_weight.shape[1], block_out, input_grad, fa, fb, (attn_gain, attn_shift, mlp_gain, mlp_shift)
    )
    return (
        block_out, input_grad, attn_gain_grad, attn_shift_grad, qw.T, qb, kw.T, kb, vw.T, vb, ow, ob, mlp_gain_grad,
        mlp_shift_grad, uw, ub, dw, db,
    )


def solution(mesh):
    rows = P(("dp", "mp"), None)
    placed = (
        rows, P("dp", None), P(), P(), P(None, "mp"), P("mp"), P(), P(), P(), P(), P("mp", None), P(), P(), P(),
        P(None, "mp"), P("mp"), P("mp", None), P(), rows,
    )
    outs = (
        rows, rows, P(), P(), P(None, "mp"), P("mp"), P(), P(), P(), P(), P("mp", None), P(), P(), P(),
        P(None, "mp"), P("mp"), P("mp", None), P(),
    )
    return jax.shard_map(partial(per_device, mesh.shape["dp"]), mesh=mesh, in_specs=placed, out_specs=outs, check_vma=False)
```

```python
from functools import partial

import jax
import jax.numpy as jnp
from jax import lax
from jax.experimental import pallas as pl
from jax.experimental.pallas import tpu as pltpu
from jax.sharding import PartitionSpec as P

HD = 64
ROT = 16
HALF = ROT // 2
SLOT = 2048
VALID = 1792
LONGEST = 1024
DOCS = 4
BIG = 1e30
SPARE = 16
OUT_EVERY = 6
EPS = 1e-05
BLK = 256
NBLK = SLOT // BLK
BAND = LONGEST // BLK
PADBLK = VALID // BLK
LANES = 128
MP = 4
SHARD = SLOT // MP
RING = 8
EVENTS = RING + 1
F32 = jnp.float32
BF16 = jnp.bfloat16
MESH = pl.DeviceIdType.MESH


def dot(a, b):
    return lax.dot_general(a, b, (((1,), (0,)), ((), ())), preferred_element_type=F32)


def dot_t(a, b):
    return lax.dot_general(a, b, (((1,), (1,)), ((), ())), preferred_element_type=F32)


def t_dot(a, b):
    return lax.dot_general(a, b, (((0,), (0,)), ((), ())), preferred_element_type=F32)


def key_blocks(i):
    if i >= PADBLK:
        return list(range(PADBLK, i + 1))
    return list(range(max(0, i - BAND), i + 1))


SLOTS = {}
for _i in range(PADBLK):
    for _j in key_blocks(_i):
        SLOTS[(_i, _j)] = len(SLOTS)
NSLOT = len(SLOTS)
KV_ROW, Q_ROW = 256, 384


def doc_begin(slot, ends):
    begin = jnp.zeros_like(slot)
    for end in ends:
        begin = jnp.where(slot >= end, end, begin)
    return begin


def doc_ends(doc_ref):
    ends = []
    total = 0
    for d in range(DOCS):
        total = total + doc_ref[0, d]
        ends.append(total)
    return ends


def build_tables(doc_ref, cos_ref, sine_ref):
    ends = doc_ends(doc_ref)
    slot = lax.broadcasted_iota(jnp.int32, (HALF, SLOT), 1)
    freq_index = lax.broadcasted_iota(jnp.int32, (HALF, SLOT), 0)
    position = (slot - doc_begin(slot, ends)).astype(F32)
    freq = jnp.zeros((HALF, SLOT), F32)
    for i in range(HALF):
        freq = jnp.where(freq_index == i, 10000.0 ** (-(2.0 * i) / ROT), freq)
    angle = position * freq
    lane = lax.broadcasted_iota(jnp.int32, (3 * HALF, LANES), 1) % HD
    row = lax.broadcasted_iota(jnp.int32, (3 * HALF, LANES), 0) % HALF
    low = jnp.where(lane == row, 1.0, 0.0)
    high = jnp.where(lane == row + HALF, 1.0, 0.0)
    rest = lax.broadcasted_iota(jnp.int32, (SLOT, LANES), 1) % HD >= ROT

    def parts(v):
        a = v.astype(BF16)
        r = v - a.astype(F32)
        b = r.astype(BF16)
        c = (r - b.astype(F32)).astype(BF16)
        return jnp.concatenate([a, b, c], axis=0)

    cos_ref[...] = jnp.where(rest, 1.0, t_dot(parts(jnp.cos(angle)), (low + high).astype(BF16)))
    sine_ref[...] = t_dot(parts(jnp.sin(angle)), (high - low).astype(BF16))


def partner(v):
    lane = lax.broadcasted_iota(jnp.int32, v.shape, 1) % HD
    return jnp.where(lane < HALF, pltpu.roll(v, LANES - HALF, 1), pltpu.roll(v, HALF, 1))


def rope(v, cos, sine):
    return v * cos + partner(v) * sine


def unrope(v, cos, sine):
    return v * cos - partner(v) * sine


def top_and_rest(v):
    top = v.astype(BF16)
    return top, (v - top.astype(F32)).astype(BF16)


def rows_of(first, count):
    return pl.ds(pl.multiple_of(first, count), count)


class Rings:
    CHAINS = ((0, 4, 0), (1, 3, 0), (0, 3, 1), (1, 4, 1))

    def __init__(self, source, stage, slots, final, recv, send, place, right, left):
        self.source, self.stage, self.slots, self.final = source, stage, slots, final
        self.recv, self.send, self.place = recv, send, place
        self.to = (right, left)
        self.rows, self.lanes = stage.shape[2], stage.shape[3]

    def copy(self, r, chain, src, dst, step):
        return pltpu.make_async_remote_copy(
            src_ref=src, dst_ref=dst, send_sem=self.send.at[r, chain], recv_sem=self.recv.at[r, chain, step],
            device_id={"dp": self.to[self.CHAINS[chain][0]]}, device_id_type=MESH,
        )

    def at(self, r, ahead):
        chunk = lax.rem(self.place + 2 * RING + ahead, RING)
        return rows_of((r * RING + chunk) * self.rows, self.rows)

    def event(self, r, e):
        stage, slots, source, final = self.stage, self.slots, self.source, self.final
        for chain, (left, hops, side) in enumerate(self.CHAINS):
            sign = -1 if left else 1
            lanes = pl.ds(side * self.lanes, self.lanes)
            own = self.at(r, sign * (hops - e))

            @pl.when(e == 0)
            def _():
                stage[r, chain] = source[own, lanes].astype(BF16)
                self.copy(r, chain, stage.at[r, chain], slots.at[r, chain, 0], 0).start()

            @pl.when((e >= 1) & (e < hops))
            def _():
                got = slots.at[r, chain, e - 1]
                self.copy(r, chain, stage.at[r, chain], got, e - 1).wait_recv()
                slots[r, chain, e - 1] = (slots[r, chain, e - 1].astype(F32) + source[own, lanes]).astype(BF16)
                self.copy(r, chain, stage.at[r, chain], got, e - 1).wait_send()
                self.copy(r, chain, got, slots.at[r, chain, e], e).start()

        @pl.when(e == 4)
        def _():
            self.settle(r)
            self.release(r)

        for chain, (left, hops, side) in enumerate(self.CHAINS):
            sign = -1 if left else 1
            here = final.at[self.at(r, sign * (4 - e)), pl.ds(side * self.lanes, self.lanes)]

            @pl.when((e > 4) & (e <= 4 + hops))
            def _():
                self.copy(r, chain, stage.at[r, chain], here, e - 1).wait_recv()
                self.copy(r, chain, here, here, e - 1).wait_send()

            @pl.when((e > 4) & (e < 4 + hops))
            def _():
                self.copy(r, chain, here, here, e).start()

    def settle(self, r):
        for chain, (left, hops, side) in enumerate(self.CHAINS):
            got = self.slots.at[r, chain, hops - 1]
            self.copy(r, chain, self.stage.at[r, chain], got, hops - 1).wait_recv()
            self.copy(r, chain, self.stage.at[r, chain], got, hops - 1).wait_send()
        mine = self.at(r, 0)
        for side in range(2):
            lanes = pl.ds(side * self.lanes, self.lanes)
            pair = [self.slots[r, c, self.CHAINS[c][1] - 1].astype(F32) for c in (2 * side, 2 * side + 1)]
            self.final[mine, lanes] = (self.source[mine, lanes] + pair[0] + pair[1]).astype(BF16)

    def release(self, r):
        for chain, (left, hops, side) in enumerate(self.CHAINS):
            here = self.final.at[self.at(r, 0), pl.ds(side * self.lanes, self.lanes)]
            self.copy(r, chain, here, here, 4).start()


class Scatter:
    def __init__(self, part, mate_in, cross_in, send, recv, m, mate, cross):
        self.part, self.mate_in, self.cross_in, self.send, self.recv = part, mate_in, cross_in, send, recv
        self.m, self.mate, self.cross = m, mate, cross

    def copy(self, src, dst, index, to):
        return pltpu.make_async_remote_copy(
            src_ref=src, dst_ref=dst, send_sem=self.send.at[index], recv_sem=self.recv.at[index],
            device_id={"mp": to}, device_id_type=MESH,
        )

    def to_mate(self, b):
        index = (b // 4) * 2 + b % 2
        return self.copy(self.part.at[pl.ds(b * BLK, BLK), :], self.mate_in.at[index], index, self.mate)

    def to_cross(self, b):
        index = (b // 4) * 2 + b % 2
        return self.copy(self.mate_in.at[index], self.cross_in.at[b % 2], 4 + b % 2, self.cross)

    def mine(self, b):
        return self.m % 2 == (b // 2) % 2

    def offer(self, b):
        @pl.when(jnp.logical_not(self.mine(b)))
        def _():
            self.to_mate(b).start()

    def collect(self, b):
        index = (b // 4) * 2 + b % 2

        @pl.when(self.mine(b))
        def _():
            self.to_mate(b).wait_recv()

            @pl.when(self.m // 2 != b // 4)
            def _():
                def add(r, carry):
                    at = rows_of(r * 32, 32)
                    own = self.part[rows_of(b * BLK + r * 32, 32), :].astype(F32)
                    self.mate_in[index, at, :] = (self.mate_in[index, at, :].astype(F32) + own).astype(BF16)
                    return carry

                lax.fori_loop(0, BLK // 32, add, 0)
                self.to_cross(b).start()

    def total(self, k, at):
        own = self.part[rows_of((2 * self.m + k) * BLK + at, 32), :].astype(F32)
        index = (self.m // 2) * 2 + k
        return own + self.mate_in[index, rows_of(at, 32), :].astype(F32) + self.cross_in[k, rows_of(at, 32), :].astype(F32)

    def arrived(self, k):
        self.copy(self.mate_in.at[0], self.cross_in.at[k], 4 + k, self.cross).wait_recv()

    def drain(self, b):
        @pl.when(jnp.logical_not(self.mine(b)))
        def _():
            self.to_mate(b).wait_send()

        @pl.when(self.mine(b) & (self.m // 2 != b // 4))
        def _():
            self.to_cross(b).wait_send()


def layer_kernel(
    heads,
    doc_ref, tok_hbm, grad_hbm, ag_in, as_in, wq_ref, bq_in, wk_ref, bk_in, wv_ref, bv_in, wo_ref, ob_in, db_in, mg_in, ms_in,
    wu_hbm, bu_in, wd_hbm,
    bout_hbm, ingrad_hbm, fa_hbm, fb_hbm,
    xs, gm, outp, em, ga, gb, q, qt, kx, vx, dctx, dct, left_in, cos, sine, dqh, dkv, dqkv, wqkv, wo, wu, wd, bqkv, gsum, rows_in, dsum,
    min_,
    st_a, sl_a, dg, st_b, sl_b, f_b,
    mo, co, hid, ce, swap,
    loc, ag_send, ag_recv, ra_r, ra_s, rb_r, rb_s, so_s, so_r, se_s, se_r, bf_s, bf_r,
):
    pairs = (heads + 1) // 2
    width = pairs * LANES
    used = heads * HD
    depth = tok_hbm.shape[1]
    ff = wu.shape[1]
    misc = Q_ROW + used
    m = lax.axis_index("mp")
    d = lax.axis_index("dp")
    mate = m + 1 - 2 * (m % 2)
    cross = (m + 2) % MP
    far = (mate + 2) % MP
    inner, outer = d % RING, d // RING
    place = jnp.where(inner % 2 == 0, inner // 2, RING - 1 - inner // 2)

    def seat(p):
        return outer * RING + jnp.where(p < RING // 2, 2 * p, 2 * (RING - 1 - p) + 1)

    right, left = seat((place + 1) % RING), seat((place + RING - 1) % RING)
    rings_a = Rings(ga, st_a, sl_a, dg, ra_r, ra_s, place, right, left)
    rings_b = Rings(gb, st_b, sl_b, f_b, rb_r, rb_s, place, right, left)

    local = [
        pltpu.make_async_copy(tok_hbm, xs.at[rows_of(m * SHARD, SHARD), :], loc.at[0]),
        pltpu.make_async_copy(wu_hbm, wu, loc.at[1]),
        pltpu.make_async_copy(wd_hbm, wd, loc.at[2]),
    ]
    own_tokens = pltpu.make_async_copy(tok_hbm, min_, loc.at[3])
    for c in local:
        c.start()
    local_g = [
        pltpu.make_async_copy(grad_hbm.at[pl.ds(k * BLK, BLK), :], gm.at[rows_of(m * SHARD + k * BLK, BLK), :], loc.at[4 + k])
        for k in range(2)
    ]

    def valid(shard, k):
        return 2 * shard + k < PADBLK

    for k in range(2):
        @pl.when(valid(m, k))
        def _():
            local_g[k].start()
    gm[VALID:, :] = jnp.zeros((SLOT - VALID, depth), BF16)

    barrier = pltpu.get_barrier_semaphore()
    for to in ({"mp": mate}, {"mp": cross}, {"dp": right}, {"dp": left}):
        pl.semaphore_signal(barrier, inc=1, device_id=to, device_id_type=MESH)
    pl.semaphore_wait(barrier, 4)

    def send(src, dst, index, to):
        return pltpu.make_async_remote_copy(
            src_ref=src, dst_ref=dst, send_sem=ag_send.at[index], recv_sem=ag_recv.at[index], device_id={"mp": to}, device_id_type=MESH
        )

    def half(ref, shard, k):
        return ref.at[rows_of(shard * SHARD + k * BLK, BLK), :]

    def x_cross(shard, k):
        return send(tok_hbm.at[pl.ds(k * BLK, BLK), :], half(xs, shard, k), k, cross)

    def x_mate(shard, k):
        return send(tok_hbm.at[pl.ds(k * BLK, BLK), :], half(xs, shard, k), 2 + k, mate)

    def g_cross(shard, k):
        return send(grad_hbm.at[pl.ds(k * BLK, BLK), :], half(gm, shard, k), 4 + k, cross)

    def g_mate(shard, k):
        return send(grad_hbm.at[pl.ds(k * BLK, BLK), :], half(gm, shard, k), 6 + k, mate)

    def x_pass(shard, k):
        return send(half(xs, shard, k), half(xs, shard, k), 8 + k, mate)

    def g_pass(shard, k):
        return send(half(gm, shard, k), half(gm, shard, k), 10 + k, mate)

    for k in range(2):
        x_cross(m, k).start()
    for k in range(2):
        x_mate(m, k).start()
    for k in range(2):
        @pl.when(valid(m, k))
        def _():
            g_mate(m, k).start()
    for k in range(2):
        @pl.when(valid(m, k))
        def _():
            g_cross(m, k).start()

    build_tables(doc_ref, cos, sine)
    for n, ref in enumerate((ag_in, as_in, mg_in, ms_in, bu_in)):
        rows_in[n : n + 1, :] = ref[...].reshape(1, depth)
    ag_row, as_row, mg_row, ms_row, bu_row = (rows_in.at[n : n + 1, :] for n in range(5))
    rows_in[5:6, :] = ob_in[...].reshape(1, depth) + db_in[...].reshape(1, depth)
    wqkv[:used, :] = wq_ref[...]
    bqkv[:, :used] = bq_in[...].reshape(1, used)
    wo[:used, :] = wo_ref[...]
    if used < width:
        wqkv[used:width, :] = jnp.zeros((width - used, depth), BF16)
        bqkv[:, used:width] = jnp.zeros((1, width - used), F32)
        wo[used:, :] = jnp.zeros((width - used, depth), BF16)
    wqkv[width : width + HD, :] = wk_ref[...]
    wqkv[width + HD :, :] = wv_ref[...]
    bqkv[:, width : width + HD] = bk_in[...].reshape(1, HD)
    bqkv[:, width + HD :] = bv_in[...].reshape(1, HD)
    ga[...] = jnp.zeros_like(ga)
    gb[...] = jnp.zeros_like(gb)
    gsum[...] = jnp.zeros_like(gsum)
    dsum[...] = jnp.zeros_like(dsum)
    dqkv[VALID:, :] = jnp.zeros((SLOT - VALID, width + LANES), BF16)
    fwd_steps = NBLK * heads
    bwd_steps = PADBLK * heads
    steps = fwd_steps + bwd_steps
    lead = 3
    chip = m // 2
    hooks_in_loop = lead + steps - NBLK // 2 * heads
    spare = SPARE
    down_at, up_at = pl.ds(0, ff), pl.ds(ff, depth)

    def times(vector, weight, product):
        acc = jnp.zeros((8, depth), F32)
        for part in top_and_rest(jnp.broadcast_to(vector, (8, vector.shape[1]))):
            acc = acc + product(part, weight[...])
        return acc[:1]

    def early_rings(t):
        total = 4 * EVENTS
        hooks = hooks_in_loop + spare

        def one(n, carry):
            rings_a.event(n % 4, n // 4)
            return carry

        lax.fori_loop(jnp.maximum(t, 0) * total // hooks, jnp.maximum(t + 1, 0) * total // hooks, one, 0)

    scat_o = Scatter(outp, mo, co, so_s, so_r, m, mate, cross)
    scat_e = Scatter(em, hid, ce, se_s, se_r, m, mate, cross)
    ends = doc_ends(doc_ref)
    lane = lax.broadcasted_iota(jnp.int32, (BLK, LANES), 1)
    low = lane < HD

    def body(hp, probs, total):
        half_lanes = depth // 2

        def attn_in():
            return jnp.concatenate([dqkv[:SHARD, :], dqkv[SHARD : 2 * SHARD, :]], axis=1)

        def ff_forward(c):
            first = pl.multiple_of(c * SHARD, SHARD)
            here = pl.ds(first, SHARD)

            def moments(r, carry):
                for part in range(8):
                    at = rows_of(first + r * 128 + part * 16, 16)
                    v = xs[at, :].astype(F32)
                    mean = jnp.mean(v, axis=-1, keepdims=True)
                    v = v - mean
                    inv = lax.rsqrt(jnp.mean(v * v, axis=-1, keepdims=True) + EPS)
                    to = pl.ds(part * 16, 16)
                    dkv[to, rows_of(r * LANES, LANES)] = jnp.broadcast_to(mean, (16, LANES))
                    dkv[to, rows_of((4 + r) * LANES, LANES)] = jnp.broadcast_to(inv, (16, LANES))
                return carry

            lax.fori_loop(0, SHARD // 128, moments, 0)

            def norm(r, carry):
                at = rows_of(first + r * 32, 32)
                to = rows_of(r * 32, 32)
                sub = rows_of(lax.rem(r * 32, LANES), 32)
                mean = jnp.concatenate([dkv[sub, rows_of(r // 4 * LANES, LANES)]] * (depth // LANES), axis=1)
                inv = jnp.concatenate([dkv[sub, rows_of((4 + r // 4) * LANES, LANES)]] * (depth // LANES), axis=1)
                v = (xs[at, :].astype(F32) - mean) * inv
                xs[at, :] = v.astype(BF16)
                a = (v * ag_row[...] + as_row[...]).astype(BF16)
                dqkv[to, :] = a[:, :half_lanes]
                dqkv[rows_of(SHARD + r * 32, 32), :] = a[:, half_lanes:]
                min_[to, :] = (v * mg_row[...] + ms_row[...]).astype(BF16)
                return carry

            lax.fori_loop(0, SHARD // 32, norm, 0)
            ct, st = cos[here, :], sine[here, :]
            ain = attn_in()
            qf = dot_t(ain, wqkv[:width, :]) + bqkv[:, :width]
            slot = first + lax.broadcasted_iota(jnp.int32, (SHARD, LANES), 0)
            lane = lax.broadcasted_iota(jnp.int32, (SHARD, LANES), 1)
            low = lane < HD
            doc = jnp.zeros((SHARD, LANES), jnp.int32)
            for end in doc_ends(doc_ref):
                doc = jnp.where(slot >= end, doc + 1, doc)
            same = lane % HD == doc
            mark = jnp.where(same, -BIG, 0.0)
            for p in range(pairs):
                v = rope(qf[:, p * LANES : (p + 1) * LANES], ct, st) * HD**-0.5
                qt[p * LANES : (p + 1) * LANES, here] = jnp.transpose(v).astype(BF16)
                q[2 * p, here, :] = jnp.where(low, v, mark).astype(BF16)
                if 2 * p + 1 < heads:
                    q[2 * p + 1, here, :] = jnp.where(low, mark, v).astype(BF16)
            kvf = dot_t(ain, wqkv[width:, :]) + bqkv[:, width:]
            keys = rope(kvf, ct, st)
            other = jnp.where(same | (lane % HD > DOCS), 0.0, 1.0)
            kx[0, here, :] = jnp.where(low, keys, other).astype(BF16)
            kx[1, here, :] = jnp.where(low, other, pltpu.roll(keys, HD, 1)).astype(BF16)
            vx[0, here, :] = jnp.where(low, pltpu.roll(kvf, HD, 1), 1.0).astype(BF16)
            vx[1, here, :] = jnp.where(low, 1.0, kvf).astype(BF16)
            hp[...] = dot(min_[...], wu[...])

            def act(r, carry):
                to = rows_of(r * 32, 32)
                v = hp[to, :] + bu_row[...]
                cdf = 0.5 * (1.0 + lax.erf(v * (0.5**0.5)))
                pdf = jnp.exp(-0.5 * v * v) * (2.0 * jnp.pi) ** -0.5
                hid[c % 2 * 2 + r // (BLK // 32), rows_of(lax.rem(r * 32, BLK), 32), :] = (v * cdf).astype(BF16)
                dg[rows_of(first + r * 32, 32), :] = (cdf + v * pdf).astype(BF16)
                return carry

            lax.fori_loop(0, SHARD // 32, act, 0)
            outp[here, :] = dot(hid[pl.ds(c % 2 * 2, 2)].reshape(SHARD, ff), wd[...]).astype(BF16)

        def ff_backward(c, k):
            first = pl.multiple_of(c * SHARD + k * BLK, BLK)
            hp[:BLK, :] = dot_t(gm[pl.ds(first, BLK), :], wd[...])

            def back(r, carry):
                acc, gacc = carry
                at = rows_of(first + r * 32, 32)
                v = hp[rows_of(r * 32, 32), :] * dg[at, :].astype(F32)
                dg[at, :] = v.astype(BF16)
                gv = gm[at, :].astype(F32)
                acc = acc + (v[:8] + v[8:16]) + (v[16:24] + v[24:])
                return acc, gacc + (gv[:8] + gv[8:16]) + (gv[16:24] + gv[24:])

            acc, gacc = lax.fori_loop(0, BLK // 32, back, (jnp.zeros((8, ff), F32), jnp.zeros((8, depth), F32)))
            gsum[:8, :] += gacc
            gsum[8:, :] += acc

        def weights(chip):
            rows = rows_of(chip * 2 * SHARD, 2 * SHARD)
            ga[down_at, :] += t_dot(hid[...].reshape(2 * SHARD, ff), gm[rows, :])
            ga[up_at, :] += t_dot(xs[rows, :], dg[rows, :])

        def shard_of(which):
            return jnp.where(which == 0, m, jnp.where(which == 1, mate, jnp.where(which == 2, cross, far)))

        def after(shard):
            here = rows_of(shard * SHARD, SHARD)
            em[here, :] = (dot_t(dg[here, :], wu[...]) * mg_row[...]).astype(BF16)
            dc = dot_t(gm[here, :], wo[...]).astype(BF16)
            for p in range(pairs):
                dctx[p, here, :] = dc[:, p * LANES : (p + 1) * LANES]

        def norm_grads():
            up_bias = jnp.sum(gsum[8:, :], axis=0, keepdims=True)
            gb[used : used + 8, :] = jnp.concatenate(
                [jnp.sum(gsum[:8, :], axis=0, keepdims=True), up_bias, jnp.zeros((6, depth), F32)], axis=0
            )
            ones = jnp.ones((8, LANES), BF16)
            gain = jnp.zeros((8, depth), F32)
            for c in range(0, ff, LANES):
                for part in top_and_rest(wu[:, c : c + LANES].astype(F32) * ga[up_at, c : c + LANES]):
                    gain = gain + dot_t(ones, part)
            gb[misc + 11 : misc + 12, :] = gain[:1]
            gb[misc + 12 : misc + 13, :] = times(up_bias, wu, dot_t)

        causal = lax.broadcasted_iota(jnp.int32, (BLK, BLK), 1) <= lax.broadcasted_iota(jnp.int32, (BLK, BLK), 0)

        def scores(n):
            return hp.at[pl.ds(n // 3 * BLK, BLK), pl.ds(n % 3 * BLK, BLK)]

        def att_forward(i, h):
            at = pl.ds(i * BLK, BLK)
            blocks = key_blocks(i)
            qb = q[h, at, :]
            half = h % 2
            peak = None
            for n, j in enumerate(blocks):
                s = dot_t(qb, kx[half, pl.ds(j * BLK, BLK), :])
                if i == j:
                    s = jnp.where(causal, s, -BIG)
                scores(n)[...] = s
                peak = s if peak is None else jnp.maximum(peak, s)
            top = jnp.max(peak, axis=-1, keepdims=True)
            acc = jnp.zeros((BLK, LANES), F32)
            for n, j in enumerate(blocks):
                e = jnp.exp(scores(n)[...] - top).astype(BF16)
                if i < PADBLK:
                    probs[h, SLOTS[(i, j)]] = e
                acc = acc + dot(e, vx[half, pl.ds(j * BLK, BLK), :])
            total[h] = acc

            @pl.when(h == heads - 1)
            def _():
                context = []
                for p in range(pairs):
                    full = 2 * p + 1 < heads
                    first, second = total[2 * p], total[2 * p + 1] if full else None
                    norm = jnp.where(low, pltpu.roll(first, HD, 1), pltpu.roll(second, HD, 1) if full else 1.0)
                    norm = 1.0 / norm
                    c = jnp.where(low, first, second if full else 0.0) * norm
                    context.append(c.astype(BF16))
                    if i < PADBLK:
                        scaled = dctx[p, at, :].astype(F32) * norm
                        dcs = scaled.astype(BF16).astype(F32)
                        dct[p * LANES : (p + 1) * LANES, at] = jnp.transpose(dcs).astype(BF16)
                        prod = dcs * c
                        for side in range(2 if full else 1):
                            inside = low if side == 0 else ~low
                            r = -jnp.sum(jnp.where(inside, prod, 0.0), axis=-1, keepdims=True)
                            r_top = r.astype(BF16).astype(F32)
                            extra = jnp.where(lane % HD == 0, r_top, jnp.where(lane % HD == 1, r - r_top, 0.0))
                            left_in[2 * p + side, at, :] = jnp.where(inside, dcs, extra).astype(BF16)
                for p in range(pairs):
                    dctx[p, at, :] = context[p]
                outp[at, :] = (dot(jnp.concatenate(context, axis=1), wo[...]) + outp[at, :].astype(F32)).astype(BF16)
                scat_o.offer(i)
                before = (i - 1) % NBLK
                if i % (NBLK // 2) > 0:
                    scat_o.collect(before)
                else:
                    @pl.when(chip != i // (NBLK // 2))
                    def _():
                        scat_o.collect(before)

        def att_backward(i, h):
            at = pl.ds(i * BLK, BLK)
            half = h % 2
            lhs = left_in[h, at, :]
            mine = rows_of(h * HD, HD)
            q_turned, d_turned = qt[mine, at], dct[mine, at]
            acc = jnp.zeros((BLK, LANES), F32)
            for j in key_blocks(i):
                jat = pl.ds(j * BLK, BLK)
                e = probs[h, SLOTS[(i, j)]]
                ds = (e.astype(F32) * dot_t(lhs, vx[half, jat, :])).astype(BF16)
                acc = acc + dot(ds, kx[half, jat, :])
                dkv[:HD, jat] += dot(q_turned, ds)
                dkv[HD:, jat] += dot(d_turned, e)
            dqh[h] = acc

            @pl.when(h == heads - 1)
            def _():
                ct, st = cos[at, :], sine[at, :]
                for p in range(pairs):
                    full = 2 * p + 1 < heads
                    v = jnp.where(low, dqh[2 * p], dqh[2 * p + 1] if full else 0.0)
                    dqkv[at, p * LANES : (p + 1) * LANES] = (unrope(v, ct, st) * HD**-0.5).astype(BF16)
                v = jnp.transpose(dkv[:, at])
                dqkv[at, width:] = jnp.where(low, unrope(v, ct, st), v).astype(BF16)
                dsum[:1, :] += jnp.sum(dqkv[at, :].astype(F32), axis=0, keepdims=True)
                em[at, :] = (dot(dqkv[at, :], wqkv[...]) * ag_row[...] + em[at, :].astype(F32)).astype(BF16)
                scat_e.offer(i)
                if i < PADBLK - 1:
                    scat_e.collect(i + 1)

        def out_rings(n):
            @pl.when(n % OUT_EVERY == 0)
            def _():
                def one(r, carry):
                    rings_b.event(r, n // OUT_EVERY)
                    return carry

                lax.fori_loop(0, 2, one, 0)

        plan = [(0, 0, 0), (1, 0, 0), (1, 0, 1), (0, 1, 0), (1, 1, 0), (1, 1, 1), (2, 0, 0), (3, 0, 0), (3, 1, 0), (0, 2, 0), (0, 3, 0)]
        plan += [(1, 2, 0), (1, 2, 1), (1, 3, 0), (1, 3, 1), (2, 2, 0), (3, 2, 0), (3, 3, 0), (4, 0, 0)]
        before = 11
        early = NBLK // 2 * heads
        after_all = len(plan) + early
        hooked = 16 + early

        def pick(s, column):
            value = plan[0][column]
            for n, entry in enumerate(plan):
                if entry[column] != plan[0][column]:
                    value = jnp.where(s == n, entry[column], value)
            return value

        def at_step(n):
            return lambda action: pl.when(step_now[0] == n)(action)

        step_now = [None]

        def step(s, carry):
            planned = (s < before) | ((s >= before + early) & (s < after_all))
            p = jnp.where(s < before, s, s - early)
            step_now[0] = jnp.where(planned, p, -1)
            t = jnp.where(s < after_all, s - before, s - after_all + early)
            early_rings(s - hooked)

            @at_step(0)
            def _():
                for c in local:
                    c.wait()

            @at_step(1)
            def _():
                for k in range(2):
                    @pl.when(valid(m, k))
                    def _():
                        local_g[k].wait()

            @at_step(3)
            def _():
                for k in range(2):
                    x_mate(mate, k).wait_recv()

            @at_step(4)
            def _():
                for k in range(2):
                    @pl.when(valid(mate, k))
                    def _():
                        g_mate(mate, k).wait_recv()

            @at_step(7)
            def _():
                for k in range(2):
                    x_cross(m, k).wait_send()
                    x_cross(cross, k).wait_recv()
                    x_pass(cross, k).start()

            @at_step(9)
            def _():
                for k in range(2):
                    x_pass(cross, k).wait_send()

            @at_step(10)
            def _():
                for k in range(2):
                    x_pass(far, k).wait_recv()

            for k in range(2):
                @at_step(11 + k)
                def _():
                    @pl.when(valid(cross, k))
                    def _():
                        g_cross(cross, k).wait_recv()
                        g_pass(cross, k).start()

                @at_step(13 + k)
                def _():
                    @pl.when(valid(far, k))
                    def _():
                        g_pass(far, k).wait_recv()

            @pl.when(jnp.logical_not(planned) & (t == fwd_steps))
            def _():
                own_tokens.start()
                dkv[...] = jnp.zeros_like(dkv)
                for b in (NBLK // 2 - 1, NBLK - 1):
                    @pl.when(chip != b // (NBLK // 2))
                    def _():
                        scat_o.collect(b)
                for p in range(pairs):
                    some = min(used - p * LANES, LANES)
                    gb[p * LANES : p * LANES + some, :] = t_dot(dctx[p], gm[...])[:some, :]

            @pl.when(jnp.logical_not(planned) & (t >= fwd_steps))
            def _():
                out_rings(t - fwd_steps)

            shard = shard_of(pick(p, 1))
            half = pick(p, 2)
            h = t % heads
            forward_block = (t // heads + chip * (NBLK // 2)) % NBLK
            backward_block = (t - fwd_steps) // heads
            kind = jnp.where(planned, pick(p, 0), jnp.where(t < fwd_steps, 5, 6))
            lax.switch(
                kind,
                [
                    lambda: ff_forward(shard), lambda: ff_backward(shard, half), lambda: weights(shard // 2), lambda: after(shard),
                    norm_grads,
                    lambda: lax.switch(forward_block, [partial(att_forward, i) for i in range(NBLK)], h),
                    lambda: lax.switch(backward_block, [partial(att_backward, i) for i in reversed(range(PADBLK))], h),
                ],
            )
            return carry

        lax.fori_loop(0, after_all + steps - early, step, 0)

    pl.run_scoped(
        body, pltpu.VMEM((SHARD, ff), F32), pltpu.VMEM((heads, NSLOT, BLK, BLK), BF16), pltpu.VMEM((heads, BLK, LANES), F32),
    )
    for k in range(2):
        x_mate(m, k).wait_send()

        @pl.when(valid(m, k))
        def _():
            g_cross(m, k).wait_send()
            g_mate(m, k).wait_send()

        @pl.when(valid(cross, k))
        def _():
            g_pass(cross, k).wait_send()

    scat_e.collect(0)
    rows = VALID
    gb[KV_ROW : KV_ROW + LANES, :] = t_dot(dqkv[:rows, width:], xs[:rows, :])
    rings_b.event(2, 0)
    gb[Q_ROW:misc, :] = t_dot(dqkv[:rows, :width], xs[:rows, :])[:used, :]
    rings_b.event(3, 0)
    sums = dsum[:1, :]
    gb[misc : misc + 1, : width + LANES] = sums
    gb[misc + 8 : misc + 9, :LANES] = sums[:, width:]
    gain = jnp.sum(wqkv[:used, :].astype(F32) * gb[Q_ROW:misc, :], axis=0, keepdims=True)
    gb[misc + 9 : misc + 10, :] = gain + jnp.sum(
        wqkv[width:, :].astype(F32) * gb[KV_ROW : KV_ROW + LANES, :], axis=0, keepdims=True
    )
    gb[misc + 10 : misc + 11, :] = times(sums, wqkv, dot)
    rings_b.event(4, 0)

    def exchange(stage, to):
        return pltpu.make_async_remote_copy(
            src_ref=swap.at[2 * stage], dst_ref=swap.at[2 * stage + 1], send_sem=bf_s.at[stage], recv_sem=bf_r.at[stage],
            device_id={"mp": to}, device_id_type=MESH,
        )

    def finish_out(r, carry):
        at = pl.multiple_of(r * 32, 32)
        v = min_[rows_of(at, 32), :].astype(F32) + scat_o.total(r // (BLK // 32), lax.rem(at, BLK)) + rows_in[5:6, :]
        outp[rows_of(m * SHARD + at, 32), :] = v.astype(BF16)
        return carry

    def finish_in(r, carry):
        at = pl.multiple_of(r * 32, 32)
        v = min_[rows_of(at, 32), :].astype(F32)
        v = v - jnp.mean(v, axis=-1, keepdims=True)
        inv = lax.rsqrt(jnp.mean(v * v, axis=-1, keepdims=True) + EPS)
        v = v * inv
        e = scat_e.total(r // (BLK // 32), lax.rem(at, BLK))
        e = inv * (e - jnp.mean(e, axis=-1, keepdims=True) - v * jnp.mean(e * v, axis=-1, keepdims=True))
        g = gm[rows_of(m * SHARD + at, 32), :].astype(F32)
        min_[rows_of(at, 32), :] = (e + g).astype(BF16)
        return carry

    out_block = pltpu.make_async_copy(outp.at[rows_of(m * SHARD, SHARD), :], bout_hbm, loc.at[1])
    out_in = pltpu.make_async_copy(min_, ingrad_hbm, loc.at[2])

    done = (bwd_steps - 1) // OUT_EVERY

    def tail(e, carry):
        def late(n, carry):
            early_rings(hooks_in_loop + n)
            return carry

        def one(r, carry):
            step = jnp.where(r < 2, e + done, e)

            @pl.when(jnp.where(r < 2, step < EVENTS, (e != 4) | (r == 3)))
            def _():
                rings_b.event(r, step)

            return carry

        @pl.when(e == 4)
        def _():
            rings_b.settle(2)
            rings_b.settle(4)
            swap[0, :16, :] = f_b[rings_b.at(2, 0), :]
            swap[0, 16:, :] = f_b[rings_b.at(4, 0), :]
            exchange(0, mate).start()

        lax.fori_loop(0, 5, one, 0)

        @pl.when(e == 4)
        def _():
            exchange(0, mate).wait()
            swap[2] = (swap[0].astype(F32) + swap[1].astype(F32)).astype(BF16)
            exchange(1, cross).start()

        lax.fori_loop((e - 1) * spare // (EVENTS - 1), e * spare // (EVENTS - 1), late, 0)

        @pl.when(e == 4)
        def _():
            exchange(1, cross).wait()
            both = swap[2].astype(F32) + swap[3].astype(F32)
            f_b[rings_b.at(2, 0), :] = both[:16].astype(BF16)
            last = lax.broadcasted_iota(jnp.int32, (16, depth), 0) >= jnp.where(place == used // 16 % RING, 8, 16)
            f_b[rings_b.at(4, 0), :] = jnp.where(last, both[16:], swap[0, 16:, :].astype(F32)).astype(BF16)
            rings_b.release(2)
            rings_b.release(4)

        @pl.when(e == 1)
        def _():
            own_tokens.wait()
            for k in range(2):
                scat_o.arrived(k)

        @pl.when(e <= 4)
        def _():
            lax.fori_loop((e - 1) * (SHARD // 128), e * (SHARD // 128), finish_out, 0)

        @pl.when(e == 4)
        def _():
            out_block.start()

        @pl.when(e == 5)
        def _():
            for k in range(2):
                @pl.when(valid(m, k))
                def _():
                    scat_e.arrived(k)

            @pl.when(jnp.logical_not(valid(m, 1)))
            def _():
                min_[BLK:, :] = jnp.zeros((BLK, depth), BF16)

        @pl.when((e >= 5) & (e < 8))
        def _():
            limit = jnp.where(valid(m, 1), SHARD, BLK) // 32
            lax.fori_loop((e - 5) * limit // 3, (e - 4) * limit // 3, finish_in, 0)

        @pl.when(e == 7)
        def _():
            out_in.start()

        return carry

    lax.fori_loop(1, EVENTS, tail, 0)
    out_a = pltpu.make_async_copy(dg.at[: ff + depth, :], fa_hbm, loc.at[0])
    out_a.start()
    out_b = pltpu.make_async_copy(f_b, fb_hbm, loc.at[3])
    out_b.start()
    for b in range(NBLK):
        scat_o.drain(b)
        if b < PADBLK:
            scat_e.drain(b)
    for c in (out_a, out_b, out_block, out_in):
        c.wait()


VM = pl.BlockSpec(memory_space=pltpu.VMEM)
SM = pl.BlockSpec(memory_space=pltpu.SMEM)
ANY = pl.BlockSpec(memory_space=pl.ANY)


def run_layer(heads, doc, tokens, grads, small, wu, bu, wd):
    depth = tokens.shape[1]
    ff = wu.shape[1]
    pairs = (heads + 1) // 2
    width = pairs * LANES
    wide = width + LANES
    sh = jax.ShapeDtypeStruct
    vm = pltpu.VMEM
    dma = pltpu.SemaphoreType.DMA
    a_rows, b_rows = ff + depth, KV_ROW + 384

    def ring_refs(rows, count):
        chunk = rows // (count * RING)
        return [vm((count, 4, chunk, depth // 2), BF16), vm((count, 4, 4, chunk, depth // 2), BF16), vm((rows, depth), BF16)]

    scratch = [
        vm((SLOT, depth), BF16), vm((SLOT, depth), BF16), vm((SLOT, depth), BF16), vm((SLOT, depth), BF16),
        vm((a_rows, depth), F32), vm((b_rows, depth), F32),
        vm((heads, SLOT, LANES), BF16), vm((width, SLOT), BF16), vm((2, SLOT, LANES), BF16), vm((2, SLOT, LANES), BF16),
        vm((pairs, SLOT, LANES), BF16), vm((width, VALID), BF16), vm((heads, VALID, LANES), BF16),
        vm((SLOT, LANES), F32), vm((SLOT, LANES), F32), vm((heads, BLK, LANES), F32),
        vm((LANES, VALID), F32), vm((SLOT, wide), BF16), vm((wide, depth), BF16), vm((width, depth), BF16),
        vm((depth, ff), BF16), vm((ff, depth), BF16), vm((1, wide), F32), vm((16, depth), F32), vm((8, depth), F32), vm((8, wide), F32),
        vm((SHARD, depth), BF16),
        *ring_refs(a_rows, 4)[:2], vm((SLOT, ff), BF16), *ring_refs(b_rows, 5),
        vm((4, BLK, depth), BF16), vm((2, BLK, depth), BF16), vm((4, BLK, depth), BF16), vm((2, BLK, depth), BF16),
        vm((4, 32, depth), BF16),
        dma((8,)), dma((12,)), dma((12,)), dma((4, 4, 8)), dma((4, 4)), dma((5, 4, 8)), dma((5, 4)),
        dma((6,)), dma((6,)), dma((6,)), dma((6,)), dma((2,)), dma((2,)),
    ]
    return pl.pallas_call(
        partial(layer_kernel, heads),
        out_shape=(
            sh((SHARD, depth), BF16), sh((SHARD, depth), BF16), sh((a_rows, depth), BF16), sh((b_rows, depth), BF16),
        ),
        in_specs=[SM, ANY, ANY] + [VM] * 13 + [ANY, VM, ANY],
        out_specs=[ANY] * 4,
        scratch_shapes=scratch,
        compiler_params=pltpu.CompilerParams(vmem_limit_bytes=67043328, collective_id=0, has_side_effects=True),
        name="layer",
    )(doc, tokens, grads, *small, wu, bu, wd)


def final_kernel(
    heads, ff,
    bout_hbm, ingrad_hbm, fa_hbm, fb_hbm, ag_in, as_in, mg_in, ms_in,
    bout_out, ingrad_out, attn_gain, attn_shift, qw_out, qb_out, kw_out, kb_out, vw_out, vb_out, ow_out, ob_out,
    mlp_gain, mlp_shift, uw_out, ub_out, dw_out, db_out,
    blocks, fa, fb, wide, out, qw, kw, vw, turned, sem,
):
    depth = fa.shape[1]
    used = heads * HD
    pairs = (heads + 1) // 2
    width = pairs * LANES
    misc = Q_ROW + used
    stores = []

    def load(src, dst, n):
        copy = pltpu.make_async_copy(src, dst, sem.at[n])
        copy.start()
        return copy

    def store(src, dst):
        copy = pltpu.make_async_copy(src, dst, sem.at[12 + len(stores)])
        copy.start()
        stores.append(copy)

    piece = 384
    parts = (ff + depth) // piece
    small = load(fb_hbm, fb, 0)
    loads = [load(fa_hbm.at[pl.ds(n * piece, piece), :], fa.at[pl.ds(n * piece, piece), :], 1 + n) for n in range(parts)]
    passed = [load(ref, blocks.at[n], 8 + n) for n, ref in enumerate((bout_hbm, ingrad_hbm))]
    row = lambda ref: ref[...].reshape(1, depth)
    ag, as_, mg, ms = row(ag_in), row(as_in), row(mg_in), row(ms_in)
    turned[...] = jnp.transpose(jnp.concatenate([mg, ms, jnp.zeros((6, depth), F32)], axis=0))
    small.wait()
    extra = fb[used : used + 16, :].astype(F32)
    g_sum, up_bias = extra[:1], extra[1:2]
    for n in range(parts):
        loads[n].wait()
        at = n * piece
        if at < ff:
            wide[pl.ds(at, piece), :] = fa[pl.ds(at, piece), :].astype(F32)
            store(wide.at[pl.ds(at, piece), :], dw_out.at[pl.ds(at, piece), :])
        else:
            to = at - ff
            wide[pl.ds(at, piece), :] = (
                fa[pl.ds(at, piece), :].astype(F32) * turned[to : to + piece, 0:1] + turned[to : to + piece, 1:2] * up_bias
            )
            store(wide.at[pl.ds(at, piece), :], uw_out.at[pl.ds(to, piece), :])
    for n, dst in enumerate((bout_out, ingrad_out)):
        passed[n].wait()
        store(blocks.at[n], dst)
    out[...] = fb[:used, :].astype(F32)
    store(out, ow_out)
    last = fb[misc : misc + 16, :].astype(F32)
    kv_bias = last[8:9, :LANES]
    biases = last[:1, :width]

    def outer(vector, other):
        a, b = top_and_rest(vector)
        c, e = top_and_rest(other)
        return t_dot(jnp.concatenate([a, a, b, b], axis=0), jnp.concatenate([c, e, c, e], axis=0))

    qw[...] = fb[Q_ROW:misc, :].astype(F32) * ag + outer(biases[:, :used], as_)
    store(qw, qw_out)
    kv = fb[KV_ROW : KV_ROW + LANES, :].astype(F32) * ag + outer(kv_bias, as_)
    kw[...] = kv[:HD]
    vw[...] = kv[HD:]
    store(kw, kw_out)
    store(vw, vw_out)
    for n, ref in enumerate((attn_gain, attn_shift, mlp_gain, mlp_shift)):
        ref[...] = last[9 + n : 10 + n].reshape(depth)
    kb_out[...] = kv_bias[:, :HD].reshape(HD)
    vb_out[...] = kv_bias[:, HD:].reshape(HD)
    qb_out[...] = biases[:, :used].reshape(used)
    ob_out[...] = g_sum.reshape(depth)
    db_out[...] = g_sum.reshape(depth)
    ub_out[...] = up_bias.reshape(ff)
    for c in stores:
        c.wait()


def run_final(heads, ff, block_out, input_grad, fa, fb, gains):
    shard, depth = block_out.shape
    used = heads * HD
    sh = jax.ShapeDtypeStruct
    vm = pltpu.VMEM
    line = lambda n: sh((n,), F32)
    return pl.pallas_call(
        partial(final_kernel, heads, ff),
        out_shape=(
            sh((shard, depth), BF16), sh((shard, depth), BF16), line(depth), line(depth), sh((used, depth), F32), line(used),
            sh((HD, depth), F32), line(HD), sh((HD, depth), F32), line(HD), sh((used, depth), F32), line(depth),
            line(depth), line(depth), sh((depth, ff), F32), line(ff), sh((ff, depth), F32), line(depth),
        ),
        in_specs=[ANY] * 4 + [VM] * 4,
        out_specs=[ANY, ANY, VM, VM, ANY, VM, ANY, VM, ANY, VM, ANY, VM, VM, VM, ANY, VM, ANY, VM],
        scratch_shapes=[
            vm((2, shard, depth), BF16), vm(fa.shape, fa.dtype), vm(fb.shape, fb.dtype), vm((ff + depth, depth), F32),
            vm((used, depth), F32), vm((used, depth), F32), vm((HD, depth), F32), vm((HD, depth), F32), vm((depth, 8), F32),
            pltpu.SemaphoreType.DMA((24,)),
        ],
        compiler_params=pltpu.CompilerParams(vmem_limit_bytes=67043328),
        name="final",
    )(block_out, input_grad, fa, fb, *gains)


def per_device(
    ways,
    tokens, doc_lengths, attn_gain, attn_shift, query_weight, query_bias, key_weight, key_bias, value_weight, value_bias,
    out_weight, out_bias, mlp_gain, mlp_shift, up_weight, up_bias, down_weight, down_bias, out_grad,
):
    heads = query_weight.shape[1] // HD
    small = (
        attn_gain, attn_shift, query_weight.T, query_bias, key_weight.T, key_bias, value_weight.T, value_bias,
        out_weight, out_bias, down_bias, mlp_gain, mlp_shift,
    )
    block_out, input_grad, fa, fb = run_layer(
        heads, doc_lengths, tokens, out_grad, small, up_weight, up_bias, down_weight
    )
    if ways > RING:
        groups = [[i + RING * o for o in range(ways // RING)] for i in range(RING)]
        fa, fb = lax.psum((fa.astype(F32), fb.astype(F32)), "dp", axis_index_groups=groups)
    (
        block_out, input_grad, attn_gain_grad, attn_shift_grad, qw, qb, kw, kb, vw, vb, ow, ob, mlp_gain_grad, mlp_shift_grad,
        uw, ub, dw, db,
    ) = run_final(
        heads, up_weight.shape[1], block_out, input_grad, fa, fb, (attn_gain, attn_shift, mlp_gain, mlp_shift)
    )
    return (
        block_out, input_grad, attn_gain_grad, attn_shift_grad, qw.T, qb, kw.T, kb, vw.T, vb, ow, ob, mlp_gain_grad,
        mlp_shift_grad, uw, ub, dw, db,
    )


def solution(mesh):
    rows = P(("dp", "mp"), None)
    placed = (
        rows, P("dp", None), P(), P(), P(None, "mp"), P("mp"), P(), P(), P(), P(), P("mp", None), P(), P(), P(),
        P(None, "mp"), P("mp"), P("mp", None), P(), rows,
    )
    outs = (
        rows, rows, P(), P(), P(None, "mp"), P("mp"), P(), P(), P(), P(), P("mp", None), P(), P(), P(),
        P(None, "mp"), P("mp"), P("mp", None), P(),
    )
    return jax.shard_map(partial(per_device, mesh.shape["dp"]), mesh=mesh, in_specs=placed, out_specs=outs, check_vma=False)
```

```python
from functools import partial

import jax
import jax.numpy as jnp
from jax import lax
from jax.experimental import pallas as pl
from jax.experimental.pallas import tpu as pltpu
from jax.sharding import PartitionSpec as P

HD = 64
ROT = 16
HALF = ROT // 2
SLOT = 2048
VALID = 1792
LONGEST = 1024
DOCS = 4
BIG = 1e30
RATE = 11
EPS = 1e-05
BLK = 256
NBLK = SLOT // BLK
BAND = LONGEST // BLK
PADBLK = VALID // BLK
LANES = 128
MP = 4
SHARD = SLOT // MP
RING = 8
EVENTS = RING + 1
F32 = jnp.float32
BF16 = jnp.bfloat16
MESH = pl.DeviceIdType.MESH


def dot(a, b):
    return lax.dot_general(a, b, (((1,), (0,)), ((), ())), preferred_element_type=F32)


def dot_t(a, b):
    return lax.dot_general(a, b, (((1,), (1,)), ((), ())), preferred_element_type=F32)


def t_dot(a, b):
    return lax.dot_general(a, b, (((0,), (0,)), ((), ())), preferred_element_type=F32)


def key_blocks(i):
    if i >= PADBLK:
        return list(range(PADBLK, i + 1))
    return list(range(max(0, i - BAND), i + 1))


SLOTS = {}
for _i in range(PADBLK):
    for _j in key_blocks(_i):
        SLOTS[(_i, _j)] = len(SLOTS)
NSLOT = len(SLOTS)
KV_ROW, Q_ROW = 256, 384


def doc_begin(slot, ends):
    begin = jnp.zeros_like(slot)
    for end in ends:
        begin = jnp.where(slot >= end, end, begin)
    return begin


def doc_ends(doc_ref):
    ends = []
    total = 0
    for d in range(DOCS):
        total = total + doc_ref[0, d]
        ends.append(total)
    return ends


def build_tables(doc_ref, cos_ref, sine_ref):
    ends = doc_ends(doc_ref)
    slot = lax.broadcasted_iota(jnp.int32, (HALF, SLOT), 1)
    freq_index = lax.broadcasted_iota(jnp.int32, (HALF, SLOT), 0)
    position = (slot - doc_begin(slot, ends)).astype(F32)
    freq = jnp.zeros((HALF, SLOT), F32)
    for i in range(HALF):
        freq = jnp.where(freq_index == i, 10000.0 ** (-(2.0 * i) / ROT), freq)
    angle = position * freq
    lane = lax.broadcasted_iota(jnp.int32, (3 * HALF, LANES), 1) % HD
    row = lax.broadcasted_iota(jnp.int32, (3 * HALF, LANES), 0) % HALF
    low = jnp.where(lane == row, 1.0, 0.0)
    high = jnp.where(lane == row + HALF, 1.0, 0.0)
    rest = lax.broadcasted_iota(jnp.int32, (SLOT, LANES), 1) % HD >= ROT

    def parts(v):
        a = v.astype(BF16)
        r = v - a.astype(F32)
        b = r.astype(BF16)
        c = (r - b.astype(F32)).astype(BF16)
        return jnp.concatenate([a, b, c], axis=0)

    cos_ref[...] = jnp.where(rest, 1.0, t_dot(parts(jnp.cos(angle)), (low + high).astype(BF16)))
    sine_ref[...] = t_dot(parts(jnp.sin(angle)), (high - low).astype(BF16))


def partner(v):
    lane = lax.broadcasted_iota(jnp.int32, v.shape, 1) % HD
    return jnp.where(lane < HALF, pltpu.roll(v, LANES - HALF, 1), pltpu.roll(v, HALF, 1))


def rope(v, cos, sine):
    return v * cos + partner(v) * sine


def unrope(v, cos, sine):
    return v * cos - partner(v) * sine


def top_and_rest(v):
    top = v.astype(BF16)
    return top, (v - top.astype(F32)).astype(BF16)


def rows_of(first, count):
    return pl.ds(pl.multiple_of(first, count), count)


class Rings:
    CHAINS = ((0, 4, 0), (1, 3, 0), (0, 3, 1), (1, 4, 1))

    def __init__(self, source, stage, slots, final, recv, send, place, right, left):
        self.source, self.stage, self.slots, self.final = source, stage, slots, final
        self.recv, self.send, self.place = recv, send, place
        self.to = (right, left)
        self.rows, self.lanes = stage.shape[2], stage.shape[3]

    def copy(self, r, chain, src, dst, step):
        return pltpu.make_async_remote_copy(
            src_ref=src, dst_ref=dst, send_sem=self.send.at[r, chain], recv_sem=self.recv.at[r, chain, step],
            device_id={"dp": self.to[self.CHAINS[chain][0]]}, device_id_type=MESH,
        )

    def at(self, r, ahead):
        chunk = lax.rem(self.place + 2 * RING + ahead, RING)
        return rows_of((r * RING + chunk) * self.rows, self.rows)

    def event(self, r, e):
        stage, slots, source, final = self.stage, self.slots, self.source, self.final
        for chain, (left, hops, side) in enumerate(self.CHAINS):
            sign = -1 if left else 1
            lanes = pl.ds(side * self.lanes, self.lanes)
            own = self.at(r, sign * (hops - e))

            @pl.when(e == 0)
            def _():
                stage[r, chain] = source[own, lanes].astype(BF16)
                self.copy(r, chain, stage.at[r, chain], slots.at[r, chain, 0], 0).start()

            @pl.when((e >= 1) & (e < hops))
            def _():
                got = slots.at[r, chain, e - 1]
                self.copy(r, chain, stage.at[r, chain], got, e - 1).wait_recv()
                slots[r, chain, e - 1] = (slots[r, chain, e - 1].astype(F32) + source[own, lanes]).astype(BF16)
                self.copy(r, chain, stage.at[r, chain], got, e - 1).wait_send()
                self.copy(r, chain, got, slots.at[r, chain, e], e).start()

        @pl.when(e == 4)
        def _():
            self.settle(r)
            self.release(r)

        for chain, (left, hops, side) in enumerate(self.CHAINS):
            sign = -1 if left else 1
            here = final.at[self.at(r, sign * (4 - e)), pl.ds(side * self.lanes, self.lanes)]

            @pl.when((e > 4) & (e <= 4 + hops))
            def _():
                self.copy(r, chain, stage.at[r, chain], here, e - 1).wait_recv()
                self.copy(r, chain, here, here, e - 1).wait_send()

            @pl.when((e > 4) & (e < 4 + hops))
            def _():
                self.copy(r, chain, here, here, e).start()

    def settle(self, r):
        for chain, (left, hops, side) in enumerate(self.CHAINS):
            got = self.slots.at[r, chain, hops - 1]
            self.copy(r, chain, self.stage.at[r, chain], got, hops - 1).wait_recv()
            self.copy(r, chain, self.stage.at[r, chain], got, hops - 1).wait_send()
        mine = self.at(r, 0)
        for side in range(2):
            lanes = pl.ds(side * self.lanes, self.lanes)
            pair = [self.slots[r, c, self.CHAINS[c][1] - 1].astype(F32) for c in (2 * side, 2 * side + 1)]
            self.final[mine, lanes] = (self.source[mine, lanes] + pair[0] + pair[1]).astype(BF16)

    def release(self, r):
        for chain, (left, hops, side) in enumerate(self.CHAINS):
            here = self.final.at[self.at(r, 0), pl.ds(side * self.lanes, self.lanes)]
            self.copy(r, chain, here, here, 4).start()


class Scatter:
    def __init__(self, part, mate_in, cross_in, send, recv, m, mate, cross):
        self.part, self.mate_in, self.cross_in, self.send, self.recv = part, mate_in, cross_in, send, recv
        self.m, self.mate, self.cross = m, mate, cross

    def copy(self, src, dst, index, to):
        return pltpu.make_async_remote_copy(
            src_ref=src, dst_ref=dst, send_sem=self.send.at[index], recv_sem=self.recv.at[index],
            device_id={"mp": to}, device_id_type=MESH,
        )

    def to_mate(self, b):
        index = (b // 4) * 2 + b % 2
        return self.copy(self.part.at[pl.ds(b * BLK, BLK), :], self.mate_in.at[index], index, self.mate)

    def to_cross(self, b):
        index = (b // 4) * 2 + b % 2
        return self.copy(self.mate_in.at[index], self.cross_in.at[b % 2], 4 + b % 2, self.cross)

    def mine(self, b):
        return self.m % 2 == (b // 2) % 2

    def offer(self, b):
        @pl.when(jnp.logical_not(self.mine(b)))
        def _():
            self.to_mate(b).start()

    def collect(self, b):
        index = (b // 4) * 2 + b % 2

        @pl.when(self.mine(b))
        def _():
            self.to_mate(b).wait_recv()

            @pl.when(self.m // 2 != b // 4)
            def _():
                def add(r, carry):
                    at = rows_of(r * 32, 32)
                    own = self.part[rows_of(b * BLK + r * 32, 32), :].astype(F32)
                    self.mate_in[index, at, :] = (self.mate_in[index, at, :].astype(F32) + own).astype(BF16)
                    return carry

                lax.fori_loop(0, BLK // 32, add, 0)
                self.to_cross(b).start()

    def total(self, k, at, count=32):
        own = self.part[rows_of((2 * self.m + k) * BLK + at, count), :].astype(F32)
        index = (self.m // 2) * 2 + k
        return own + self.mate_in[index, rows_of(at, count), :].astype(F32) + self.cross_in[k, rows_of(at, count), :].astype(F32)

    def arrived(self, k):
        self.copy(self.mate_in.at[0], self.cross_in.at[k], 4 + k, self.cross).wait_recv()

    def drain(self, b):
        @pl.when(jnp.logical_not(self.mine(b)))
        def _():
            self.to_mate(b).wait_send()

        @pl.when(self.mine(b) & (self.m // 2 != b // 4))
        def _():
            self.to_cross(b).wait_send()


def layer_kernel(
    heads,
    doc_ref, tok_hbm, grad_hbm, ag_in, as_in, wq_ref, bq_in, wk_ref, bk_in, wv_ref, bv_in, wo_ref, ob_in, db_in, mg_in, ms_in,
    wu_hbm, bu_in, wd_hbm,
    bout_hbm, ingrad_hbm, fa_hbm, fb_hbm,
    xs, gm, outp, em, ga, gb, q, qt, kx, vx, dctx, dct, left_in, cos, sine, dqh, dkv, dqkv, wqkv, wo, wu, wd, bqkv, gsum, rows_in, dsum,
    min_,
    st_a, sl_a, dg, st_b, sl_b, f_b,
    mo, co, hid, ce, swap, io,
    loc, ag_send, ag_recv, ra_r, ra_s, rb_r, rb_s, so_s, so_r, se_s, se_r, bf_s, bf_r,
):
    pairs = (heads + 1) // 2
    width = pairs * LANES
    used = heads * HD
    depth = tok_hbm.shape[1]
    ff = wu.shape[1]
    misc = Q_ROW + used
    m = lax.axis_index("mp")
    d = lax.axis_index("dp")
    mate = m + 1 - 2 * (m % 2)
    cross = (m + 2) % MP
    far = (mate + 2) % MP
    inner, outer = d % RING, d // RING
    place = jnp.where(inner % 2 == 0, inner // 2, RING - 1 - inner // 2)

    def seat(p):
        return outer * RING + jnp.where(p < RING // 2, 2 * p, 2 * (RING - 1 - p) + 1)

    right, left = seat((place + 1) % RING), seat((place + RING - 1) % RING)
    rings_a = Rings(ga, st_a, sl_a, dg, ra_r, ra_s, place, right, left)
    rings_b = Rings(gb, st_b, sl_b, f_b, rb_r, rb_s, place, right, left)

    local = [
        pltpu.make_async_copy(tok_hbm, xs.at[rows_of(m * SHARD, SHARD), :], loc.at[0]),
        pltpu.make_async_copy(wu_hbm, wu, loc.at[1]),
        pltpu.make_async_copy(wd_hbm, wd, loc.at[2]),
    ]
    own_tokens = pltpu.make_async_copy(tok_hbm, min_, loc.at[3])
    for c in local:
        c.start()
    local_g = [
        pltpu.make_async_copy(grad_hbm.at[pl.ds(k * BLK, BLK), :], gm.at[rows_of(m * SHARD + k * BLK, BLK), :], loc.at[4 + k])
        for k in range(2)
    ]

    def valid(shard, k):
        return 2 * shard + k < PADBLK

    for k in range(2):
        @pl.when(valid(m, k))
        def _():
            local_g[k].start()
    gm[VALID:, :] = jnp.zeros((SLOT - VALID, depth), BF16)

    barrier = pltpu.get_barrier_semaphore()
    for to in ({"mp": mate}, {"mp": cross}, {"dp": right}, {"dp": left}):
        pl.semaphore_signal(barrier, inc=1, device_id=to, device_id_type=MESH)
    pl.semaphore_wait(barrier, 4)

    def send(src, dst, index, to):
        return pltpu.make_async_remote_copy(
            src_ref=src, dst_ref=dst, send_sem=ag_send.at[index], recv_sem=ag_recv.at[index], device_id={"mp": to}, device_id_type=MESH
        )

    def half(ref, shard, k):
        return ref.at[rows_of(shard * SHARD + k * BLK, BLK), :]

    def x_cross(shard, k):
        return send(tok_hbm.at[pl.ds(k * BLK, BLK), :], half(xs, shard, k), k, cross)

    def x_mate(shard, k):
        return send(tok_hbm.at[pl.ds(k * BLK, BLK), :], half(xs, shard, k), 2 + k, mate)

    def g_cross(shard, k):
        return send(grad_hbm.at[pl.ds(k * BLK, BLK), :], half(gm, shard, k), 4 + k, cross)

    def g_mate(shard, k):
        return send(grad_hbm.at[pl.ds(k * BLK, BLK), :], half(gm, shard, k), 6 + k, mate)

    def x_pass(shard, k):
        return send(half(xs, shard, k), half(xs, shard, k), 8 + k, mate)

    def g_pass(shard, k):
        return send(half(gm, shard, k), half(gm, shard, k), 10 + k, mate)

    for k in range(2):
        x_cross(m, k).start()
    for k in range(2):
        x_mate(m, k).start()
    for k in range(2):
        @pl.when(valid(m, k))
        def _():
            g_mate(m, k).start()
    build_tables(doc_ref, cos, sine)
    for n, ref in enumerate((ag_in, as_in, mg_in, ms_in, bu_in)):
        rows_in[n : n + 1, :] = ref[...].reshape(1, depth)
    ag_row, as_row, mg_row, ms_row, bu_row = (rows_in.at[n : n + 1, :] for n in range(5))
    rows_in[5:6, :] = ob_in[...].reshape(1, depth) + db_in[...].reshape(1, depth)
    wqkv[:used, :] = wq_ref[...]
    bqkv[:, :used] = bq_in[...].reshape(1, used)
    wo[:used, :] = wo_ref[...]
    if used < width:
        wqkv[used:width, :] = jnp.zeros((width - used, depth), BF16)
        bqkv[:, used:width] = jnp.zeros((1, width - used), F32)
        wo[used:, :] = jnp.zeros((width - used, depth), BF16)
    wqkv[width : width + HD, :] = wk_ref[...]
    wqkv[width + HD :, :] = wv_ref[...]
    bqkv[:, width : width + HD] = bk_in[...].reshape(1, HD)
    bqkv[:, width + HD :] = bv_in[...].reshape(1, HD)
    ga[...] = jnp.zeros_like(ga)
    gb[...] = jnp.zeros_like(gb)
    gsum[...] = jnp.zeros_like(gsum)
    dsum[...] = jnp.zeros_like(dsum)
    dqkv[VALID:, :] = jnp.zeros((SLOT - VALID, width + LANES), BF16)
    fwd_steps = NBLK * heads
    bwd_steps = PADBLK * heads
    steps = fwd_steps + bwd_steps
    lead = 3
    chip = m // 2
    hooks_in_loop = lead + steps - NBLK // 2 * heads
    spare = max(0, -(-4 * EVENTS * 16 // RATE) - hooks_in_loop)
    down_at, up_at = pl.ds(0, ff), pl.ds(ff, depth)

    def times(vector, weight, product):
        acc = jnp.zeros((8, depth), F32)
        for part in top_and_rest(jnp.broadcast_to(vector, (8, vector.shape[1]))):
            acc = acc + product(part, weight[...])
        return acc[:1]

    def early_rings(t):
        def one(n, carry):
            rings_a.event(lax.rem(n, 4), lax.div(n, 4))
            return carry

        def due(t):
            return jnp.minimum(lax.div(jnp.maximum(t, 0) * RATE, 16), 4 * EVENTS)

        lax.fori_loop(due(t), due(t + 1), one, 0)

    scat_o = Scatter(outp, mo, co, so_s, so_r, m, mate, cross)
    scat_e = Scatter(em, hid, ce, se_s, se_r, m, mate, cross)
    ends = doc_ends(doc_ref)
    lane = lax.broadcasted_iota(jnp.int32, (BLK, LANES), 1)
    low = lane < HD

    def body(hp, probs, total):
        half_lanes = depth // 2

        def attn_in():
            return jnp.concatenate([dqkv[:SHARD, :], dqkv[SHARD : 2 * SHARD, :]], axis=1)

        def ff_forward(c):
            first = pl.multiple_of(c * SHARD, SHARD)
            here = pl.ds(first, SHARD)

            def moments(r, carry):
                for part in range(8):
                    at = rows_of(first + r * 128 + part * 16, 16)
                    v = xs[at, :].astype(F32)
                    mean = jnp.mean(v, axis=-1, keepdims=True)
                    v = v - mean
                    inv = lax.rsqrt(jnp.mean(v * v, axis=-1, keepdims=True) + EPS)
                    to = pl.ds(part * 16, 16)
                    dkv[to, rows_of(r * LANES, LANES)] = jnp.broadcast_to(mean, (16, LANES))
                    dkv[to, rows_of((4 + r) * LANES, LANES)] = jnp.broadcast_to(inv, (16, LANES))
                return carry

            lax.fori_loop(0, SHARD // 128, moments, 0)

            def norm(r, carry):
                at = rows_of(first + r * 32, 32)
                to = rows_of(r * 32, 32)
                sub = rows_of(lax.rem(r * 32, LANES), 32)
                mean = jnp.concatenate([dkv[sub, rows_of(r // 4 * LANES, LANES)]] * (depth // LANES), axis=1)
                inv = jnp.concatenate([dkv[sub, rows_of((4 + r // 4) * LANES, LANES)]] * (depth // LANES), axis=1)
                v = (xs[at, :].astype(F32) - mean) * inv
                xs[at, :] = v.astype(BF16)
                a = (v * ag_row[...] + as_row[...]).astype(BF16)
                dqkv[to, :] = a[:, :half_lanes]
                dqkv[rows_of(SHARD + r * 32, 32), :] = a[:, half_lanes:]
                min_[to, :] = (v * mg_row[...] + ms_row[...]).astype(BF16)
                return carry

            lax.fori_loop(0, SHARD // 32, norm, 0)
            ct, st = cos[here, :], sine[here, :]
            ain = attn_in()
            qf = dot_t(ain, wqkv[:width, :]) + bqkv[:, :width]
            slot = first + lax.broadcasted_iota(jnp.int32, (SHARD, LANES), 0)
            lane = lax.broadcasted_iota(jnp.int32, (SHARD, LANES), 1)
            low = lane < HD
            doc = jnp.zeros((SHARD, LANES), jnp.int32)
            for end in doc_ends(doc_ref):
                doc = jnp.where(slot >= end, doc + 1, doc)
            same = lane % HD == doc
            mark = jnp.where(same, -BIG, 0.0)
            for p in range(pairs):
                v = rope(qf[:, p * LANES : (p + 1) * LANES], ct, st) * HD**-0.5
                qt[p * LANES : (p + 1) * LANES, here] = jnp.transpose(v).astype(BF16)
                q[2 * p, here, :] = jnp.where(low, v, mark).astype(BF16)
                if 2 * p + 1 < heads:
                    q[2 * p + 1, here, :] = jnp.where(low, mark, v).astype(BF16)
            kvf = dot_t(ain, wqkv[width:, :]) + bqkv[:, width:]
            keys = rope(kvf, ct, st)
            other = jnp.where(same | (lane % HD > DOCS), 0.0, 1.0)
            kx[0, here, :] = jnp.where(low, keys, other).astype(BF16)
            kx[1, here, :] = jnp.where(low, other, pltpu.roll(keys, HD, 1)).astype(BF16)
            vx[0, here, :] = jnp.where(low, pltpu.roll(kvf, HD, 1), 1.0).astype(BF16)
            vx[1, here, :] = jnp.where(low, 1.0, kvf).astype(BF16)
            hp[...] = dot(min_[...], wu[...])

            def act(r, carry):
                to = rows_of(r * 32, 32)
                v = hp[to, :] + bu_row[...]
                cdf = 0.5 * (1.0 + lax.erf(v * (0.5**0.5)))
                pdf = jnp.exp(-0.5 * v * v) * (2.0 * jnp.pi) ** -0.5
                hid[c % 2 * 2 + r // (BLK // 32), rows_of(lax.rem(r * 32, BLK), 32), :] = (v * cdf).astype(BF16)
                dg[rows_of(first + r * 32, 32), :] = (cdf + v * pdf).astype(BF16)
                return carry

            lax.fori_loop(0, SHARD // 32, act, 0)
            outp[here, :] = dot(hid[pl.ds(c % 2 * 2, 2)].reshape(SHARD, ff), wd[...]).astype(BF16)

        def ff_backward(c, k):
            first = pl.multiple_of(c * SHARD + k * BLK, BLK)
            hp[:BLK, :] = dot_t(gm[pl.ds(first, BLK), :], wd[...])

            def back(r, carry):
                acc, gacc = carry
                at = rows_of(first + r * 32, 32)
                v = hp[rows_of(r * 32, 32), :] * dg[at, :].astype(F32)
                dg[at, :] = v.astype(BF16)
                gv = gm[at, :].astype(F32)
                acc = acc + (v[:8] + v[8:16]) + (v[16:24] + v[24:])
                return acc, gacc + (gv[:8] + gv[8:16]) + (gv[16:24] + gv[24:])

            acc, gacc = lax.fori_loop(0, BLK // 32, back, (jnp.zeros((8, ff), F32), jnp.zeros((8, depth), F32)))
            gsum[:8, :] += gacc
            gsum[8:, :] += acc

        def weights(chip):
            rows = rows_of(chip * 2 * SHARD, 2 * SHARD)
            ga[down_at, :] += t_dot(hid[...].reshape(2 * SHARD, ff), gm[rows, :])
            ga[up_at, :] += t_dot(xs[rows, :], dg[rows, :])

        def shard_of(which):
            return jnp.where(which == 0, m, jnp.where(which == 1, mate, jnp.where(which == 2, cross, far)))

        def after(shard):
            here = rows_of(shard * SHARD, SHARD)
            em[here, :] = (dot_t(dg[here, :], wu[...]) * mg_row[...]).astype(BF16)
            dc = dot_t(gm[here, :], wo[...]).astype(BF16)
            for p in range(pairs):
                dctx[p, here, :] = dc[:, p * LANES : (p + 1) * LANES]

        def norm_grads():
            up_bias = jnp.sum(gsum[8:, :], axis=0, keepdims=True)
            gb[used : used + 8, :] = jnp.concatenate(
                [jnp.sum(gsum[:8, :], axis=0, keepdims=True), up_bias, jnp.zeros((6, depth), F32)], axis=0
            )
            ones = jnp.ones((8, LANES), BF16)
            for r in range(0, depth, LANES):
                folded = jnp.zeros((LANES, LANES), F32)
                for c in range(0, ff, LANES):
                    folded = folded + wu[r : r + LANES, c : c + LANES].astype(F32) * ga[ff + r : ff + r + LANES, c : c + LANES]
                top, rest = top_and_rest(folded)
                gain = dot_t(ones, top) + dot_t(ones, rest)
                gb[misc + 11 : misc + 12, r : r + LANES] = gain[:1]
            gb[misc + 12 : misc + 13, :] = times(up_bias, wu, dot_t)

        causal = lax.broadcasted_iota(jnp.int32, (BLK, BLK), 1) <= lax.broadcasted_iota(jnp.int32, (BLK, BLK), 0)

        def scores(n):
            return hp.at[pl.ds(n // 3 * BLK, BLK), pl.ds(n % 3 * BLK, BLK)]

        def att_forward(i, h):
            at = pl.ds(i * BLK, BLK)
            blocks = key_blocks(i)
            qb = q[h, at, :]
            half = h % 2
            peak = None
            for n, j in enumerate(blocks):
                s = dot_t(qb, kx[half, pl.ds(j * BLK, BLK), :])
                if i == j:
                    s = jnp.where(causal, s, -BIG)
                scores(n)[...] = s
                peak = s if peak is None else jnp.maximum(peak, s)
            top = jnp.max(peak, axis=-1, keepdims=True)
            acc = jnp.zeros((BLK, LANES), F32)
            for n, j in enumerate(blocks):
                e = jnp.exp(scores(n)[...] - top).astype(BF16)
                if i < PADBLK:
                    probs[h, SLOTS[(i, j)]] = e
                acc = acc + dot(e, vx[half, pl.ds(j * BLK, BLK), :])
            total[h] = acc

            @pl.when(h == heads - 1)
            def _():
                context = []
                for p in range(pairs):
                    full = 2 * p + 1 < heads
                    first, second = total[2 * p], total[2 * p + 1] if full else None
                    norm = jnp.where(low, pltpu.roll(first, HD, 1), pltpu.roll(second, HD, 1) if full else 1.0)
                    norm = 1.0 / norm
                    c = jnp.where(low, first, second if full else 0.0) * norm
                    context.append(c.astype(BF16))
                    if i < PADBLK:
                        scaled = dctx[p, at, :].astype(F32) * norm
                        dcs = scaled.astype(BF16).astype(F32)
                        dct[p * LANES : (p + 1) * LANES, at] = jnp.transpose(dcs).astype(BF16)
                        prod = dcs * c
                        for side in range(2 if full else 1):
                            inside = low if side == 0 else ~low
                            r = -jnp.sum(jnp.where(inside, prod, 0.0), axis=-1, keepdims=True)
                            r_top = r.astype(BF16).astype(F32)
                            extra = jnp.where(lane % HD == 0, r_top, jnp.where(lane % HD == 1, r - r_top, 0.0))
                            left_in[2 * p + side, at, :] = jnp.where(inside, dcs, extra).astype(BF16)
                for p in range(pairs):
                    dctx[p, at, :] = context[p]
                outp[at, :] = (dot(jnp.concatenate(context, axis=1), wo[...]) + outp[at, :].astype(F32)).astype(BF16)
                scat_o.offer(i)
                before = (i - 1) % NBLK
                if i % (NBLK // 2) > 0:
                    scat_o.collect(before)
                else:
                    @pl.when(chip != i // (NBLK // 2))
                    def _():
                        scat_o.collect(before)

        def att_backward(i, h):
            at = pl.ds(i * BLK, BLK)
            half = h % 2
            lhs = left_in[h, at, :]
            mine = rows_of(h * HD, HD)
            q_turned, d_turned = qt[mine, at], dct[mine, at]
            acc = jnp.zeros((BLK, LANES), F32)
            for j in key_blocks(i):
                jat = pl.ds(j * BLK, BLK)
                e = probs[h, SLOTS[(i, j)]]
                ds = (e.astype(F32) * dot_t(lhs, vx[half, jat, :])).astype(BF16)
                acc = acc + dot(ds, kx[half, jat, :])
                dkv[:HD, jat] += dot(q_turned, ds)
                dkv[HD:, jat] += dot(d_turned, e)
            dqh[h] = acc

            @pl.when(h == heads - 1)
            def _():
                ct, st = cos[at, :], sine[at, :]
                for p in range(pairs):
                    full = 2 * p + 1 < heads
                    v = jnp.where(low, dqh[2 * p], dqh[2 * p + 1] if full else 0.0)
                    dqkv[at, p * LANES : (p + 1) * LANES] = (unrope(v, ct, st) * HD**-0.5).astype(BF16)
                v = jnp.transpose(dkv[:, at])
                dqkv[at, width:] = jnp.where(low, unrope(v, ct, st), v).astype(BF16)
                dsum[:1, :] += jnp.sum(dqkv[at, :].astype(F32), axis=0, keepdims=True)
                em[at, :] = (dot(dqkv[at, :], wqkv[...]) * ag_row[...] + em[at, :].astype(F32)).astype(BF16)
                scat_e.offer(i)
                if i < PADBLK - 1:
                    scat_e.collect(i + 1)

        def out_rings(blocks):
            @pl.when(lax.rem(blocks, 2) == 0)
            def _():
                def one(r, carry):
                    rings_b.event(r, lax.div(blocks, 2))
                    return carry

                lax.fori_loop(0, 2, one, 0)

        plan = [(0, 0, 0), (1, 0, 0), (1, 0, 1), (0, 1, 0), (1, 1, 0), (1, 1, 1), (2, 0, 0), (3, 0, 0), (3, 1, 0), (0, 2, 0), (0, 3, 0)]
        plan += [(1, 2, 0), (1, 2, 1), (1, 3, 0), (1, 3, 1), (2, 2, 0), (3, 2, 0), (3, 3, 0), (4, 0, 0)]
        before = 11
        early = NBLK // 2 * heads
        after_all = len(plan) + early
        hooked = 16 + early

        def pick(p):
            code = jnp.int32(0)
            for n, (what, whose, part) in enumerate(plan):
                code = jnp.where(p == n, what + 8 * whose + 32 * part, code)
            return lax.rem(code, 8), lax.rem(lax.div(code, 8), 4), lax.div(code, 32)

        def at_step(n):
            return lambda action: pl.when(step_now[0] == n)(action)

        step_now = [None]

        def step(s, carry):
            block, h = carry
            planned = (s < before) | ((s >= before + early) & (s < after_all))
            p = jnp.where(s < before, s, s - early)
            step_now[0] = jnp.where(planned, p, -1)
            early_rings(s - hooked)

            @at_step(0)
            def _():
                for c in local:
                    c.wait()

            @at_step(1)
            def _():
                for k in range(2):
                    @pl.when(valid(m, k))
                    def _():
                        local_g[k].wait()

            @at_step(3)
            def _():
                for k in range(2):
                    x_mate(mate, k).wait_recv()

            @at_step(4)
            def _():
                for k in range(2):
                    @pl.when(valid(mate, k))
                    def _():
                        g_mate(mate, k).wait_recv()

            @at_step(7)
            def _():
                for k in range(2):
                    x_cross(m, k).wait_send()

                    @pl.when(valid(m, k))
                    def _():
                        g_cross(m, k).start()

                for k in range(2):
                    x_cross(cross, k).wait_recv()
                    x_pass(cross, k).start()

            @at_step(9)
            def _():
                for k in range(2):
                    x_pass(cross, k).wait_send()

            @at_step(10)
            def _():
                for k in range(2):
                    x_pass(far, k).wait_recv()

            for k in range(2):
                @at_step(11 + k)
                def _():
                    @pl.when(valid(cross, k))
                    def _():
                        g_cross(cross, k).wait_recv()
                        g_pass(cross, k).start()

                @at_step(13 + k)
                def _():
                    @pl.when(valid(far, k))
                    def _():
                        g_pass(far, k).wait_recv()

            @pl.when(jnp.logical_not(planned) & (block == NBLK) & (h == 0))
            def _():
                own_tokens.start()
                dkv[...] = jnp.zeros_like(dkv)
                for b in (NBLK // 2 - 1, NBLK - 1):
                    @pl.when(chip != b // (NBLK // 2))
                    def _():
                        scat_o.collect(b)
                for p in range(pairs):
                    some = min(used - p * LANES, LANES)
                    gb[p * LANES : p * LANES + some, :] = t_dot(dctx[p], gm[...])[:some, :]

            @pl.when(jnp.logical_not(planned) & (block >= NBLK) & (h == 0))
            def _():
                out_rings(block - NBLK)

            what, whose, half = pick(p)
            shard = shard_of(whose)
            forward_block = lax.rem(block + chip * (NBLK // 2), NBLK)
            backward_block = jnp.maximum(block - NBLK, 0)
            kind = jnp.where(planned, what, jnp.where(block < NBLK, 5, 6))
            lax.switch(
                kind,
                [
                    lambda: ff_forward(shard), lambda: ff_backward(shard, half), lambda: weights(lax.div(shard, 2)), lambda: after(shard),
                    norm_grads,
                    lambda: lax.switch(forward_block, [partial(att_forward, i) for i in range(NBLK)], h),
                    lambda: lax.switch(backward_block, [partial(att_backward, i) for i in reversed(range(PADBLK))], h),
                ],
            )
            last = h == heads - 1
            following = jnp.where(last, block + 1, block), jnp.where(last, 0, h + 1)
            return jnp.where(planned, block, following[0]), jnp.where(planned, h, following[1])

        lax.fori_loop(0, after_all + steps - early, step, (jnp.int32(0), jnp.int32(0)))

    pl.run_scoped(
        body, pltpu.VMEM((SHARD, ff), F32), pltpu.VMEM((heads, NSLOT, BLK, BLK), BF16), pltpu.VMEM((heads, BLK, LANES), F32),
    )
    for k in range(2):
        x_mate(m, k).wait_send()

        @pl.when(valid(m, k))
        def _():
            g_cross(m, k).wait_send()
            g_mate(m, k).wait_send()

        @pl.when(valid(cross, k))
        def _():
            g_pass(cross, k).wait_send()

    scat_e.collect(0)
    rows = VALID
    gb[KV_ROW : KV_ROW + LANES, :] = t_dot(dqkv[:rows, width:], xs[:rows, :])
    rings_b.event(2, 0)
    gb[Q_ROW:misc, :] = t_dot(dqkv[:rows, :width], xs[:rows, :])[:used, :]
    rings_b.event(3, 0)
    sums = dsum[:1, :]
    gb[misc : misc + 1, : width + LANES] = sums
    gb[misc + 8 : misc + 9, :LANES] = sums[:, width:]
    gain = jnp.sum(wqkv[:used, :].astype(F32) * gb[Q_ROW:misc, :], axis=0, keepdims=True)
    gb[misc + 9 : misc + 10, :] = gain + jnp.sum(
        wqkv[width:, :].astype(F32) * gb[KV_ROW : KV_ROW + LANES, :], axis=0, keepdims=True
    )
    gb[misc + 10 : misc + 11, :] = times(sums, wqkv, dot)
    rings_b.event(4, 0)

    def exchange(stage, to):
        return pltpu.make_async_remote_copy(
            src_ref=swap.at[2 * stage], dst_ref=swap.at[2 * stage + 1], send_sem=bf_s.at[stage], recv_sem=bf_r.at[stage],
            device_id={"mp": to}, device_id_type=MESH,
        )

    def finish_out(r, carry):
        at = pl.multiple_of(r * 32, 32)
        v = min_[rows_of(at, 32), :].astype(F32) + scat_o.total(r // (BLK // 32), lax.rem(at, BLK)) + rows_in[5:6, :]
        outp[rows_of(m * SHARD + at, 32), :] = v.astype(BF16)
        return carry

    def finish_in(r, carry):
        for part in range(4):
            at = pl.multiple_of(r * 64 + part * 16, 16)
            rows = rows_of(at, 16)
            v = min_[rows, :].astype(F32)
            v = v - jnp.mean(v, axis=-1, keepdims=True)
            inv = lax.rsqrt(jnp.mean(v * v, axis=-1, keepdims=True) + EPS)
            v = v * inv
            e = scat_e.total(r // (BLK // 64), lax.rem(at, BLK), 16)
            e = inv * (e - jnp.mean(e, axis=-1, keepdims=True) - v * jnp.mean(e * v, axis=-1, keepdims=True))
            g = gm[rows_of(m * SHARD + at, 16), :].astype(F32)
            io[part] = (e + g).astype(BF16)
        for part in range(4):
            min_[rows_of(r * 64 + part * 16, 16), :] = io[part]
        return carry

    out_block = pltpu.make_async_copy(outp.at[rows_of(m * SHARD, SHARD), :], bout_hbm, loc.at[1])
    out_in = pltpu.make_async_copy(min_, ingrad_hbm, loc.at[2])

    done = (PADBLK - 1) // 2

    def tail(e, carry):
        def late(n, carry):
            early_rings(hooks_in_loop + n)
            return carry

        def one(r, carry):
            step = jnp.where(r < 2, e + done, e)

            @pl.when(jnp.where(r < 2, step < EVENTS, (e != 4) | (r == 3)))
            def _():
                rings_b.event(r, step)

            return carry

        @pl.when(e == 4)
        def _():
            rings_b.settle(2)
            rings_b.settle(4)
            swap[0, :16, :] = f_b[rings_b.at(2, 0), :]
            swap[0, 16:, :] = f_b[rings_b.at(4, 0), :]
            exchange(0, mate).start()

        lax.fori_loop(0, 5, one, 0)

        @pl.when(e == 4)
        def _():
            exchange(0, mate).wait()
            swap[2] = (swap[0].astype(F32) + swap[1].astype(F32)).astype(BF16)
            exchange(1, cross).start()

        lax.fori_loop(lax.div((e - 1) * spare, EVENTS - 1), lax.div(e * spare, EVENTS - 1), late, 0)

        @pl.when(e == 4)
        def _():
            exchange(1, cross).wait()
            both = swap[2].astype(F32) + swap[3].astype(F32)
            f_b[rings_b.at(2, 0), :] = both[:16].astype(BF16)
            last = lax.broadcasted_iota(jnp.int32, (16, depth), 0) >= jnp.where(place == used // 16 % RING, 8, 16)
            f_b[rings_b.at(4, 0), :] = jnp.where(last, both[16:], swap[0, 16:, :].astype(F32)).astype(BF16)
            rings_b.release(2)
            rings_b.release(4)

        @pl.when(e == 1)
        def _():
            own_tokens.wait()
            for k in range(2):
                scat_o.arrived(k)

        @pl.when(e <= 4)
        def _():
            lax.fori_loop((e - 1) * (SHARD // 128), e * (SHARD // 128), finish_out, 0)

        @pl.when(e == 4)
        def _():
            out_block.start()

        @pl.when(e == 5)
        def _():
            for k in range(2):
                @pl.when(valid(m, k))
                def _():
                    scat_e.arrived(k)

            @pl.when(jnp.logical_not(valid(m, 1)))
            def _():
                min_[BLK:, :] = jnp.zeros((BLK, depth), BF16)

        @pl.when((e >= 5) & (e < 8))
        def _():
            limit = jnp.where(valid(m, 1), SHARD, BLK) // 64
            lax.fori_loop((e - 5) * limit // 3, (e - 4) * limit // 3, finish_in, 0)

        @pl.when(e == 7)
        def _():
            out_in.start()

        return carry

    lax.fori_loop(1, EVENTS, tail, 0)
    out_a = pltpu.make_async_copy(dg.at[: ff + depth, :], fa_hbm, loc.at[0])
    out_a.start()
    out_b = pltpu.make_async_copy(f_b, fb_hbm, loc.at[3])
    out_b.start()
    for b in range(NBLK):
        scat_o.drain(b)
        if b < PADBLK:
            scat_e.drain(b)
    for c in (out_a, out_b, out_block, out_in):
        c.wait()


VM = pl.BlockSpec(memory_space=pltpu.VMEM)
SM = pl.BlockSpec(memory_space=pltpu.SMEM)
ANY = pl.BlockSpec(memory_space=pl.ANY)


def run_layer(heads, doc, tokens, grads, small, wu, bu, wd):
    depth = tokens.shape[1]
    ff = wu.shape[1]
    pairs = (heads + 1) // 2
    width = pairs * LANES
    wide = width + LANES
    sh = jax.ShapeDtypeStruct
    vm = pltpu.VMEM
    dma = pltpu.SemaphoreType.DMA
    a_rows, b_rows = ff + depth, KV_ROW + 384

    def ring_refs(rows, count):
        chunk = rows // (count * RING)
        return [vm((count, 4, chunk, depth // 2), BF16), vm((count, 4, 4, chunk, depth // 2), BF16), vm((rows, depth), BF16)]

    scratch = [
        vm((SLOT, depth), BF16), vm((SLOT, depth), BF16), vm((SLOT, depth), BF16), vm((SLOT, depth), BF16),
        vm((a_rows, depth), F32), vm((b_rows, depth), F32),
        vm((heads, SLOT, LANES), BF16), vm((width, SLOT), BF16), vm((2, SLOT, LANES), BF16), vm((2, SLOT, LANES), BF16),
        vm((pairs, SLOT, LANES), BF16), vm((width, VALID), BF16), vm((heads, VALID, LANES), BF16),
        vm((SLOT, LANES), F32), vm((SLOT, LANES), F32), vm((heads, BLK, LANES), F32),
        vm((LANES, VALID), F32), vm((SLOT, wide), BF16), vm((wide, depth), BF16), vm((width, depth), BF16),
        vm((depth, ff), BF16), vm((ff, depth), BF16), vm((1, wide), F32), vm((16, depth), F32), vm((8, depth), F32), vm((8, wide), F32),
        vm((SHARD, depth), BF16),
        *ring_refs(a_rows, 4)[:2], vm((SLOT, ff), BF16), *ring_refs(b_rows, 5),
        vm((4, BLK, depth), BF16), vm((2, BLK, depth), BF16), vm((4, BLK, depth), BF16), vm((2, BLK, depth), BF16),
        vm((4, 32, depth), BF16), vm((4, 16, depth), BF16),
        dma((8,)), dma((12,)), dma((12,)), dma((4, 4, 8)), dma((4, 4)), dma((5, 4, 8)), dma((5, 4)),
        dma((6,)), dma((6,)), dma((6,)), dma((6,)), dma((2,)), dma((2,)),
    ]
    return pl.pallas_call(
        partial(layer_kernel, heads),
        out_shape=(
            sh((SHARD, depth), BF16), sh((SHARD, depth), BF16), sh((a_rows, depth), BF16), sh((b_rows, depth), BF16),
        ),
        in_specs=[SM, ANY, ANY] + [VM] * 13 + [ANY, VM, ANY],
        out_specs=[ANY] * 4,
        scratch_shapes=scratch,
        compiler_params=pltpu.CompilerParams(vmem_limit_bytes=67043328, collective_id=0, has_side_effects=True),
        name="layer",
    )(doc, tokens, grads, *small, wu, bu, wd)


def final_kernel(
    heads, ff,
    bout_hbm, ingrad_hbm, fa_hbm, fb_hbm, ag_in, as_in, mg_in, ms_in,
    bout_out, ingrad_out, attn_gain, attn_shift, qw_out, qb_out, kw_out, kb_out, vw_out, vb_out, ow_out, ob_out,
    mlp_gain, mlp_shift, uw_out, ub_out, dw_out, db_out,
    blocks, fa, fb, wide, out, qw, kw, vw, turned, sem,
):
    depth = fa.shape[1]
    used = heads * HD
    pairs = (heads + 1) // 2
    width = pairs * LANES
    misc = Q_ROW + used
    stores = []

    def load(src, dst, n):
        copy = pltpu.make_async_copy(src, dst, sem.at[n])
        copy.start()
        return copy

    def store(src, dst):
        copy = pltpu.make_async_copy(src, dst, sem.at[12 + len(stores)])
        copy.start()
        stores.append(copy)

    piece = 384
    parts = (ff + depth) // piece
    small = load(fb_hbm, fb, 0)
    loads = [load(fa_hbm.at[pl.ds(n * piece, piece), :], fa.at[pl.ds(n * piece, piece), :], 1 + n) for n in range(parts)]
    passed = [load(ref, blocks.at[n], 8 + n) for n, ref in enumerate((bout_hbm, ingrad_hbm))]
    row = lambda ref: ref[...].reshape(1, depth)
    ag, as_, mg, ms = row(ag_in), row(as_in), row(mg_in), row(ms_in)
    turned[...] = jnp.transpose(jnp.concatenate([mg, ms, jnp.zeros((6, depth), F32)], axis=0))
    small.wait()
    extra = fb[used : used + 16, :].astype(F32)
    g_sum, up_bias = extra[:1], extra[1:2]
    for n in range(parts):
        loads[n].wait()
        at = n * piece
        if at < ff:
            wide[pl.ds(at, piece), :] = fa[pl.ds(at, piece), :].astype(F32)
            store(wide.at[pl.ds(at, piece), :], dw_out.at[pl.ds(at, piece), :])
        else:
            to = at - ff
            wide[pl.ds(at, piece), :] = (
                fa[pl.ds(at, piece), :].astype(F32) * turned[to : to + piece, 0:1] + turned[to : to + piece, 1:2] * up_bias
            )
            store(wide.at[pl.ds(at, piece), :], uw_out.at[pl.ds(to, piece), :])
    for n, dst in enumerate((bout_out, ingrad_out)):
        passed[n].wait()
        store(blocks.at[n], dst)
    out[...] = fb[:used, :].astype(F32)
    store(out, ow_out)
    last = fb[misc : misc + 16, :].astype(F32)
    kv_bias = last[8:9, :LANES]
    biases = last[:1, :width]

    def outer(vector, other):
        a, b = top_and_rest(vector)
        c, e = top_and_rest(other)
        return t_dot(jnp.concatenate([a, a, b, b], axis=0), jnp.concatenate([c, e, c, e], axis=0))

    qw[...] = fb[Q_ROW:misc, :].astype(F32) * ag + outer(biases[:, :used], as_)
    store(qw, qw_out)
    kv = fb[KV_ROW : KV_ROW + LANES, :].astype(F32) * ag + outer(kv_bias, as_)
    kw[...] = kv[:HD]
    vw[...] = kv[HD:]
    store(kw, kw_out)
    store(vw, vw_out)
    for n, ref in enumerate((attn_gain, attn_shift, mlp_gain, mlp_shift)):
        ref[...] = last[9 + n : 10 + n].reshape(depth)
    kb_out[...] = kv_bias[:, :HD].reshape(HD)
    vb_out[...] = kv_bias[:, HD:].reshape(HD)
    qb_out[...] = biases[:, :used].reshape(used)
    ob_out[...] = g_sum.reshape(depth)
    db_out[...] = g_sum.reshape(depth)
    ub_out[...] = up_bias.reshape(ff)
    for c in stores:
        c.wait()


def run_final(heads, ff, block_out, input_grad, fa, fb, gains):
    shard, depth = block_out.shape
    used = heads * HD
    sh = jax.ShapeDtypeStruct
    vm = pltpu.VMEM
    line = lambda n: sh((n,), F32)
    return pl.pallas_call(
        partial(final_kernel, heads, ff),
        out_shape=(
            sh((shard, depth), BF16), sh((shard, depth), BF16), line(depth), line(depth), sh((used, depth), F32), line(used),
            sh((HD, depth), F32), line(HD), sh((HD, depth), F32), line(HD), sh((used, depth), F32), line(depth),
            line(depth), line(depth), sh((depth, ff), F32), line(ff), sh((ff, depth), F32), line(depth),
        ),
        in_specs=[ANY] * 4 + [VM] * 4,
        out_specs=[ANY, ANY, VM, VM, ANY, VM, ANY, VM, ANY, VM, ANY, VM, VM, VM, ANY, VM, ANY, VM],
        scratch_shapes=[
            vm((2, shard, depth), BF16), vm(fa.shape, fa.dtype), vm(fb.shape, fb.dtype), vm((ff + depth, depth), F32),
            vm((used, depth), F32), vm((used, depth), F32), vm((HD, depth), F32), vm((HD, depth), F32), vm((depth, 8), F32),
            pltpu.SemaphoreType.DMA((24,)),
        ],
        compiler_params=pltpu.CompilerParams(vmem_limit_bytes=67043328),
        name="final",
    )(block_out, input_grad, fa, fb, *gains)


def per_device(
    ways,
    tokens, doc_lengths, attn_gain, attn_shift, query_weight, query_bias, key_weight, key_bias, value_weight, value_bias,
    out_weight, out_bias, mlp_gain, mlp_shift, up_weight, up_bias, down_weight, down_bias, out_grad,
):
    heads = query_weight.shape[1] // HD
    small = (
        attn_gain, attn_shift, query_weight.T, query_bias, key_weight.T, key_bias, value_weight.T, value_bias,
        out_weight, out_bias, down_bias, mlp_gain, mlp_shift,
    )
    block_out, input_grad, fa, fb = run_layer(
        heads, doc_lengths, tokens, out_grad, small, up_weight, up_bias, down_weight
    )
    if ways > RING:
        groups = [[i + RING * o for o in range(ways // RING)] for i in range(RING)]
        fa, fb = lax.psum((fa.astype(F32), fb.astype(F32)), "dp", axis_index_groups=groups)
    (
        block_out, input_grad, attn_gain_grad, attn_shift_grad, qw, qb, kw, kb, vw, vb, ow, ob, mlp_gain_grad, mlp_shift_grad,
        uw, ub, dw, db,
    ) = run_final(
        heads, up_weight.shape[1], block_out, input_grad, fa, fb, (attn_gain, attn_shift, mlp_gain, mlp_shift)
    )
    return (
        block_out, input_grad, attn_gain_grad, attn_shift_grad, qw.T, qb, kw.T, kb, vw.T, vb, ow, ob, mlp_gain_grad,
        mlp_shift_grad, uw, ub, dw, db,
    )


def solution(mesh):
    rows = P(("dp", "mp"), None)
    placed = (
        rows, P("dp", None), P(), P(), P(None, "mp"), P("mp"), P(), P(), P(), P(), P("mp", None), P(), P(), P(),
        P(None, "mp"), P("mp"), P("mp", None), P(), rows,
    )
    outs = (
        rows, rows, P(), P(), P(None, "mp"), P("mp"), P(), P(), P(), P(), P("mp", None), P(), P(), P(),
        P(None, "mp"), P("mp"), P("mp", None), P(),
    )
    return jax.shard_map(partial(per_device, mesh.shape["dp"]), mesh=mesh, in_specs=placed, out_specs=outs, check_vma=False)
```

```python
from functools import partial

import jax
import jax.numpy as jnp
from jax import lax
from jax.experimental import pallas as pl
from jax.experimental.pallas import tpu as pltpu
from jax.sharding import PartitionSpec as P

HD = 64
ROT = 16
HALF = ROT // 2
SLOT = 2048
VALID = 1792
LONGEST = 1024
DOCS = 4
BIG = 1e30
RATE = 12
EPS = 1e-05
BLK = 256
NBLK = SLOT // BLK
BAND = LONGEST // BLK
PADBLK = VALID // BLK
LANES = 128
MP = 4
SHARD = SLOT // MP
RING = 8
EVENTS = RING + 1
F32 = jnp.float32
BF16 = jnp.bfloat16
MESH = pl.DeviceIdType.MESH


def dot(a, b):
    return lax.dot_general(a, b, (((1,), (0,)), ((), ())), preferred_element_type=F32)


def dot_t(a, b):
    return lax.dot_general(a, b, (((1,), (1,)), ((), ())), preferred_element_type=F32)


def t_dot(a, b):
    return lax.dot_general(a, b, (((0,), (0,)), ((), ())), preferred_element_type=F32)


def key_blocks(i):
    if i >= PADBLK:
        return list(range(PADBLK, i + 1))
    return list(range(max(0, i - BAND), i + 1))


SLOTS = {}
for _i in range(PADBLK):
    for _j in key_blocks(_i):
        SLOTS[(_i, _j)] = len(SLOTS)
NSLOT = len(SLOTS)
KV_ROW, Q_ROW = 256, 384


def doc_begin(slot, ends):
    begin = jnp.zeros_like(slot)
    for end in ends:
        begin = jnp.where(slot >= end, end, begin)
    return begin


def doc_ends(doc_ref):
    ends = []
    total = 0
    for d in range(DOCS):
        total = total + doc_ref[0, d]
        ends.append(total)
    return ends


def build_tables(doc_ref, cos_ref, sine_ref):
    ends = doc_ends(doc_ref)
    slot = lax.broadcasted_iota(jnp.int32, (HALF, SLOT), 1)
    freq_index = lax.broadcasted_iota(jnp.int32, (HALF, SLOT), 0)
    position = (slot - doc_begin(slot, ends)).astype(F32)
    freq = jnp.zeros((HALF, SLOT), F32)
    for i in range(HALF):
        freq = jnp.where(freq_index == i, 10000.0 ** (-(2.0 * i) / ROT), freq)
    angle = position * freq
    lane = lax.broadcasted_iota(jnp.int32, (3 * HALF, LANES), 1) % HD
    row = lax.broadcasted_iota(jnp.int32, (3 * HALF, LANES), 0) % HALF
    low = jnp.where(lane == row, 1.0, 0.0)
    high = jnp.where(lane == row + HALF, 1.0, 0.0)
    rest = lax.broadcasted_iota(jnp.int32, (SLOT, LANES), 1) % HD >= ROT

    def parts(v):
        a = v.astype(BF16)
        r = v - a.astype(F32)
        b = r.astype(BF16)
        c = (r - b.astype(F32)).astype(BF16)
        return jnp.concatenate([a, b, c], axis=0)

    cos_ref[...] = jnp.where(rest, 1.0, t_dot(parts(jnp.cos(angle)), (low + high).astype(BF16)))
    sine_ref[...] = t_dot(parts(jnp.sin(angle)), (high - low).astype(BF16))


def partner(v):
    lane = lax.broadcasted_iota(jnp.int32, v.shape, 1) % HD
    return jnp.where(lane < HALF, pltpu.roll(v, LANES - HALF, 1), pltpu.roll(v, HALF, 1))


def rope(v, cos, sine):
    return v * cos + partner(v) * sine


def unrope(v, cos, sine):
    return v * cos - partner(v) * sine


def top_and_rest(v):
    top = v.astype(BF16)
    return top, (v - top.astype(F32)).astype(BF16)


def rows_of(first, count):
    return pl.ds(pl.multiple_of(first, count), count)


class Rings:
    CHAINS = ((0, 4, 0), (1, 3, 0), (0, 3, 1), (1, 4, 1))

    def __init__(self, source, stage, slots, final, recv, send, place, right, left):
        self.source, self.stage, self.slots, self.final = source, stage, slots, final
        self.recv, self.send, self.place = recv, send, place
        self.to = (right, left)
        self.rows, self.lanes = stage.shape[2], stage.shape[3]

    def copy(self, r, chain, src, dst, step):
        return pltpu.make_async_remote_copy(
            src_ref=src, dst_ref=dst, send_sem=self.send.at[r, chain], recv_sem=self.recv.at[r, chain, step],
            device_id={"dp": self.to[self.CHAINS[chain][0]]}, device_id_type=MESH,
        )

    def at(self, r, ahead):
        chunk = lax.rem(self.place + 2 * RING + ahead, RING)
        return rows_of((r * RING + chunk) * self.rows, self.rows)

    def event(self, r, e):
        stage, slots, source, final = self.stage, self.slots, self.source, self.final
        for chain, (left, hops, side) in enumerate(self.CHAINS):
            sign = -1 if left else 1
            lanes = pl.ds(side * self.lanes, self.lanes)
            own = self.at(r, sign * (hops - e))

            @pl.when(e == 0)
            def _():
                stage[r, chain] = source[own, lanes].astype(BF16)
                self.copy(r, chain, stage.at[r, chain], slots.at[r, chain, 0], 0).start()

            @pl.when((e >= 1) & (e < hops))
            def _():
                got = slots.at[r, chain, e - 1]
                self.copy(r, chain, stage.at[r, chain], got, e - 1).wait_recv()
                slots[r, chain, e - 1] = (slots[r, chain, e - 1].astype(F32) + source[own, lanes]).astype(BF16)
                self.copy(r, chain, stage.at[r, chain], got, e - 1).wait_send()
                self.copy(r, chain, got, slots.at[r, chain, e], e).start()

        @pl.when(e == 4)
        def _():
            self.settle(r)
            self.release(r)

        for chain, (left, hops, side) in enumerate(self.CHAINS):
            sign = -1 if left else 1
            here = final.at[self.at(r, sign * (4 - e)), pl.ds(side * self.lanes, self.lanes)]

            @pl.when((e > 4) & (e <= 4 + hops))
            def _():
                self.copy(r, chain, stage.at[r, chain], here, e - 1).wait_recv()
                self.copy(r, chain, here, here, e - 1).wait_send()

            @pl.when((e > 4) & (e < 4 + hops))
            def _():
                self.copy(r, chain, here, here, e).start()

    def settle(self, r):
        for chain, (left, hops, side) in enumerate(self.CHAINS):
            got = self.slots.at[r, chain, hops - 1]
            self.copy(r, chain, self.stage.at[r, chain], got, hops - 1).wait_recv()
            self.copy(r, chain, self.stage.at[r, chain], got, hops - 1).wait_send()
        mine = self.at(r, 0)
        for side in range(2):
            lanes = pl.ds(side * self.lanes, self.lanes)
            pair = [self.slots[r, c, self.CHAINS[c][1] - 1].astype(F32) for c in (2 * side, 2 * side + 1)]
            self.final[mine, lanes] = (self.source[mine, lanes] + pair[0] + pair[1]).astype(BF16)

    def release(self, r):
        for chain, (left, hops, side) in enumerate(self.CHAINS):
            here = self.final.at[self.at(r, 0), pl.ds(side * self.lanes, self.lanes)]
            self.copy(r, chain, here, here, 4).start()


class Scatter:
    def __init__(self, part, mate_in, cross_in, send, recv, m, mate, cross):
        self.part, self.mate_in, self.cross_in, self.send, self.recv = part, mate_in, cross_in, send, recv
        self.m, self.mate, self.cross = m, mate, cross

    def copy(self, src, dst, index, to):
        return pltpu.make_async_remote_copy(
            src_ref=src, dst_ref=dst, send_sem=self.send.at[index], recv_sem=self.recv.at[index],
            device_id={"mp": to}, device_id_type=MESH,
        )

    def to_mate(self, b):
        index = (b // 4) * 2 + b % 2
        return self.copy(self.part.at[pl.ds(b * BLK, BLK), :], self.mate_in.at[index], index, self.mate)

    def to_cross(self, b):
        index = (b // 4) * 2 + b % 2
        return self.copy(self.mate_in.at[index], self.cross_in.at[b % 2], 4 + b % 2, self.cross)

    def mine(self, b):
        return self.m % 2 == (b // 2) % 2

    def offer(self, b):
        @pl.when(jnp.logical_not(self.mine(b)))
        def _():
            self.to_mate(b).start()

    def collect(self, b):
        index = (b // 4) * 2 + b % 2

        @pl.when(self.mine(b))
        def _():
            self.to_mate(b).wait_recv()

            @pl.when(self.m // 2 != b // 4)
            def _():
                def add(r, carry):
                    at = rows_of(r * 32, 32)
                    own = self.part[rows_of(b * BLK + r * 32, 32), :].astype(F32)
                    self.mate_in[index, at, :] = (self.mate_in[index, at, :].astype(F32) + own).astype(BF16)
                    return carry

                lax.fori_loop(0, BLK // 32, add, 0)
                self.to_cross(b).start()

    def total(self, k, at, count=32):
        own = self.part[rows_of((2 * self.m + k) * BLK + at, count), :].astype(F32)
        index = (self.m // 2) * 2 + k
        return own + self.mate_in[index, rows_of(at, count), :].astype(F32) + self.cross_in[k, rows_of(at, count), :].astype(F32)

    def arrived(self, k):
        self.copy(self.mate_in.at[0], self.cross_in.at[k], 4 + k, self.cross).wait_recv()

    def drain(self, b):
        @pl.when(jnp.logical_not(self.mine(b)))
        def _():
            self.to_mate(b).wait_send()

        @pl.when(self.mine(b) & (self.m // 2 != b // 4))
        def _():
            self.to_cross(b).wait_send()


def layer_kernel(
    heads,
    doc_ref, tok_hbm, grad_hbm, ag_in, as_in, wq_ref, bq_in, wk_ref, bk_in, wv_ref, bv_in, wo_ref, ob_in, db_in, mg_in, ms_in,
    wu_hbm, bu_in, wd_hbm,
    bout_hbm, ingrad_hbm, fa_hbm, fb_hbm,
    xs, gm, outp, em, ga, gb, q, qt, kx, vx, dctx, dct, left_in, cos, sine, dqh, dkv, dqkv, wqkv, wo, wu, wd, bqkv, gsum, rows_in, dsum,
    min_,
    st_a, sl_a, dg, st_b, sl_b, f_b,
    mo, co, hid, ce, swap, io,
    loc, ag_send, ag_recv, ra_r, ra_s, rb_r, rb_s, so_s, so_r, se_s, se_r, bf_s, bf_r,
):
    pairs = (heads + 1) // 2
    width = pairs * LANES
    used = heads * HD
    depth = tok_hbm.shape[1]
    ff = wu.shape[1]
    misc = Q_ROW + used
    m = lax.axis_index("mp")
    d = lax.axis_index("dp")
    mate = m + 1 - 2 * (m % 2)
    cross = (m + 2) % MP
    far = (mate + 2) % MP
    inner, outer = d % RING, d // RING
    place = jnp.where(inner % 2 == 0, inner // 2, RING - 1 - inner // 2)

    def seat(p):
        return outer * RING + jnp.where(p < RING // 2, 2 * p, 2 * (RING - 1 - p) + 1)

    right, left = seat((place + 1) % RING), seat((place + RING - 1) % RING)
    rings_a = Rings(ga, st_a, sl_a, dg, ra_r, ra_s, place, right, left)
    rings_b = Rings(gb, st_b, sl_b, f_b, rb_r, rb_s, place, right, left)

    local = [
        pltpu.make_async_copy(tok_hbm, xs.at[rows_of(m * SHARD, SHARD), :], loc.at[0]),
        pltpu.make_async_copy(wu_hbm, wu, loc.at[1]),
        pltpu.make_async_copy(wd_hbm, wd, loc.at[2]),
    ]
    own_tokens = pltpu.make_async_copy(tok_hbm, min_, loc.at[3])
    for c in local:
        c.start()
    local_g = [
        pltpu.make_async_copy(grad_hbm.at[pl.ds(k * BLK, BLK), :], gm.at[rows_of(m * SHARD + k * BLK, BLK), :], loc.at[4 + k])
        for k in range(2)
    ]

    def valid(shard, k):
        return 2 * shard + k < PADBLK

    for k in range(2):
        @pl.when(valid(m, k))
        def _():
            local_g[k].start()
    gm[VALID:, :] = jnp.zeros((SLOT - VALID, depth), BF16)

    barrier = pltpu.get_barrier_semaphore()
    for to in ({"mp": mate}, {"mp": cross}, {"dp": right}, {"dp": left}):
        pl.semaphore_signal(barrier, inc=1, device_id=to, device_id_type=MESH)
    pl.semaphore_wait(barrier, 4)

    def send(src, dst, index, to):
        return pltpu.make_async_remote_copy(
            src_ref=src, dst_ref=dst, send_sem=ag_send.at[index], recv_sem=ag_recv.at[index], device_id={"mp": to}, device_id_type=MESH
        )

    def half(ref, shard, k):
        return ref.at[rows_of(shard * SHARD + k * BLK, BLK), :]

    def x_cross(shard, k):
        return send(tok_hbm.at[pl.ds(k * BLK, BLK), :], half(xs, shard, k), k, cross)

    def x_mate(shard, k):
        return send(tok_hbm.at[pl.ds(k * BLK, BLK), :], half(xs, shard, k), 2 + k, mate)

    def g_cross(shard, k):
        return send(grad_hbm.at[pl.ds(k * BLK, BLK), :], half(gm, shard, k), 4 + k, cross)

    def g_mate(shard, k):
        return send(grad_hbm.at[pl.ds(k * BLK, BLK), :], half(gm, shard, k), 6 + k, mate)

    def x_pass(shard, k):
        return send(half(xs, shard, k), half(xs, shard, k), 8 + k, mate)

    def g_pass(shard, k):
        return send(half(gm, shard, k), half(gm, shard, k), 10 + k, mate)

    for k in range(2):
        x_cross(m, k).start()
    for k in range(2):
        x_mate(m, k).start()
    for k in range(2):
        @pl.when(valid(m, k))
        def _():
            g_mate(m, k).start()
    build_tables(doc_ref, cos, sine)
    for n, ref in enumerate((ag_in, as_in, mg_in, ms_in, bu_in)):
        rows_in[n : n + 1, :] = ref[...].reshape(1, depth)
    ag_row, as_row, mg_row, ms_row, bu_row = (rows_in.at[n : n + 1, :] for n in range(5))
    rows_in[5:6, :] = ob_in[...].reshape(1, depth) + db_in[...].reshape(1, depth)
    wqkv[:used, :] = wq_ref[...]
    bqkv[:, :used] = bq_in[...].reshape(1, used)
    wo[:used, :] = wo_ref[...]
    if used < width:
        wqkv[used:width, :] = jnp.zeros((width - used, depth), BF16)
        bqkv[:, used:width] = jnp.zeros((1, width - used), F32)
        wo[used:, :] = jnp.zeros((width - used, depth), BF16)
    wqkv[width : width + HD, :] = wk_ref[...]
    wqkv[width + HD :, :] = wv_ref[...]
    bqkv[:, width : width + HD] = bk_in[...].reshape(1, HD)
    bqkv[:, width + HD :] = bv_in[...].reshape(1, HD)
    ga[...] = jnp.zeros_like(ga)
    gb[...] = jnp.zeros_like(gb)
    gsum[...] = jnp.zeros_like(gsum)
    dsum[...] = jnp.zeros_like(dsum)
    dqkv[VALID:, :] = jnp.zeros((SLOT - VALID, width + LANES), BF16)
    fwd_steps = NBLK * heads
    bwd_steps = PADBLK * heads
    steps = fwd_steps + bwd_steps
    lead = 3
    chip = m // 2
    hooks_in_loop = lead + steps - NBLK // 2 * heads
    spare = max(0, -(-4 * EVENTS * 16 // RATE) - hooks_in_loop)
    down_at, up_at = pl.ds(0, ff), pl.ds(ff, depth)

    def times(vector, weight, product):
        acc = jnp.zeros((8, depth), F32)
        for part in top_and_rest(jnp.broadcast_to(vector, (8, vector.shape[1]))):
            acc = acc + product(part, weight[...])
        return acc[:1]

    def early_rings(t):
        def one(n, carry):
            rings_a.event(lax.rem(n, 4), lax.div(n, 4))
            return carry

        def due(t):
            return jnp.minimum(lax.div(jnp.maximum(t, 0) * RATE, 16), 4 * EVENTS)

        lax.fori_loop(due(t), due(t + 1), one, 0)

    scat_o = Scatter(outp, mo, co, so_s, so_r, m, mate, cross)
    scat_e = Scatter(em, hid, ce, se_s, se_r, m, mate, cross)
    ends = doc_ends(doc_ref)
    lane = lax.broadcasted_iota(jnp.int32, (BLK, LANES), 1)
    low = lane < HD

    def body(hp, probs, total):
        half_lanes = depth // 2

        def attn_in():
            return jnp.concatenate([dqkv[:SHARD, :], dqkv[SHARD : 2 * SHARD, :]], axis=1)

        def ff_forward(c):
            first = pl.multiple_of(c * SHARD, SHARD)
            here = pl.ds(first, SHARD)

            def moments(r, carry):
                for part in range(8):
                    at = rows_of(first + r * 128 + part * 16, 16)
                    v = xs[at, :].astype(F32)
                    mean = jnp.mean(v, axis=-1, keepdims=True)
                    v = v - mean
                    inv = lax.rsqrt(jnp.mean(v * v, axis=-1, keepdims=True) + EPS)
                    to = pl.ds(part * 16, 16)
                    dkv[to, rows_of(r * LANES, LANES)] = jnp.broadcast_to(mean, (16, LANES))
                    dkv[to, rows_of((4 + r) * LANES, LANES)] = jnp.broadcast_to(inv, (16, LANES))
                return carry

            lax.fori_loop(0, SHARD // 128, moments, 0)

            def norm(r, carry):
                at = rows_of(first + r * 32, 32)
                to = rows_of(r * 32, 32)
                sub = rows_of(lax.rem(r * 32, LANES), 32)
                mean = jnp.concatenate([dkv[sub, rows_of(r // 4 * LANES, LANES)]] * (depth // LANES), axis=1)
                inv = jnp.concatenate([dkv[sub, rows_of((4 + r // 4) * LANES, LANES)]] * (depth // LANES), axis=1)
                v = (xs[at, :].astype(F32) - mean) * inv
                xs[at, :] = v.astype(BF16)
                a = (v * ag_row[...] + as_row[...]).astype(BF16)
                dqkv[to, :] = a[:, :half_lanes]
                dqkv[rows_of(SHARD + r * 32, 32), :] = a[:, half_lanes:]
                min_[to, :] = (v * mg_row[...] + ms_row[...]).astype(BF16)
                return carry

            lax.fori_loop(0, SHARD // 32, norm, 0)
            ct, st = cos[here, :], sine[here, :]
            ain = attn_in()
            qf = dot_t(ain, wqkv[:width, :]) + bqkv[:, :width]
            slot = first + lax.broadcasted_iota(jnp.int32, (SHARD, LANES), 0)
            lane = lax.broadcasted_iota(jnp.int32, (SHARD, LANES), 1)
            low = lane < HD
            doc = jnp.zeros((SHARD, LANES), jnp.int32)
            for end in doc_ends(doc_ref):
                doc = jnp.where(slot >= end, doc + 1, doc)
            same = lane % HD == doc
            mark = jnp.where(same, -BIG, 0.0)
            for p in range(pairs):
                v = rope(qf[:, p * LANES : (p + 1) * LANES], ct, st) * HD**-0.5
                qt[p * LANES : (p + 1) * LANES, here] = jnp.transpose(v.astype(BF16))
                q[2 * p, here, :] = jnp.where(low, v, mark).astype(BF16)
                if 2 * p + 1 < heads:
                    q[2 * p + 1, here, :] = jnp.where(low, mark, v).astype(BF16)
            kvf = dot_t(ain, wqkv[width:, :]) + bqkv[:, width:]
            keys = rope(kvf, ct, st)
            other = jnp.where(same | (lane % HD > DOCS), 0.0, 1.0)
            kx[0, here, :] = jnp.where(low, keys, other).astype(BF16)
            kx[1, here, :] = jnp.where(low, other, pltpu.roll(keys, HD, 1)).astype(BF16)
            vx[0, here, :] = jnp.where(low, pltpu.roll(kvf, HD, 1), 1.0).astype(BF16)
            vx[1, here, :] = jnp.where(low, 1.0, kvf).astype(BF16)
            hp[...] = dot(min_[...], wu[...])

            def act(r, carry):
                to = rows_of(r * 32, 32)
                v = hp[to, :] + bu_row[...]
                cdf = 0.5 * (1.0 + lax.erf(v * (0.5**0.5)))
                pdf = jnp.exp(-0.5 * v * v) * (2.0 * jnp.pi) ** -0.5
                hid[c % 2 * 2 + r // (BLK // 32), rows_of(lax.rem(r * 32, BLK), 32), :] = (v * cdf).astype(BF16)
                dg[rows_of(first + r * 32, 32), :] = (cdf + v * pdf).astype(BF16)
                return carry

            lax.fori_loop(0, SHARD // 32, act, 0)
            outp[here, :] = dot(hid[pl.ds(c % 2 * 2, 2)].reshape(SHARD, ff), wd[...]).astype(BF16)

        def ff_backward(c, k):
            first = pl.multiple_of(c * SHARD + k * BLK, BLK)
            here = pl.ds(first, BLK)
            pl.when(valid(c, k))(lambda: hidden_grads(first))

            @pl.when(jnp.logical_not(valid(c, k)))
            def _():
                dg[here, :] = jnp.zeros((BLK, ff), BF16)

        def hidden_grads(first):
            hp[:BLK, :] = dot_t(gm[pl.ds(first, BLK), :], wd[...])

            def back(r, carry):
                acc, gacc = carry
                at = rows_of(first + r * 32, 32)
                v = hp[rows_of(r * 32, 32), :] * dg[at, :].astype(F32)
                dg[at, :] = v.astype(BF16)
                gv = gm[at, :].astype(F32)
                acc = acc + (v[:8] + v[8:16]) + (v[16:24] + v[24:])
                return acc, gacc + (gv[:8] + gv[8:16]) + (gv[16:24] + gv[24:])

            acc, gacc = lax.fori_loop(0, BLK // 32, back, (jnp.zeros((8, ff), F32), jnp.zeros((8, depth), F32)))
            gsum[:8, :] += gacc
            gsum[8:, :] += acc

        def weights(chip):
            rows = rows_of(chip * 2 * SHARD, 2 * SHARD)
            ga[down_at, :] += t_dot(hid[...].reshape(2 * SHARD, ff), gm[rows, :])
            ga[up_at, :] += t_dot(xs[rows, :], dg[rows, :])

        def shard_of(which):
            return jnp.where(which == 0, m, jnp.where(which == 1, mate, jnp.where(which == 2, cross, far)))

        def after(shard):
            here = rows_of(shard * SHARD, SHARD)
            em[here, :] = (dot_t(dg[here, :], wu[...]) * mg_row[...]).astype(BF16)
            dc = dot_t(gm[here, :], wo[...]).astype(BF16)
            for p in range(pairs):
                dctx[p, here, :] = dc[:, p * LANES : (p + 1) * LANES]

        def norm_grads():
            up_bias = jnp.sum(gsum[8:, :], axis=0, keepdims=True)
            gb[used : used + 8, :] = jnp.concatenate(
                [jnp.sum(gsum[:8, :], axis=0, keepdims=True), up_bias, jnp.zeros((6, depth), F32)], axis=0
            )
            ones = jnp.ones((8, LANES), BF16)
            for r in range(0, depth, LANES):
                folded = jnp.zeros((LANES, LANES), F32)
                for c in range(0, ff, LANES):
                    folded = folded + wu[r : r + LANES, c : c + LANES].astype(F32) * ga[ff + r : ff + r + LANES, c : c + LANES]
                top, rest = top_and_rest(folded)
                gain = dot_t(ones, top) + dot_t(ones, rest)
                gb[misc + 11 : misc + 12, r : r + LANES] = gain[:1]
            gb[misc + 12 : misc + 13, :] = times(up_bias, wu, dot_t)

        causal = lax.broadcasted_iota(jnp.int32, (BLK, BLK), 1) <= lax.broadcasted_iota(jnp.int32, (BLK, BLK), 0)

        def scores(n):
            return hp.at[pl.ds(n // 3 * BLK, BLK), pl.ds(n % 3 * BLK, BLK)]

        def att_forward(i, h):
            at = pl.ds(i * BLK, BLK)
            blocks = key_blocks(i)
            qb = q[h, at, :]
            half = h % 2
            peak = None
            for n, j in enumerate(blocks):
                s = dot_t(qb, kx[half, pl.ds(j * BLK, BLK), :])
                if i == j:
                    s = jnp.where(causal, s, -BIG)
                scores(n)[...] = s
                peak = s if peak is None else jnp.maximum(peak, s)
            top = jnp.max(peak, axis=-1, keepdims=True)
            acc = jnp.zeros((BLK, LANES), F32)
            for n, j in enumerate(blocks):
                e = jnp.exp(scores(n)[...] - top).astype(BF16)
                if i < PADBLK:
                    probs[h, SLOTS[(i, j)]] = e
                acc = acc + dot(e, vx[half, pl.ds(j * BLK, BLK), :])
            total[h] = acc

            @pl.when(h == heads - 1)
            def _():
                context = []
                for p in range(pairs):
                    full = 2 * p + 1 < heads
                    first, second = total[2 * p], total[2 * p + 1] if full else None
                    norm = jnp.where(low, pltpu.roll(first, HD, 1), pltpu.roll(second, HD, 1) if full else 1.0)
                    norm = 1.0 / norm
                    c = jnp.where(low, first, second if full else 0.0) * norm
                    context.append(c.astype(BF16))
                    if i < PADBLK:
                        scaled = dctx[p, at, :].astype(F32) * norm
                        dcs = scaled.astype(BF16).astype(F32)
                        dct[p * LANES : (p + 1) * LANES, at] = jnp.transpose(dcs.astype(BF16))
                        prod = dcs * c
                        for side in range(2 if full else 1):
                            inside = low if side == 0 else ~low
                            r = -jnp.sum(jnp.where(inside, prod, 0.0), axis=-1, keepdims=True)
                            r_top = r.astype(BF16).astype(F32)
                            extra = jnp.where(lane % HD == 0, r_top, jnp.where(lane % HD == 1, r - r_top, 0.0))
                            left_in[2 * p + side, at, :] = jnp.where(inside, dcs, extra).astype(BF16)
                for p in range(pairs):
                    dctx[p, at, :] = context[p]
                outp[at, :] = (dot(jnp.concatenate(context, axis=1), wo[...]) + outp[at, :].astype(F32)).astype(BF16)
                scat_o.offer(i)
                before = (i - 1) % NBLK
                if i % (NBLK // 2) > 0:
                    scat_o.collect(before)
                else:
                    @pl.when(chip != i // (NBLK // 2))
                    def _():
                        scat_o.collect(before)

        def att_backward(i, h):
            at = pl.ds(i * BLK, BLK)
            half = h % 2
            lhs = left_in[h, at, :]
            mine = rows_of(h * HD, HD)
            q_turned, d_turned = qt[mine, at], dct[mine, at]
            acc = jnp.zeros((BLK, LANES), F32)
            for j in key_blocks(i):
                jat = pl.ds(j * BLK, BLK)
                e = probs[h, SLOTS[(i, j)]]
                ds = (e.astype(F32) * dot_t(lhs, vx[half, jat, :])).astype(BF16)
                acc = acc + dot(ds, kx[half, jat, :])
                dkv[:HD, jat] += dot(q_turned, ds)
                dkv[HD:, jat] += dot(d_turned, e)
            dqh[h] = acc

            @pl.when(h == heads - 1)
            def _():
                ct, st = cos[at, :], sine[at, :]
                for p in range(pairs):
                    full = 2 * p + 1 < heads
                    v = jnp.where(low, dqh[2 * p], dqh[2 * p + 1] if full else 0.0)
                    dqkv[at, p * LANES : (p + 1) * LANES] = (unrope(v, ct, st) * HD**-0.5).astype(BF16)
                v = jnp.transpose(dkv[:, at])
                dqkv[at, width:] = jnp.where(low, unrope(v, ct, st), v).astype(BF16)
                dsum[:1, :] += jnp.sum(dqkv[at, :].astype(F32), axis=0, keepdims=True)
                em[at, :] = (dot(dqkv[at, :], wqkv[...]) * ag_row[...] + em[at, :].astype(F32)).astype(BF16)
                scat_e.offer(i)
                if i < PADBLK - 1:
                    scat_e.collect(i + 1)

        def out_rings(blocks):
            @pl.when(lax.rem(blocks, 2) == 0)
            def _():
                def one(r, carry):
                    rings_b.event(r, lax.div(blocks, 2))
                    return carry

                lax.fori_loop(0, 2, one, 0)

        plan = [(0, 0, 0), (1, 0, 0), (1, 0, 1), (0, 1, 0), (1, 1, 0), (1, 1, 1), (2, 0, 0), (3, 0, 0), (3, 1, 0), (0, 2, 0), (0, 3, 0)]
        plan += [(1, 2, 0), (1, 2, 1), (1, 3, 0), (1, 3, 1), (2, 2, 0), (3, 2, 0), (3, 3, 0), (4, 0, 0)]
        before = 11
        early = NBLK // 2 * heads
        after_all = len(plan) + early
        hooked = 16 + early

        def pick(p):
            code = jnp.int32(0)
            for n, (what, whose, part) in enumerate(plan):
                code = jnp.where(p == n, what + 8 * whose + 32 * part, code)
            return lax.rem(code, 8), lax.rem(lax.div(code, 8), 4), lax.div(code, 32)

        def at_step(n):
            return lambda action: pl.when(step_now[0] == n)(action)

        step_now = [None]

        def step(s, carry):
            block, h = carry
            planned = (s < before) | ((s >= before + early) & (s < after_all))
            p = jnp.where(s < before, s, s - early)
            step_now[0] = jnp.where(planned, p, -1)
            early_rings(s - hooked)

            @at_step(0)
            def _():
                for c in local:
                    c.wait()

            @at_step(1)
            def _():
                for k in range(2):
                    @pl.when(valid(m, k))
                    def _():
                        local_g[k].wait()

            @at_step(3)
            def _():
                for k in range(2):
                    x_mate(mate, k).wait_recv()

            @at_step(4)
            def _():
                for k in range(2):
                    @pl.when(valid(mate, k))
                    def _():
                        g_mate(mate, k).wait_recv()

            @at_step(7)
            def _():
                for k in range(2):
                    x_cross(m, k).wait_send()

                    @pl.when(valid(m, k))
                    def _():
                        g_cross(m, k).start()

                for k in range(2):
                    x_cross(cross, k).wait_recv()
                    x_pass(cross, k).start()

            @at_step(9)
            def _():
                for k in range(2):
                    x_pass(cross, k).wait_send()

            @at_step(10)
            def _():
                for k in range(2):
                    x_pass(far, k).wait_recv()

            for k in range(2):
                @at_step(11 + k)
                def _():
                    @pl.when(valid(cross, k))
                    def _():
                        g_cross(cross, k).wait_recv()
                        g_pass(cross, k).start()

                @at_step(13 + k)
                def _():
                    @pl.when(valid(far, k))
                    def _():
                        g_pass(far, k).wait_recv()

            @pl.when(jnp.logical_not(planned) & (block == NBLK) & (h == 0))
            def _():
                own_tokens.start()
                dkv[...] = jnp.zeros_like(dkv)
                for b in (NBLK // 2 - 1, NBLK - 1):
                    @pl.when(chip != b // (NBLK // 2))
                    def _():
                        scat_o.collect(b)
                for p in range(pairs):
                    some = min(used - p * LANES, LANES)
                    gb[p * LANES : p * LANES + some, :] = t_dot(dctx[p], gm[...])[:some, :]

            @pl.when(jnp.logical_not(planned) & (block >= NBLK) & (h == 0))
            def _():
                out_rings(block - NBLK)

            what, whose, half = pick(p)
            shard = shard_of(whose)
            forward_block = lax.rem(block + chip * (NBLK // 2), NBLK)
            backward_block = jnp.maximum(block - NBLK, 0)
            kind = jnp.where(planned, what, jnp.where(block < NBLK, 5, 6))
            lax.switch(
                kind,
                [
                    lambda: ff_forward(shard), lambda: ff_backward(shard, half), lambda: weights(lax.div(shard, 2)), lambda: after(shard),
                    norm_grads,
                    lambda: lax.switch(forward_block, [partial(att_forward, i) for i in range(NBLK)], h),
                    lambda: lax.switch(backward_block, [partial(att_backward, i) for i in reversed(range(PADBLK))], h),
                ],
            )
            last = h == heads - 1
            following = jnp.where(last, block + 1, block), jnp.where(last, 0, h + 1)
            return jnp.where(planned, block, following[0]), jnp.where(planned, h, following[1])

        lax.fori_loop(0, after_all + steps - early, step, (jnp.int32(0), jnp.int32(0)))

    pl.run_scoped(
        body, pltpu.VMEM((SHARD, ff), F32), pltpu.VMEM((heads, NSLOT, BLK, BLK), BF16), pltpu.VMEM((heads, BLK, LANES), F32),
    )
    for k in range(2):
        x_mate(m, k).wait_send()

        @pl.when(valid(m, k))
        def _():
            g_cross(m, k).wait_send()
            g_mate(m, k).wait_send()

        @pl.when(valid(cross, k))
        def _():
            g_pass(cross, k).wait_send()

    scat_e.collect(0)
    rows = VALID
    gb[KV_ROW : KV_ROW + LANES, :] = t_dot(dqkv[:rows, width:], xs[:rows, :])
    rings_b.event(2, 0)
    gb[Q_ROW:misc, :] = t_dot(dqkv[:rows, :width], xs[:rows, :])[:used, :]
    rings_b.event(3, 0)
    sums = dsum[:1, :]
    gb[misc : misc + 1, : width + LANES] = sums
    gb[misc + 8 : misc + 9, :LANES] = sums[:, width:]
    gain = jnp.sum(wqkv[:used, :].astype(F32) * gb[Q_ROW:misc, :], axis=0, keepdims=True)
    gb[misc + 9 : misc + 10, :] = gain + jnp.sum(
        wqkv[width:, :].astype(F32) * gb[KV_ROW : KV_ROW + LANES, :], axis=0, keepdims=True
    )
    gb[misc + 10 : misc + 11, :] = times(sums, wqkv, dot)
    rings_b.event(4, 0)

    def exchange(stage, to):
        return pltpu.make_async_remote_copy(
            src_ref=swap.at[2 * stage], dst_ref=swap.at[2 * stage + 1], send_sem=bf_s.at[stage], recv_sem=bf_r.at[stage],
            device_id={"mp": to}, device_id_type=MESH,
        )

    def finish_out(r, carry):
        at = pl.multiple_of(r * 32, 32)
        v = min_[rows_of(at, 32), :].astype(F32) + scat_o.total(r // (BLK // 32), lax.rem(at, BLK)) + rows_in[5:6, :]
        outp[rows_of(m * SHARD + at, 32), :] = v.astype(BF16)
        return carry

    def finish_in(r, carry):
        for part in range(4):
            at = pl.multiple_of(r * 64 + part * 16, 16)
            rows = rows_of(at, 16)
            v = min_[rows, :].astype(F32)
            v = v - jnp.mean(v, axis=-1, keepdims=True)
            inv = lax.rsqrt(jnp.mean(v * v, axis=-1, keepdims=True) + EPS)
            v = v * inv
            e = scat_e.total(r // (BLK // 64), lax.rem(at, BLK), 16)
            e = inv * (e - jnp.mean(e, axis=-1, keepdims=True) - v * jnp.mean(e * v, axis=-1, keepdims=True))
            g = gm[rows_of(m * SHARD + at, 16), :].astype(F32)
            io[part] = (e + g).astype(BF16)
        for part in range(4):
            min_[rows_of(r * 64 + part * 16, 16), :] = io[part]
        return carry

    out_block = pltpu.make_async_copy(outp.at[rows_of(m * SHARD, SHARD), :], bout_hbm, loc.at[1])
    out_in = pltpu.make_async_copy(min_, ingrad_hbm, loc.at[2])

    done = (PADBLK - 1) // 2

    def tail(e, carry):
        def late(n, carry):
            early_rings(hooks_in_loop + n)
            return carry

        def one(r, carry):
            step = jnp.where(r < 2, e + done, e)

            @pl.when(jnp.where(r < 2, step < EVENTS, (e != 4) | (r == 3)))
            def _():
                rings_b.event(r, step)

            return carry

        @pl.when(e == 4)
        def _():
            rings_b.settle(2)
            rings_b.settle(4)
            swap[0, :16, :] = f_b[rings_b.at(2, 0), :]
            swap[0, 16:, :] = f_b[rings_b.at(4, 0), :]
            exchange(0, mate).start()

        lax.fori_loop(0, 5, one, 0)

        @pl.when(e == 4)
        def _():
            exchange(0, mate).wait()
            swap[2] = (swap[0].astype(F32) + swap[1].astype(F32)).astype(BF16)
            exchange(1, cross).start()

        lax.fori_loop(lax.div((e - 1) * spare, EVENTS - 1), lax.div(e * spare, EVENTS - 1), late, 0)

        @pl.when(e == 4)
        def _():
            exchange(1, cross).wait()
            both = swap[2].astype(F32) + swap[3].astype(F32)
            f_b[rings_b.at(2, 0), :] = both[:16].astype(BF16)
            last = lax.broadcasted_iota(jnp.int32, (16, depth), 0) >= jnp.where(place == used // 16 % RING, 8, 16)
            f_b[rings_b.at(4, 0), :] = jnp.where(last, both[16:], swap[0, 16:, :].astype(F32)).astype(BF16)
            rings_b.release(2)
            rings_b.release(4)

        @pl.when(e == 1)
        def _():
            own_tokens.wait()
            for k in range(2):
                scat_o.arrived(k)

        @pl.when(e <= 4)
        def _():
            lax.fori_loop((e - 1) * (SHARD // 128), e * (SHARD // 128), finish_out, 0)

        @pl.when(e == 4)
        def _():
            out_block.start()

        @pl.when(e == 5)
        def _():
            for k in range(2):
                @pl.when(valid(m, k))
                def _():
                    scat_e.arrived(k)

            @pl.when(jnp.logical_not(valid(m, 1)))
            def _():
                min_[BLK:, :] = jnp.zeros((BLK, depth), BF16)

        @pl.when((e >= 5) & (e < 8))
        def _():
            limit = jnp.where(valid(m, 1), SHARD, BLK) // 64
            lax.fori_loop((e - 5) * limit // 3, (e - 4) * limit // 3, finish_in, 0)

        @pl.when(e == 7)
        def _():
            out_in.start()

        return carry

    lax.fori_loop(1, EVENTS, tail, 0)
    out_a = pltpu.make_async_copy(dg.at[: ff + depth, :], fa_hbm, loc.at[0])
    out_a.start()
    out_b = pltpu.make_async_copy(f_b, fb_hbm, loc.at[3])
    out_b.start()
    for b in range(NBLK):
        scat_o.drain(b)
        if b < PADBLK:
            scat_e.drain(b)
    for c in (out_a, out_b, out_block, out_in):
        c.wait()


VM = pl.BlockSpec(memory_space=pltpu.VMEM)
SM = pl.BlockSpec(memory_space=pltpu.SMEM)
ANY = pl.BlockSpec(memory_space=pl.ANY)


def run_layer(heads, doc, tokens, grads, small, wu, bu, wd):
    depth = tokens.shape[1]
    ff = wu.shape[1]
    pairs = (heads + 1) // 2
    width = pairs * LANES
    wide = width + LANES
    sh = jax.ShapeDtypeStruct
    vm = pltpu.VMEM
    dma = pltpu.SemaphoreType.DMA
    a_rows, b_rows = ff + depth, KV_ROW + 384

    def ring_refs(rows, count):
        chunk = rows // (count * RING)
        return [vm((count, 4, chunk, depth // 2), BF16), vm((count, 4, 4, chunk, depth // 2), BF16), vm((rows, depth), BF16)]

    scratch = [
        vm((SLOT, depth), BF16), vm((SLOT, depth), BF16), vm((SLOT, depth), BF16), vm((SLOT, depth), BF16),
        vm((a_rows, depth), F32), vm((b_rows, depth), F32),
        vm((heads, SLOT, LANES), BF16), vm((width, SLOT), BF16), vm((2, SLOT, LANES), BF16), vm((2, SLOT, LANES), BF16),
        vm((pairs, SLOT, LANES), BF16), vm((width, VALID), BF16), vm((heads, VALID, LANES), BF16),
        vm((SLOT, LANES), F32), vm((SLOT, LANES), F32), vm((heads, BLK, LANES), F32),
        vm((LANES, VALID), F32), vm((SLOT, wide), BF16), vm((wide, depth), BF16), vm((width, depth), BF16),
        vm((depth, ff), BF16), vm((ff, depth), BF16), vm((1, wide), F32), vm((16, depth), F32), vm((8, depth), F32), vm((8, wide), F32),
        vm((SHARD, depth), BF16),
        *ring_refs(a_rows, 4)[:2], vm((SLOT, ff), BF16), *ring_refs(b_rows, 5),
        vm((4, BLK, depth), BF16), vm((2, BLK, depth), BF16), vm((4, BLK, depth), BF16), vm((2, BLK, depth), BF16),
        vm((4, 32, depth), BF16), vm((4, 16, depth), BF16),
        dma((8,)), dma((12,)), dma((12,)), dma((4, 4, 8)), dma((4, 4)), dma((5, 4, 8)), dma((5, 4)),
        dma((6,)), dma((6,)), dma((6,)), dma((6,)), dma((2,)), dma((2,)),
    ]
    return pl.pallas_call(
        partial(layer_kernel, heads),
        out_shape=(
            sh((SHARD, depth), BF16), sh((SHARD, depth), BF16), sh((a_rows, depth), BF16), sh((b_rows, depth), BF16),
        ),
        in_specs=[SM, ANY, ANY] + [VM] * 13 + [ANY, VM, ANY],
        out_specs=[ANY] * 4,
        scratch_shapes=scratch,
        compiler_params=pltpu.CompilerParams(vmem_limit_bytes=67043328, collective_id=0, has_side_effects=True),
        name="layer",
    )(doc, tokens, grads, *small, wu, bu, wd)


def final_kernel(
    heads, ff,
    bout_hbm, ingrad_hbm, fa_hbm, fb_hbm, ag_in, as_in, mg_in, ms_in,
    bout_out, ingrad_out, attn_gain, attn_shift, qw_out, qb_out, kw_out, kb_out, vw_out, vb_out, ow_out, ob_out,
    mlp_gain, mlp_shift, uw_out, ub_out, dw_out, db_out,
    blocks, fa, fb, wide, out, qw, kw, vw, turned, sem,
):
    depth = fa.shape[1]
    used = heads * HD
    pairs = (heads + 1) // 2
    width = pairs * LANES
    misc = Q_ROW + used
    stores = []

    def load(src, dst, n):
        copy = pltpu.make_async_copy(src, dst, sem.at[n])
        copy.start()
        return copy

    def store(src, dst):
        copy = pltpu.make_async_copy(src, dst, sem.at[12 + len(stores)])
        copy.start()
        stores.append(copy)

    piece = 384
    parts = (ff + depth) // piece
    small = load(fb_hbm, fb, 0)
    loads = [load(fa_hbm.at[pl.ds(n * piece, piece), :], fa.at[pl.ds(n * piece, piece), :], 1 + n) for n in range(parts)]
    passed = [load(ref, blocks.at[n], 8 + n) for n, ref in enumerate((bout_hbm, ingrad_hbm))]
    row = lambda ref: ref[...].reshape(1, depth)
    ag, as_, mg, ms = row(ag_in), row(as_in), row(mg_in), row(ms_in)
    turned[...] = jnp.transpose(jnp.concatenate([mg, ms, jnp.zeros((6, depth), F32)], axis=0))
    small.wait()
    extra = fb[used : used + 16, :].astype(F32)
    g_sum, up_bias = extra[:1], extra[1:2]
    for n in range(parts):
        loads[n].wait()
        at = n * piece
        if at < ff:
            wide[pl.ds(at, piece), :] = fa[pl.ds(at, piece), :].astype(F32)
            store(wide.at[pl.ds(at, piece), :], dw_out.at[pl.ds(at, piece), :])
        else:
            to = at - ff
            wide[pl.ds(at, piece), :] = (
                fa[pl.ds(at, piece), :].astype(F32) * turned[to : to + piece, 0:1] + turned[to : to + piece, 1:2] * up_bias
            )
            store(wide.at[pl.ds(at, piece), :], uw_out.at[pl.ds(to, piece), :])
    for n, dst in enumerate((bout_out, ingrad_out)):
        passed[n].wait()
        store(blocks.at[n], dst)
    out[...] = fb[:used, :].astype(F32)
    store(out, ow_out)
    last = fb[misc : misc + 16, :].astype(F32)
    kv_bias = last[8:9, :LANES]
    biases = last[:1, :width]

    def outer(vector, other):
        a, b = top_and_rest(vector)
        c, e = top_and_rest(other)
        return t_dot(jnp.concatenate([a, a, b, b], axis=0), jnp.concatenate([c, e, c, e], axis=0))

    qw[...] = fb[Q_ROW:misc, :].astype(F32) * ag + outer(biases[:, :used], as_)
    store(qw, qw_out)
    kv = fb[KV_ROW : KV_ROW + LANES, :].astype(F32) * ag + outer(kv_bias, as_)
    kw[...] = kv[:HD]
    vw[...] = kv[HD:]
    store(kw, kw_out)
    store(vw, vw_out)
    for n, ref in enumerate((attn_gain, attn_shift, mlp_gain, mlp_shift)):
        ref[...] = last[9 + n : 10 + n].reshape(depth)
    kb_out[...] = kv_bias[:, :HD].reshape(HD)
    vb_out[...] = kv_bias[:, HD:].reshape(HD)
    qb_out[...] = biases[:, :used].reshape(used)
    ob_out[...] = g_sum.reshape(depth)
    db_out[...] = g_sum.reshape(depth)
    ub_out[...] = up_bias.reshape(ff)
    for c in stores:
        c.wait()


def run_final(heads, ff, block_out, input_grad, fa, fb, gains):
    shard, depth = block_out.shape
    used = heads * HD
    sh = jax.ShapeDtypeStruct
    vm = pltpu.VMEM
    line = lambda n: sh((n,), F32)
    return pl.pallas_call(
        partial(final_kernel, heads, ff),
        out_shape=(
            sh((shard, depth), BF16), sh((shard, depth), BF16), line(depth), line(depth), sh((used, depth), F32), line(used),
            sh((HD, depth), F32), line(HD), sh((HD, depth), F32), line(HD), sh((used, depth), F32), line(depth),
            line(depth), line(depth), sh((depth, ff), F32), line(ff), sh((ff, depth), F32), line(depth),
        ),
        in_specs=[ANY] * 4 + [VM] * 4,
        out_specs=[ANY, ANY, VM, VM, ANY, VM, ANY, VM, ANY, VM, ANY, VM, VM, VM, ANY, VM, ANY, VM],
        scratch_shapes=[
            vm((2, shard, depth), BF16), vm(fa.shape, fa.dtype), vm(fb.shape, fb.dtype), vm((ff + depth, depth), F32),
            vm((used, depth), F32), vm((used, depth), F32), vm((HD, depth), F32), vm((HD, depth), F32), vm((depth, 8), F32),
            pltpu.SemaphoreType.DMA((24,)),
        ],
        compiler_params=pltpu.CompilerParams(vmem_limit_bytes=67043328),
        name="final",
    )(block_out, input_grad, fa, fb, *gains)


def per_device(
    ways,
    tokens, doc_lengths, attn_gain, attn_shift, query_weight, query_bias, key_weight, key_bias, value_weight, value_bias,
    out_weight, out_bias, mlp_gain, mlp_shift, up_weight, up_bias, down_weight, down_bias, out_grad,
):
    heads = query_weight.shape[1] // HD
    small = (
        attn_gain, attn_shift, query_weight.T, query_bias, key_weight.T, key_bias, value_weight.T, value_bias,
        out_weight, out_bias, down_bias, mlp_gain, mlp_shift,
    )
    block_out, input_grad, fa, fb = run_layer(
        heads, doc_lengths, tokens, out_grad, small, up_weight, up_bias, down_weight
    )
    if ways > RING:
        groups = [[i + RING * o for o in range(ways // RING)] for i in range(RING)]
        fa, fb = lax.psum((fa.astype(F32), fb.astype(F32)), "dp", axis_index_groups=groups)
    (
        block_out, input_grad, attn_gain_grad, attn_shift_grad, qw, qb, kw, kb, vw, vb, ow, ob, mlp_gain_grad, mlp_shift_grad,
        uw, ub, dw, db,
    ) = run_final(
        heads, up_weight.shape[1], block_out, input_grad, fa, fb, (attn_gain, attn_shift, mlp_gain, mlp_shift)
    )
    return (
        block_out, input_grad, attn_gain_grad, attn_shift_grad, qw.T, qb, kw.T, kb, vw.T, vb, ow, ob, mlp_gain_grad,
        mlp_shift_grad, uw, ub, dw, db,
    )


def solution(mesh):
    rows = P(("dp", "mp"), None)
    placed = (
        rows, P("dp", None), P(), P(), P(None, "mp"), P("mp"), P(), P(), P(), P(), P("mp", None), P(), P(), P(),
        P(None, "mp"), P("mp"), P("mp", None), P(), rows,
    )
    outs = (
        rows, rows, P(), P(), P(None, "mp"), P("mp"), P(), P(), P(), P(), P("mp", None), P(), P(), P(),
        P(None, "mp"), P("mp"), P("mp", None), P(),
    )
    return jax.shard_map(partial(per_device, mesh.shape["dp"]), mesh=mesh, in_specs=placed, out_specs=outs, check_vma=False)
```
